256 devices in a mesh: gx: 2 (over core), gy: 8 (over z), gz: 16 (over y, x).
Axes of the slice: x: 4, y: 4, z: 8, core: 2. Of those that a mesh axis runs over, the one named last changes fastest.
Arguments:
- residual: float32 [32, 128, 4096], P('gx', 'gy', 'gz'), may hold values from -6 to 6
- fdm_vectors: bfloat16 [2, 8, 16, 3, 10, 10, 128], P('gx', 'gy', 'gz'), may hold values from -2 to 2
- fdm_eigen: float32 [2, 8, 16, 3, 10, 128], P('gx', 'gy', 'gz'), may hold values from 0.1 to 4
- coarse_basis: float32 [8, 8, 8], replicated, may hold values from -0.75 to 0.75
- x_interior: float32 [2, 8, 16, 16, 16], P('gx', 'gy', 'gz'), may hold values from -1.5 to 1.5
- x_separator: float32 [2, 8, 16, 8, 16, 256], P('gx', 'gy', 'gz'), may hold values from -0.375 to 0.375
Outputs:
- preconditioned: float32 [32, 128, 4096], P('gx', 'gy', 'gz')
The draws below stay inside these ranges and needn't reach their ends.
All inputs are finite; a program needn't handle non-finite values.
Results may differ from the reference program's by a relative error of at most 0.0003.
Values sent between devices are 32-bit elements; how exact they have to be, the bound alone decides.
No kernel may reach another device: no remote copies, remote signals or barrier semaphores. Data moves between devices by JAX's collectives and lax.ppermute only.
A program may use at most 128 MiB of HBM per device.

```python
import math
import jax
import jax.numpy as jnp
from jax import lax

PTS = 8
EXT = 10
EX = 2
EY = 2
EZ = 32
KSEP = 256
ELEMS = 128
VCO = 16
CX = 16
CY = 16
CZ = 256
NX = 32
NY = 128
NZ = 4096
LEVELS = 8
N_GX = 2
N_GY = 8
N_GZ = 16


def block_levels(rng, extent, shards, low, largest):
    def one(dim, blocks):
        steps = jax.random.uniform(jax.random.fold_in(jax.random.fold_in(rng, 6), dim), (blocks,), jnp.float32, low / len(shards), largest / len(shards))
        return jnp.repeat(jnp.exp(steps), extent[dim] // blocks).reshape((-1,) + (1,) * (len(extent) - dim - 1))

    factor_of = one(*shards[0])
    for cut in shards[1:]:
        factor_of = factor_of * one(*cut)
    return factor_of


def normal_values(rng, extent, deviation, limit, shards=(), kind=jnp.bfloat16):
    drawn = deviation * jax.random.normal(rng, extent, jnp.float32)
    if shards:
        drawn = drawn * block_levels(rng, extent, shards, -0.22, 0.18)
    return jnp.clip(drawn, -limit, limit).astype(kind)


def setup_inputs(seed: int = 0) -> dict:
    arg_keys = jax.random.split(jax.random.key(seed), 7)
    residual = normal_values(arg_keys[0], (NX, NY, NZ), 1.0, 6.0, ((0, 2), (1, 8), (2, 16)), jnp.float32)
    fdm_vectors = normal_values(arg_keys[1], (N_GX, N_GY, N_GZ, 3, EXT, EXT, ELEMS), EXT ** -0.5, 2.0, ((0, 2), (1, 8), (2, 16)))
    fdm_eigen = jnp.clip(jnp.exp(math.log(4.0) - 3.6888794 * jax.random.uniform(arg_keys[2], (N_GX, N_GY, N_GZ, 3, EXT, ELEMS), jnp.float32) ** block_levels(arg_keys[2], (N_GX, N_GY, N_GZ, 3, EXT, ELEMS), ((0, 2), (1, 8), (2, 16)), -0.2, 0.2)), 0.1, 4.0)
    coarse_basis = normal_values(arg_keys[3], (PTS, PTS, PTS), 0.125, 0.75, (), jnp.float32)
    x_interior = normal_values(arg_keys[4], (N_GX, N_GY, N_GZ, VCO, VCO), VCO ** -0.5, 1.5, ((0, 2), (1, 8), (2, 16)), jnp.float32)
    x_separator = normal_values(arg_keys[5], (N_GX, N_GY, N_GZ, LEVELS, VCO, KSEP), (VCO * 16) ** -0.5, 0.375, ((0, 2), (1, 8), (2, 16)), jnp.float32)
    return dict(residual=residual, fdm_vectors=fdm_vectors, fdm_eigen=fdm_eigen, coarse_basis=coarse_basis, x_interior=x_interior, x_separator=x_separator)


HIGHEST = lax.Precision.HIGHEST


def extend_block(padded, count_x, count_y, count_z):
    along_x = jnp.stack([lax.slice_in_dim(padded, i, i + PTS * (count_x - 1) + 1, PTS, 0) for i in range(PTS + 2)], 0)
    along_y = jnp.stack([lax.slice_in_dim(along_x, j, j + PTS * (count_y - 1) + 1, PTS, 2) for j in range(PTS + 2)], 1)
    along_z = jnp.stack([lax.slice_in_dim(along_y, k, k + PTS * (count_z - 1) + 1, PTS, 4) for k in range(PTS + 2)], 2)
    return along_z.reshape(PTS + 2, PTS + 2, PTS + 2, count_x * count_y * count_z)


def solve_elements(extended, vectors, eigen):
    modes_x = vectors[0].astype(jnp.float32)
    modes_y = vectors[1].astype(jnp.float32)
    modes_z = vectors[2].astype(jnp.float32)
    temp = jnp.einsum('iae,ijke->ajke', modes_x, extended, precision=HIGHEST)
    temp = jnp.einsum('jbe,ajke->abke', modes_y, temp, precision=HIGHEST)
    temp = jnp.einsum('kce,abke->abce', modes_z, temp, precision=HIGHEST)
    denom = eigen[0][:, None, None, :] + eigen[1][None, :, None, :] + eigen[2][None, None, :, :]
    temp = temp / denom
    temp = jnp.einsum('iae,abce->ibce', modes_x, temp, precision=HIGHEST)
    temp = jnp.einsum('jbe,ibce->ijce', modes_y, temp, precision=HIGHEST)
    temp = jnp.einsum('kce,ijce->ijke', modes_z, temp, precision=HIGHEST)
    return temp


def fold_block(local, count_x, count_y, count_z, shape):
    grid = local.reshape(PTS + 2, PTS + 2, PTS + 2, count_x, count_y, count_z)
    filler = jnp.float32(0)
    summed_z = None
    for k in range(PTS + 2):
        config = ((0, 0, 0), (0, 0, 0), (0, 0, 0), (0, 0, 0), (k, shape[2] - k - PTS * (count_z - 1) - 1, PTS - 1))
        placed = lax.pad(grid[:, :, k], filler, config)
        summed_z = placed if summed_z is None else summed_z + placed
    summed_y = None
    for j in range(PTS + 2):
        config = ((0, 0, 0), (0, 0, 0), (j, shape[1] - j - PTS * (count_y - 1) - 1, PTS - 1), (0, 0, 0))
        placed = lax.pad(summed_z[:, j], filler, config)
        summed_y = placed if summed_y is None else summed_y + placed
    summed_x = None
    for i in range(PTS + 2):
        config = ((i, shape[0] - i - PTS * (count_x - 1) - 1, PTS - 1), (0, 0, 0), (0, 0, 0))
        placed = lax.pad(summed_y[i], filler, config)
        summed_x = placed if summed_x is None else summed_x + placed
    return summed_x


def schwarz_block(padded, vectors, eigen):
    extended = extend_block(padded, EX, EY, EZ)
    local = solve_elements(extended, vectors, eigen)
    return fold_block(local, EX, EY, EZ, padded.shape)


def reference(residual, fdm_vectors, fdm_eigen, coarse_basis, x_interior, x_separator):
    devices = N_GX * N_GY * N_GZ
    padded = jnp.pad(residual, 1)
    vectors_all = fdm_vectors.reshape(devices, 3, PTS + 2, PTS + 2, EX * EY * EZ)
    eigen_all = fdm_eigen.reshape(devices, 3, PTS + 2, EX * EY * EZ)

    def visit(accum, item):
        number, vectors, eigen = item
        start_x = (number // (N_GY * N_GZ)) * CX
        start_y = ((number // N_GZ) % N_GY) * CY
        start_z = (number % N_GZ) * CZ
        starts = (start_x.astype(jnp.int32), start_y.astype(jnp.int32), start_z.astype(jnp.int32))
        sizes = (CX + 2, CY + 2, CZ + 2)
        block = lax.dynamic_slice(padded, starts, sizes)
        contrib = schwarz_block(block, vectors, eigen)
        current = lax.dynamic_slice(accum, starts, sizes)
        return lax.dynamic_update_slice(accum, current + contrib, starts), None

    numbers = jnp.arange(devices, dtype=jnp.int32)
    accum, _ = lax.scan(visit, jnp.zeros_like(padded), (numbers, vectors_all, eigen_all))
    smoothed = accum[1:-1, 1:-1, 1:-1]

    view = (NX // (2 * PTS), 2, PTS, NY // (2 * PTS), 2, PTS, NZ // (2 * PTS), 2, PTS)
    weights = coarse_basis[None, None, :, None, None, :, None, None, :]
    rhs_grid = jnp.sum(residual.reshape(view) * weights, axis=(1, 2, 4, 5, 7, 8))
    coarse_rhs = rhs_grid.reshape(N_GX, EX // 2, N_GY, EY // 2, N_GZ, EZ // 2)
    coarse_rhs = coarse_rhs.transpose(0, 2, 4, 1, 3, 5).reshape(devices, VCO)

    own = x_interior.reshape(devices, VCO, VCO)
    seps = x_separator.reshape(devices, LEVELS, VCO, KSEP)
    interior_coef = jnp.einsum('dvw,dv->dw', own, coarse_rhs, precision=HIGHEST)
    partials = jnp.einsum('dlvk,dv->dlk', seps, coarse_rhs, precision=HIGHEST)
    groups = []
    for level in range(1, LEVELS + 1):
        width = 2 ** level
        summed = partials[:, level - 1].reshape(devices // width, width, KSEP).sum(axis=1)
        groups.append(jnp.repeat(summed, width, axis=0))
    separator_coef = jnp.stack(groups, 1)
    coarse_solution = jnp.einsum('dvw,dw->dv', own, interior_coef, precision=HIGHEST)
    coarse_solution = coarse_solution + jnp.einsum('dlvk,dlk->dv', seps, separator_coef, precision=HIGHEST)

    coarse_grid = coarse_solution.reshape(N_GX, N_GY, N_GZ, EX // 2, EY // 2, EZ // 2)
    coarse_grid = coarse_grid.transpose(0, 3, 1, 4, 2, 5).reshape(NX // (2 * PTS), NY // (2 * PTS), NZ // (2 * PTS))
    correction = coarse_grid[:, None, None, :, None, None, :, None, None] * weights
    preconditioned = smoothed.reshape(view) + correction
    return preconditioned.reshape(NX, NY, NZ)
```

```python
import functools

import jax
import jax.numpy as jnp
from jax import lax
from jax.experimental import pallas as pl
from jax.experimental.pallas import tpu as pltpu
from jax.sharding import PartitionSpec as P

F32 = jnp.float32
VM = pl.BlockSpec(memory_space=pltpu.VMEM)


def iotas(rows=8):
    lane = lax.broadcasted_iota(jnp.int32, (rows, 128), 1)
    sub = lax.broadcasted_iota(jnp.int32, (rows, 128), 0)
    return lane, sub


def roll(value, shift):
    shift = shift % 128
    return value if shift == 0 else pltpu.roll(value, shift, value.ndim - 1)


def row(ref, index, rows=8):
    return jnp.broadcast_to(ref[pl.ds(index, 1), :], (rows, 128))


def total(terms):
    terms = list(terms)
    while len(terms) > 1:
        terms = [a + b for a, b in zip(terms[::2], terms[1::2])] + terms[len(terms) & ~1 :]
    return terms[0]


def chain(pairs):
    acc = None
    for a, b in pairs:
        acc = a * b if acc is None else acc + a * b
    return acc


def pre_kernel(x_ref, xface_ref, basis_ref, own_ref, sep_ref, e_ref, za_ref, zb_ref, part_ref, ownsol_ref, xt, ft):
    gx = lax.axis_index("gx")
    even = lax.rem(lax.axis_index("gz"), 2) == 0
    lane, _ = iotas()
    low_q = (lane & 32) == 0
    high_p = lane >= 64
    slot = lane & 31
    turned = x_ref[...].T
    xt[0] = turned[:, :128]
    xt[1] = turned[:, 128:]
    face = jnp.concatenate([xface_ref[...], jnp.zeros((112, 256), F32)], 0).T
    ft[...] = face
    for pair in range(4):
        k0, k1 = 2 * pair, 2 * pair + 1
        pieces = [xt[p, pl.ds(k, 32, stride=8), :] for p in range(2) for k in (k0, k1)]
        block = jnp.concatenate(pieces, 0).T
        for i in range(8):
            a = block[i * 16 : i * 16 + 8]
            b = block[i * 16 + 8 : i * 16 + 16]
            e_ref[i + 1, k0] = jnp.where(low_q, a, roll(b, 32))
            e_ref[i + 1, k1] = jnp.where(low_q, roll(a, 96), b)
    for half in range(2):
        pieces = [ft[pl.ds(half * 4 + k, 32, stride=8), :] for k in range(4)]
        block = jnp.concatenate(pieces, 0).T
        a, b = block[:8], block[8:16]
        for t in range(4):
            k = half * 4 + t
            got = jnp.where(low_q, roll(a, -32 * t), roll(b, 32 - 32 * t))
            below = jnp.where(gx == 1, got, 0.0)
            above = jnp.where(gx == 0, roll(got, 64), 0.0)
            e_ref[0, k] = jnp.where(high_p, roll(e_ref[8, k], 64), below)
            e_ref[9, k] = jnp.where(high_p, above, roll(e_ref[1, k], 64))
    upper = jnp.zeros((8, 128), F32)
    lower = jnp.zeros((8, 128), F32)
    for i in range(10):
        upper = jnp.where(slot == i, roll(e_ref[i, 7], i - 31), upper)
        lower = jnp.where(slot == i, roll(e_ref[i, 0], i), lower)
    za_ref[...] = jnp.where(even, upper, lower)
    zb_ref[...] = jnp.where(even, lower, upper)
    sums = []
    for i in range(8):
        weights = basis_ref[i]
        sums.append(chain((e_ref[i + 1, k], jnp.broadcast_to(weights[:, k : k + 1], (8, 128))) for k in range(8)))
    lanes = jnp.sum(total(sums), axis=0, keepdims=True)
    lane16, sub16 = iotas(16)
    spread = jnp.where(((lane16 & 31) >> 1) == sub16, jnp.broadcast_to(lanes, (16, 128)), 0.0)
    rhs = jnp.sum(spread, axis=1, keepdims=True)
    for level in range(sep_ref.shape[0]):
        part_ref[level : level + 1, :] = jnp.sum(sep_ref[level] * rhs, axis=0, keepdims=True)
    own = own_ref[...]
    coef = jnp.sum(own * rhs, axis=0, keepdims=True)
    ownsol_ref[...] = jnp.broadcast_to(jnp.sum(own * coef, axis=1, keepdims=True), (16, 128))


def z_halo(e_ref, za_ref, zb_ref, even, slot):
    from_above = jnp.where(even, za_ref[...], zb_ref[...])
    from_below = jnp.where(even, zb_ref[...], za_ref[...])
    first, last = [], []
    for i in range(10):
        first.append(jnp.where(slot == 0, roll(from_below, -i), roll(e_ref[i, 7], 1)))
        last.append(jnp.where(slot == 31, roll(from_above, 31 - i), roll(e_ref[i, 0], -1)))
    return first, last


def y_rows(first, last, e2_ref, scr):
    for i in range(10):
        scr[pl.ds(i * 8, 8), :] = first[i]
        scr[pl.ds(128 + i * 8, 8), :] = last[i]
    low = [e2_ref[pl.ds(i * 64, 8, stride=8), :] for i in range(10)]
    high = [e2_ref[pl.ds(i * 64 + 7, 8, stride=8), :] for i in range(10)]
    low_ends = [scr[pl.ds(b, 16, stride=8), :] for b in (0, 128)]
    high_ends = [scr[pl.ds(b + 7, 16, stride=8), :] for b in (0, 128)]
    return low, high, low_ends, high_ends


def yface_kernel(e_ref, e2_ref, za_ref, zb_ref, ya_ref, yb_ref, scr):
    even_z = lax.rem(lax.axis_index("gz"), 2) == 0
    even_y = lax.rem(lax.axis_index("gy"), 2) == 0
    lane, _ = iotas()
    low_q = (lane & 32) == 0
    first, last = z_halo(e_ref, za_ref, zb_ref, even_z, lane & 31)
    low, high, low_ends, high_ends = y_rows(first, last, e2_ref, scr)
    for i in range(5):
        down = jnp.where(low_q, low[i], roll(low[i + 5], 32))
        up = jnp.where(low_q, roll(high[i + 5], 96), high[i])
        ya_ref[i * 8 : i * 8 + 8] = jnp.where(even_y, up, down)
        yb_ref[i * 8 : i * 8 + 8] = jnp.where(even_y, down, up)
    low_q = (iotas(16)[0] & 32) == 0
    down = jnp.where(low_q, low_ends[0], roll(low_ends[1], 32))
    up = jnp.where(low_q, roll(high_ends[1], 96), high_ends[0])
    ya_ref[40:56] = jnp.where(even_y, up, down)
    yb_ref[40:56] = jnp.where(even_y, down, up)


def solve_kernel(
    e_ref, e2_ref, za_ref, zb_ref, ya_ref, yb_ref, vec_ref, eig_ref,
    l_ref, hl_ref, hh_ref, xs_ref, core, jl, jh, u, s, eg, scr,
):
    gx = lax.axis_index("gx")
    even_z = lax.rem(lax.axis_index("gz"), 2) == 0
    even_y = lax.rem(lax.axis_index("gy"), 2) == 0
    lane, sub = iotas()
    low_q = (lane & 32) == 0
    first, last = z_halo(e_ref, za_ref, zb_ref, even_z, lane & 31)
    low, high, low_ends, high_ends = y_rows(first, last, e2_ref, scr)
    for i in range(10):
        core[pl.ds(i * 80, 8), :] = first[i]
        core[pl.ds(i * 80 + 72, 8), :] = last[i]
        for k in range(8):
            core[pl.ds(i * 80 + 8 + k * 8, 8), :] = e_ref[i, k]
    for i in range(10):
        at = (i % 5) * 8
        a = ya_ref[at : at + 8]
        b = yb_ref[at : at + 8]
        above = jnp.where(even_y, a, b)
        below = jnp.where(even_y, b, a)
        if i < 5:
            above, below = roll(above, 32), roll(below, 96)
        jl[pl.ds(i * 8, 8), :] = jnp.where(low_q, below, roll(high[i], 32))
        jh[pl.ds(i * 8, 8), :] = jnp.where(low_q, roll(low[i], 96), above)
    low_q16 = (iotas(16)[0] & 32) == 0
    above = jnp.where(even_y, ya_ref[40:56], yb_ref[40:56])
    below = jnp.where(even_y, yb_ref[40:56], ya_ref[40:56])
    jl[80:96] = jnp.where(low_q16, roll(below, 96), roll(high_ends[0], 32))
    jl[96:112] = jnp.where(low_q16, below, roll(high_ends[1], 32))
    jh[80:96] = jnp.where(low_q16, roll(low_ends[0], 96), roll(above, 32))
    jh[96:112] = jnp.where(low_q16, roll(low_ends[1], 96), above)
    for d in range(3):
        eg[d * 16 : d * 16 + 16] = jnp.zeros((16, 128), F32)
        eg[d * 16 : d * 16 + 10] = eig_ref[d]
        for i in range(10):
            at = (d * 10 + i) * 16
            s[at : at + 16] = jnp.zeros((16, 128), F32)
            s[at : at + 10] = vec_ref[d, i].astype(F32)

    def factor(d, i, a):
        return row(s, (d * 10 + i) * 16 + a)

    def fwd_y(i, _):
        for k in range(10):
            edge = i * 8 + k - 1 if 1 <= k <= 8 else (80 + i if k == 0 else 96 + i)
            at = (i * 10 + k) * 8
            rows = [row(jl, edge)] + [row(core, at + j) for j in range(8)] + [row(jh, edge)]
            for h in range(2):
                out = chain((s[(10 + j) * 16 + 8 * h : (10 + j) * 16 + 8 * h + 8], rows[j]) for j in range(10))
                u[pl.ds((i * 10 + k) * 16 + 8 * h, 8), :] = out
        return 0

    lax.fori_loop(0, 10, fwd_y, 0)

    def along_x(transposed):
        def step(k, _):
            for h in range(2):
                at = k * 16 + 8 * h
                held = [u[pl.ds(i * 160 + at, 8), :] for i in range(10)]
                for a in range(10):
                    u[pl.ds(a * 160 + at, 8), :] = chain(
                        (factor(0, a, i) if transposed else factor(0, i, a), held[i]) for i in range(10)
                    )
            return 0

        lax.fori_loop(0, 10, step, 0)

    along_x(False)

    def along_z(a, _):
        for h in range(2):
            at = a * 160 + 8 * h
            held = [u[pl.ds(at + k * 16, 8), :] for k in range(10)]
            base = row(eg, a) + eg[16 + 8 * h : 24 + 8 * h]
            modes = []
            for c in range(10):
                modes.append(chain((factor(2, k, c), held[k]) for k in range(10)) / (base + row(eg, 32 + c)))
            for k in range(10):
                u[pl.ds(at + k * 16, 8), :] = chain((factor(2, k, c), modes[c]) for c in range(10))
        return 0

    lax.fori_loop(0, 10, along_z, 0)
    along_x(True)
    back = [s[pl.ds(11 * 16 + b, 8, stride=16), :] for b in range(10)]

    def back_y(i, _):
        for k in range(10):
            at = (i * 10 + k) * 16
            l_ref[i, k] = chain((back[b], row(u, at + b)) for b in range(10))
        for h in range(2):
            cut = [u[pl.ds(i * 160 + 128 * h + b, 8, stride=16), :] for b in range(10)]
            hl_ref[i, 8 * h : 8 * h + 8] = chain((factor(1, 0, b), cut[b]) for b in range(10))
            hh_ref[i, 8 * h : 8 * h + 8] = chain((factor(1, 9, b), cut[b]) for b in range(10))
        return 0

    lax.fori_loop(0, 10, back_y, 0)
    high_p = lane >= 64

    def outgoing(ref, k):
        return jnp.where(gx == 0, ref[9, k], roll(ref[0, k], 64))

    for k in range(5):
        xs_ref[k * 8 : k * 8 + 8] = jnp.where(high_p, outgoing(l_ref, k), roll(outgoing(l_ref, k + 5), 64))
    high_p = iotas(16)[0] >= 64
    edge_l = jnp.where(gx == 0, hl_ref[9], roll(hl_ref[0], 64))
    edge_h = jnp.where(gx == 0, hh_ref[9], roll(hh_ref[0], 64))
    xs_ref[40:56] = jnp.where(high_p, edge_l, roll(edge_h, 64))


def fold_x(value, i, opposite, received, gx, high_p):
    if i == 8:
        return value + jnp.where(high_p, jnp.where(gx == 0, received, 0.0), roll(opposite, 64))
    if i == 1:
        return value + jnp.where(high_p, roll(opposite, 64), jnp.where(gx == 1, roll(received, 64), 0.0))
    return value


def edge_rows(hl_ref, hh_ref, xr_ref, gx):
    high_p = iotas(16)[0] >= 64
    packed = xr_ref[40:56]
    low, high = [], []
    for i in range(1, 9):
        j = {1: 9, 8: 0}.get(i, i)
        low.append(fold_x(hl_ref[i], i, hl_ref[j], packed, gx, high_p))
        high.append(fold_x(hh_ref[i], i, hh_ref[j], roll(packed, 64), gx, high_p))
    return low, high


def yfold_send_kernel(hl_ref, hh_ref, xr_ref, ya_ref, yb_ref):
    gx = lax.axis_index("gx")
    even_y = lax.rem(lax.axis_index("gy"), 2) == 0
    low_q = (iotas(16)[0] & 32) == 0
    low, high = edge_rows(hl_ref, hh_ref, xr_ref, gx)
    for i in range(4):
        down = jnp.where(low_q, low[i], roll(low[i + 4], 32))
        up = jnp.where(low_q, roll(high[i + 4], 96), high[i])
        ya_ref[i * 16 : i * 16 + 16] = jnp.where(even_y, up, down)
        yb_ref[i * 16 : i * 16 + 16] = jnp.where(even_y, down, up)


def fold_rows(hl_ref, hh_ref, xr_ref, ya_ref, yb_ref, rows_first, rows_last, gx):
    even_y = lax.rem(lax.axis_index("gy"), 2) == 0
    low_q = (iotas(16)[0] & 32) == 0
    low, high = edge_rows(hl_ref, hh_ref, xr_ref, gx)
    for i in range(8):
        at = (i % 4) * 16
        a = ya_ref[at : at + 16]
        b = yb_ref[at : at + 16]
        above = jnp.where(even_y, a, b)
        below = jnp.where(even_y, b, a)
        if i < 4:
            above, below = roll(above, 32), roll(below, 96)
        rows_last[pl.ds(i * 16, 16), :] = jnp.where(low_q, roll(low[i], 96), above)
        rows_first[pl.ds(i * 16, 16), :] = jnp.where(low_q, below, roll(high[i], 32))


def folded_xy(l_ref, xr_ref, rows_first, rows_last, i, k, gx, lane, sub):
    high_p = lane >= 64
    value = l_ref[i, k]
    if i in (1, 8):
        packed = xr_ref[(k % 5) * 8 : (k % 5) * 8 + 8]
        received = packed if k < 5 else roll(packed, 64)
        value = fold_x(value, i, l_ref[9 if i == 1 else 0, k], received, gx, high_p)
    at = (i - 1) * 16 + k
    return value + jnp.where(sub == 0, row(rows_first, at), jnp.where(sub == 7, row(rows_last, at), 0.0))


def zfold_send_kernel(l_ref, hl_ref, hh_ref, xr_ref, ya_ref, yb_ref, za_ref, zb_ref, rows_first, rows_last):
    gx = lax.axis_index("gx")
    even_z = lax.rem(lax.axis_index("gz"), 2) == 0
    lane, sub = iotas()
    slot = lane & 31
    fold_rows(hl_ref, hh_ref, xr_ref, ya_ref, yb_ref, rows_first, rows_last, gx)
    down = jnp.zeros((8, 128), F32)
    up = jnp.zeros((8, 128), F32)
    for i in range(8):
        down = jnp.where(slot == i, roll(folded_xy(l_ref, xr_ref, rows_first, rows_last, i + 1, 0, gx, lane, sub), i), down)
        up = jnp.where(slot == i, roll(folded_xy(l_ref, xr_ref, rows_first, rows_last, i + 1, 9, gx, lane, sub), i - 31), up)
    za_ref[...] = jnp.where(even_z, up, down)
    zb_ref[...] = jnp.where(even_z, down, up)


def post_kernel(
    l_ref, hl_ref, hh_ref, xr_ref, ya_ref, yb_ref, za_ref, zb_ref, basis_ref, sep_ref, run_ref, ownsol_ref,
    out_ref, rows_first, rows_last, xt, grid,
):
    gx = lax.axis_index("gx")
    even_z = lax.rem(lax.axis_index("gz"), 2) == 0
    lane, sub = iotas()
    slot = lane & 31
    low_q = (lane & 32) == 0
    fold_rows(hl_ref, hh_ref, xr_ref, ya_ref, yb_ref, rows_first, rows_last, gx)
    weighted = total(sep_ref[level] * run_ref[level : level + 1, :] for level in range(sep_ref.shape[0]))
    solution_col = ownsol_ref[:, :1] + jnp.sum(weighted, axis=1, keepdims=True)
    lane16, sub16 = iotas(16)
    spread = jnp.where(((lane16 & 31) >> 1) == sub16, jnp.broadcast_to(solution_col, (16, 128)), 0.0)
    per_element = jnp.broadcast_to(jnp.sum(spread, axis=0, keepdims=True), (8, 128))
    from_above = jnp.where(even_z, za_ref[...], zb_ref[...])
    from_below = jnp.where(even_z, zb_ref[...], za_ref[...])
    for i in range(8):
        weights = basis_ref[i]
        get = functools.partial(folded_xy, l_ref, xr_ref, rows_first, rows_last, i + 1, gx=gx, lane=lane, sub=sub)
        before, after = get(0), get(9)
        for k in range(8):
            value = get(k + 1) + jnp.broadcast_to(weights[:, k : k + 1], (8, 128)) * per_element
            if k == 0:
                value = value + jnp.where(slot == 0, roll(from_below, -i), roll(after, 1))
            if k == 7:
                value = value + jnp.where(slot == 31, roll(from_above, 31 - i), roll(before, -1))
            grid[i, k] = value
    for pair in range(4):
        k0, k1 = 2 * pair, 2 * pair + 1
        pieces = []
        for i in range(8):
            c0, c1 = grid[i, k0], grid[i, k1]
            pieces.append(jnp.where(low_q, c0, roll(c1, 32)))
            pieces.append(jnp.where(low_q, roll(c0, 96), c1))
        block = jnp.concatenate(pieces, 0).T
        for p in range(2):
            for t, k in enumerate((k0, k1)):
                at = p * 64 + t * 32
                xt[p, pl.ds(k, 32, stride=8), :] = block[at : at + 32]
    out_ref[...] = jnp.concatenate([xt[0], xt[1]], 1).T


def call(kernel, outs, scratch, n_in, name):
    return pl.pallas_call(
        kernel,
        out_shape=[jax.ShapeDtypeStruct(shape, F32) for shape in outs],
        in_specs=[VM] * n_in,
        out_specs=[VM] * len(outs),
        scratch_shapes=[pltpu.VMEM(shape, F32) for shape in scratch],
        name=name,
    )


def swap(value, axis, distance):
    return lax.ppermute(value, axis, [(i, i ^ distance) for i in range(lax.axis_size(axis))])


def swap_odd(value, axis):
    pairs = []
    for i in range(1, lax.axis_size(axis) - 1, 2):
        pairs += [(i, i + 1), (i + 1, i)]
    return lax.ppermute(value, axis, pairs)


def on_device(residual, fdm_vectors, fdm_eigen, coarse_basis, x_interior, x_separator):
    levels, unknowns, width = x_separator.shape[3:]
    x = residual.reshape(256, 256)
    vectors = fdm_vectors.reshape(3, 10, 10, 128)
    eigen = fdm_eigen.reshape(3, 10, 128)
    own = x_interior.reshape(unknowns, unknowns)
    sep = x_separator.reshape(levels, unknowns, width)
    gx = lax.axis_index("gx")
    xface = swap(jnp.where(gx == 0, residual[15], residual[0]), "gx", 1)

    e, za, zb, running, ownsol = call(
        pre_kernel,
        [(10, 8, 8, 128), (8, 128), (8, 128), (levels, width), (16, 128)],
        [(2, 256, 128), (256, 128)],
        5,
        "pre",
    )(x, xface, coarse_basis, own, sep)

    row_of = lax.broadcasted_iota(jnp.int32, running.shape, 0)
    done = 0

    def climb(running, axis, distance):
        nonlocal done
        partner = swap(running, axis, distance)
        running = running + jnp.where(row_of >= done, partner, 0.0)
        done += 1
        return running

    za, zb = swap(za, "gz", 1), swap_odd(zb, "gz")
    for axis in ("gz", "gy", "gx"):
        distance = 1
        while distance < lax.axis_size(axis):
            running = climb(running, axis, distance)
            distance *= 2

    e2 = e.reshape(640, 128)
    ya, yb = call(yface_kernel, [(56, 128)] * 2, [(256, 128)], 4, "yface")(e, e2, za, zb)
    ya, yb = swap(ya, "gy", 1), swap_odd(yb, "gy")
    local, edge_l, edge_h, xs = call(
        solve_kernel,
        [(10, 10, 8, 128), (10, 16, 128), (10, 16, 128), (56, 128)],
        [(800, 128), (112, 128), (112, 128), (1696, 128), (480, 128), (48, 128), (256, 128)],
        8,
        "solve",
    )(e, e2, za, zb, ya, yb, vectors, eigen)
    xr = swap(xs, "gx", 1)
    ya, yb = call(yfold_send_kernel, [(64, 128)] * 2, [], 3, "yfold")(edge_l, edge_h, xr)
    ya, yb = swap(ya, "gy", 1), swap_odd(yb, "gy")
    za, zb = call(zfold_send_kernel, [(8, 128)] * 2, [(128, 128)] * 2, 6, "zfold")(local, edge_l, edge_h, xr, ya, yb)
    za, zb = swap(za, "gz", 1), swap_odd(zb, "gz")
    (out,) = call(
        post_kernel,
        [(256, 256)],
        [(128, 128), (128, 128), (2, 256, 128), (8, 8, 8, 128)],
        12,
        "post",
    )(local, edge_l, edge_h, xr, ya, yb, za, zb, coarse_basis, sep, running, ownsol)
    return out.reshape(residual.shape)


def solution(mesh):
    in_specs = (
        P("gx", "gy", "gz"),
        P("gx", "gy", "gz", None, None, None, None),
        P("gx", "gy", "gz", None, None, None),
        P(),
        P("gx", "gy", "gz", None, None),
        P("gx", "gy", "gz", None, None, None),
    )
    return jax.shard_map(
        on_device, mesh=mesh, in_specs=in_specs, out_specs=P("gx", "gy", "gz"), check_vma=False
    )
```

```python
import functools

import jax
import jax.numpy as jnp
from jax import lax
from jax.experimental import pallas as pl
from jax.experimental.pallas import tpu as pltpu
from jax.sharding import PartitionSpec as P


F32 = jnp.float32
VM = pl.BlockSpec(memory_space=pltpu.VMEM)


def iotas(rows=8):
    lane = lax.broadcasted_iota(jnp.int32, (rows, 128), 1)
    sub = lax.broadcasted_iota(jnp.int32, (rows, 128), 0)
    return lane, sub


def roll(value, shift):
    shift = shift % 128
    return value if shift == 0 else pltpu.roll(value, shift, value.ndim - 1)


def row(ref, index, rows=8):
    return jnp.broadcast_to(ref[pl.ds(index, 1), :], (rows, 128))


def total(terms):
    terms = list(terms)
    while len(terms) > 1:
        terms = [a + b for a, b in zip(terms[::2], terms[1::2])] + terms[len(terms) & ~1 :]
    return terms[0]


def chain(pairs):
    acc = None
    for a, b in pairs:
        acc = a * b if acc is None else acc + a * b
    return acc


def pre_kernel(x_ref, xface_ref, basis_ref, own_ref, sep_ref, e_ref, za_ref, zb_ref, run_ref, ownsol_ref, xt, ft):
    gx = lax.axis_index("gx")
    even = lax.rem(lax.axis_index("gz"), 2) == 0
    lane, _ = iotas()
    low_q = (lane & 32) == 0
    high_p = lane >= 64
    slot = lane & 31
    turned = x_ref[...].T
    xt[0] = turned[:, :128]
    xt[1] = turned[:, 128:]
    face = jnp.concatenate([xface_ref[...], jnp.zeros((112, 256), F32)], 0).T
    ft[...] = face
    for pair in range(4):
        k0, k1 = 2 * pair, 2 * pair + 1
        pieces = [xt[p, pl.ds(k, 32, stride=8), :] for p in range(2) for k in (k0, k1)]
        block = jnp.concatenate(pieces, 0).T
        for i in range(8):
            a = block[i * 16 : i * 16 + 8]
            b = block[i * 16 + 8 : i * 16 + 16]
            e_ref[i + 1, k0] = jnp.where(low_q, a, roll(b, 32))
            e_ref[i + 1, k1] = jnp.where(low_q, roll(a, 96), b)
    for half in range(2):
        pieces = [ft[pl.ds(half * 4 + k, 32, stride=8), :] for k in range(4)]
        block = jnp.concatenate(pieces, 0).T
        a, b = block[:8], block[8:16]
        for t in range(4):
            k = half * 4 + t
            got = jnp.where(low_q, roll(a, -32 * t), roll(b, 32 - 32 * t))
            below = jnp.where(gx == 1, got, 0.0)
            above = jnp.where(gx == 0, roll(got, 64), 0.0)
            e_ref[0, k] = jnp.where(high_p, roll(e_ref[8, k], 64), below)
            e_ref[9, k] = jnp.where(high_p, above, roll(e_ref[1, k], 64))
    upper = jnp.zeros((8, 128), F32)
    lower = jnp.zeros((8, 128), F32)
    for i in range(10):
        upper = jnp.where(slot == i, roll(e_ref[i, 7], i - 31), upper)
        lower = jnp.where(slot == i, roll(e_ref[i, 0], i), lower)
    za_ref[:8] = jnp.where(even, upper, lower)
    zb_ref[...] = jnp.where(even, lower, upper)
    sums = []
    for i in range(8):
        weights = basis_ref[i]
        sums.append(chain((e_ref[i + 1, k], jnp.broadcast_to(weights[:, k : k + 1], (8, 128))) for k in range(8)))
    lanes = jnp.sum(total(sums), axis=0, keepdims=True)
    lane16, sub16 = iotas(16)
    spread = jnp.where(((lane16 & 31) >> 1) == sub16, jnp.broadcast_to(lanes, (16, 128)), 0.0)
    rhs = jnp.sum(spread, axis=1, keepdims=True)
    for level in range(sep_ref.shape[0]):
        part = jnp.sum(sep_ref[level] * rhs, axis=0, keepdims=True)
        for h in range(2):
            run_ref[8 * h + level : 8 * h + level + 1, :] = part[:, h * 128 : h * 128 + 128]
    za_ref[8:24] = run_ref[...]
    own = own_ref[...]
    coef = jnp.sum(own * rhs, axis=0, keepdims=True)
    ownsol_ref[...] = jnp.broadcast_to(jnp.sum(own * coef, axis=1, keepdims=True), (16, 128))


def sides(a, b, axis):
    index = lax.axis_index(axis)
    even = lax.rem(index, 2) == 0
    above = jnp.where(index == lax.axis_size(axis) - 1, 0.0, jnp.where(even, a, b))
    below = jnp.where(index == 0, 0.0, jnp.where(even, b, a))
    return above, below


def z_halo(e_ref, za_ref, zb_ref, slot):
    from_above, from_below = sides(za_ref[:8], zb_ref[...], "gz")
    first, last = [], []
    for i in range(10):
        first.append(jnp.where(slot == 0, roll(from_below, -i), roll(e_ref[i, 7], 1)))
        last.append(jnp.where(slot == 31, roll(from_above, 31 - i), roll(e_ref[i, 0], -1)))
    return first, last


def y_rows(first, last, e2_ref, scr):
    for i in range(10):
        scr[pl.ds(i * 8, 8), :] = first[i]
        scr[pl.ds(128 + i * 8, 8), :] = last[i]
    low = [e2_ref[pl.ds(i * 64, 8, stride=8), :] for i in range(10)]
    high = [e2_ref[pl.ds(i * 64 + 7, 8, stride=8), :] for i in range(10)]
    low_ends = [scr[pl.ds(b, 16, stride=8), :] for b in (0, 128)]
    high_ends = [scr[pl.ds(b + 7, 16, stride=8), :] for b in (0, 128)]
    return low, high, low_ends, high_ends


def yface_kernel(e_ref, e2_ref, za_ref, zb_ref, part_ref, ya_ref, yb_ref, run_ref, scr):
    run_ref[...] = part_ref[...] + za_ref[8:24]
    ya_ref[56:72] = run_ref[...]
    even_y = lax.rem(lax.axis_index("gy"), 2) == 0
    lane, _ = iotas()
    low_q = (lane & 32) == 0
    first, last = z_halo(e_ref, za_ref, zb_ref, lane & 31)
    low, high, low_ends, high_ends = y_rows(first, last, e2_ref, scr)
    for i in range(5):
        down = jnp.where(low_q, low[i], roll(low[i + 5], 32))
        up = jnp.where(low_q, roll(high[i + 5], 96), high[i])
        ya_ref[i * 8 : i * 8 + 8] = jnp.where(even_y, up, down)
        yb_ref[i * 8 : i * 8 + 8] = jnp.where(even_y, down, up)
    low_q = (iotas(16)[0] & 32) == 0
    down = jnp.where(low_q, low_ends[0], roll(low_ends[1], 32))
    up = jnp.where(low_q, roll(high_ends[1], 96), high_ends[0])
    ya_ref[40:56] = jnp.where(even_y, up, down)
    yb_ref[40:56] = jnp.where(even_y, down, up)


def solve_kernel(
    e_ref, e2_ref, za_ref, zb_ref, ya_ref, yb_ref, vec_ref, eig_ref,
    l_ref, hl_ref, hh_ref, xs_ref, core, jl, jh, u, s, eg, scr,
):
    gx = lax.axis_index("gx")
    lane, _ = iotas()
    low_q = (lane & 32) == 0
    first, last = z_halo(e_ref, za_ref, zb_ref, lane & 31)
    low, high, low_ends, high_ends = y_rows(first, last, e2_ref, scr)
    for i in range(10):
        core[pl.ds(i * 80, 8), :] = first[i]
        core[pl.ds(i * 80 + 72, 8), :] = last[i]
        for k in range(8):
            core[pl.ds(i * 80 + 8 + k * 8, 8), :] = e_ref[i, k]
    for i in range(10):
        at = (i % 5) * 8
        above, below = sides(ya_ref[at : at + 8], yb_ref[at : at + 8], "gy")
        if i < 5:
            above, below = roll(above, 32), roll(below, 96)
        jl[pl.ds(i * 8, 8), :] = jnp.where(low_q, below, roll(high[i], 32))
        jh[pl.ds(i * 8, 8), :] = jnp.where(low_q, roll(low[i], 96), above)
    low_q16 = (iotas(16)[0] & 32) == 0
    above, below = sides(ya_ref[40:56], yb_ref[40:56], "gy")
    jl[80:96] = jnp.where(low_q16, roll(below, 96), roll(high_ends[0], 32))
    jl[96:112] = jnp.where(low_q16, below, roll(high_ends[1], 32))
    jh[80:96] = jnp.where(low_q16, roll(low_ends[0], 96), roll(above, 32))
    jh[96:112] = jnp.where(low_q16, roll(low_ends[1], 96), above)
    eg[...] = jnp.ones((16, 128), F32)
    for a in range(10):
        eg[a : a + 1] = eig_ref[1, a]
        for i in range(10):
            s[(i * 10 + a) * 8 : (i * 10 + a) * 8 + 3] = vec_ref[i, a].astype(F32)

    def factor(d, i, a):
        return row(s, (i * 10 + a) * 8 + d)

    def wide(value):
        return jnp.broadcast_to(value, (8, 128))

    front = [[s[pl.ds((j * 10 + 8 * h) * 8 + 1, 8, stride=8), :] for j in range(10)] for h in range(2)]

    def fwd_y(i, _):
        for k in range(10):
            edge = i * 8 + k - 1 if 1 <= k <= 8 else (80 + i if k == 0 else 96 + i)
            at = (i * 10 + k) * 8
            rows = [row(jl, edge)] + [row(core, at + j) for j in range(8)] + [row(jh, edge)]
            for h in range(2):
                out = chain((front[h][j], rows[j]) for j in range(10))
                u[pl.ds((i * 10 + k) * 16 + 8 * h, 8), :] = out
        return 0

    lax.fori_loop(0, 10, fwd_y, 0)

    def along_x(transposed):
        def step(k, _):
            for h in range(2):
                at = k * 16 + 8 * h
                held = [u[pl.ds(i * 160 + at, 8), :] for i in range(10)]
                for a in range(10):
                    u[pl.ds(a * 160 + at, 8), :] = chain(
                        (factor(0, a, i) if transposed else factor(0, i, a), held[i]) for i in range(10)
                    )
            return 0

        lax.fori_loop(0, 10, step, 0)

    along_x(False)

    def along_z(a, _):
        for h in range(2):
            at = a * 160 + 8 * h
            held = [u[pl.ds(at + k * 16, 8), :] for k in range(10)]
            base = wide(eig_ref[0, a]) + eg[8 * h : 8 * h + 8]
            modes = []
            for c in range(10):
                modes.append(chain((factor(2, k, c), held[k]) for k in range(10)) / (base + wide(eig_ref[2, c])))
            for k in range(10):
                u[pl.ds(at + k * 16, 8), :] = chain((factor(2, k, c), modes[c]) for c in range(10))
        return 0

    lax.fori_loop(0, 10, along_z, 0)
    along_x(True)
    back = [s[pl.ds((10 + b) * 8 + 1, 8, stride=80), :] for b in range(10)]

    def back_y(i, _):
        for k in range(10):
            at = (i * 10 + k) * 16
            l_ref[i, k] = chain((back[b], row(u, at + b)) for b in range(10))
        for h in range(2):
            cut = [u[pl.ds(i * 160 + 128 * h + b, 8, stride=16), :] for b in range(10)]
            hl_ref[i, 8 * h : 8 * h + 8] = chain((factor(1, 0, b), cut[b]) for b in range(10))
            hh_ref[i, 8 * h : 8 * h + 8] = chain((factor(1, 9, b), cut[b]) for b in range(10))
        return 0

    lax.fori_loop(0, 10, back_y, 0)
    high_p = lane >= 64

    def outgoing(ref, k):
        return jnp.where(gx == 0, ref[9, k], roll(ref[0, k], 64))

    for k in range(5):
        xs_ref[k * 8 : k * 8 + 8] = jnp.where(high_p, outgoing(l_ref, k), roll(outgoing(l_ref, k + 5), 64))
    high_p = iotas(16)[0] >= 64
    edge_l = jnp.where(gx == 0, hl_ref[9], roll(hl_ref[0], 64))
    edge_h = jnp.where(gx == 0, hh_ref[9], roll(hh_ref[0], 64))
    xs_ref[40:56] = jnp.where(high_p, edge_l, roll(edge_h, 64))


def fold_x(value, i, opposite, received, gx, high_p):
    if i == 8:
        return value + jnp.where(high_p, jnp.where(gx == 0, received, 0.0), roll(opposite, 64))
    if i == 1:
        return value + jnp.where(high_p, roll(opposite, 64), jnp.where(gx == 1, roll(received, 64), 0.0))
    return value


def edge_rows(hl_ref, hh_ref, xr_ref, gx):
    high_p = iotas(16)[0] >= 64
    packed = xr_ref[40:56]
    low, high = [], []
    for i in range(1, 9):
        j = {1: 9, 8: 0}.get(i, i)
        low.append(fold_x(hl_ref[i], i, hl_ref[j], packed, gx, high_p))
        high.append(fold_x(hh_ref[i], i, hh_ref[j], roll(packed, 64), gx, high_p))
    return low, high


def yfold_send_kernel(hl_ref, hh_ref, xr_ref, ya_ref, yb_ref):
    gx = lax.axis_index("gx")
    even_y = lax.rem(lax.axis_index("gy"), 2) == 0
    low_q = (iotas(16)[0] & 32) == 0
    low, high = edge_rows(hl_ref, hh_ref, xr_ref, gx)
    for i in range(4):
        down = jnp.where(low_q, low[i], roll(low[i + 4], 32))
        up = jnp.where(low_q, roll(high[i + 4], 96), high[i])
        ya_ref[i * 16 : i * 16 + 16] = jnp.where(even_y, up, down)
        yb_ref[i * 16 : i * 16 + 16] = jnp.where(even_y, down, up)


def fold_rows(hl_ref, hh_ref, xr_ref, ya_ref, yb_ref, rows_first, rows_last, gx):
    low_q = (iotas(16)[0] & 32) == 0
    low, high = edge_rows(hl_ref, hh_ref, xr_ref, gx)
    for i in range(8):
        at = (i % 4) * 16
        above, below = sides(ya_ref[at : at + 16], yb_ref[at : at + 16], "gy")
        if i < 4:
            above, below = roll(above, 32), roll(below, 96)
        rows_last[pl.ds(i * 16, 16), :] = jnp.where(low_q, roll(low[i], 96), above)
        rows_first[pl.ds(i * 16, 16), :] = jnp.where(low_q, below, roll(high[i], 32))


def folded_xy(l_ref, xr_ref, rows_first, rows_last, i, k, gx, lane, sub):
    high_p = lane >= 64
    value = l_ref[i, k]
    if i in (1, 8):
        packed = xr_ref[(k % 5) * 8 : (k % 5) * 8 + 8]
        received = packed if k < 5 else roll(packed, 64)
        value = fold_x(value, i, l_ref[9 if i == 1 else 0, k], received, gx, high_p)
    at = (i - 1) * 16 + k
    return value + jnp.where(sub == 0, row(rows_first, at), jnp.where(sub == 7, row(rows_last, at), 0.0))


def zfold_send_kernel(l_ref, hl_ref, hh_ref, xr_ref, ya_ref, yb_ref, za_ref, zb_ref, rows_first, rows_last):
    gx = lax.axis_index("gx")
    even_z = lax.rem(lax.axis_index("gz"), 2) == 0
    lane, sub = iotas()
    slot = lane & 31
    fold_rows(hl_ref, hh_ref, xr_ref, ya_ref, yb_ref, rows_first, rows_last, gx)
    down = jnp.zeros((8, 128), F32)
    up = jnp.zeros((8, 128), F32)
    for i in range(8):
        down = jnp.where(slot == i, roll(folded_xy(l_ref, xr_ref, rows_first, rows_last, i + 1, 0, gx, lane, sub), i), down)
        up = jnp.where(slot == i, roll(folded_xy(l_ref, xr_ref, rows_first, rows_last, i + 1, 9, gx, lane, sub), i - 31), up)
    za_ref[...] = jnp.where(even_z, up, down)
    zb_ref[...] = jnp.where(even_z, down, up)


def post_kernel(
    l_ref, hl_ref, hh_ref, xr_ref, ya_ref, yb_ref, za_ref, zb_ref, basis_ref, sep_ref, run_ref, ownsol_ref,
    out_ref, rows_first, rows_last, xt, grid,
):
    gx = lax.axis_index("gx")
    lane, sub = iotas()
    slot = lane & 31
    low_q = (lane & 32) == 0
    fold_rows(hl_ref, hh_ref, xr_ref, ya_ref, yb_ref, rows_first, rows_last, gx)
    weighted = total(
        sep_ref[level][:, h * 128 : h * 128 + 128] * run_ref[8 * h + level : 8 * h + level + 1, :]
        for h in range(2)
        for level in range(sep_ref.shape[0])
    )
    solution_col = ownsol_ref[:, :1] + jnp.sum(weighted, axis=1, keepdims=True)
    lane16, sub16 = iotas(16)
    spread = jnp.where(((lane16 & 31) >> 1) == sub16, jnp.broadcast_to(solution_col, (16, 128)), 0.0)
    per_element = jnp.broadcast_to(jnp.sum(spread, axis=0, keepdims=True), (8, 128))
    from_above, from_below = sides(za_ref[...], zb_ref[...], "gz")
    for i in range(8):
        weights = basis_ref[i]
        get = functools.partial(folded_xy, l_ref, xr_ref, rows_first, rows_last, i + 1, gx=gx, lane=lane, sub=sub)
        before, after = get(0), get(9)
        for k in range(8):
            value = get(k + 1) + jnp.broadcast_to(weights[:, k : k + 1], (8, 128)) * per_element
            if k == 0:
                value = value + jnp.where(slot == 0, roll(from_below, -i), roll(after, 1))
            if k == 7:
                value = value + jnp.where(slot == 31, roll(from_above, 31 - i), roll(before, -1))
            grid[i, k] = value
    for pair in range(4):
        k0, k1 = 2 * pair, 2 * pair + 1
        pieces = []
        for i in range(8):
            c0, c1 = grid[i, k0], grid[i, k1]
            pieces.append(jnp.where(low_q, c0, roll(c1, 32)))
            pieces.append(jnp.where(low_q, roll(c0, 96), c1))
        block = jnp.concatenate(pieces, 0).T
        for p in range(2):
            for t, k in enumerate((k0, k1)):
                at = p * 64 + t * 32
                xt[p, pl.ds(k, 32, stride=8), :] = block[at : at + 32]
    out_ref[...] = jnp.concatenate([xt[0], xt[1]], 1).T


def call(kernel, outs, scratch, n_in, limit=4 << 20):
    return pl.pallas_call(
        kernel,
        out_shape=[jax.ShapeDtypeStruct(shape, F32) for shape in outs],
        in_specs=[VM] * n_in,
        out_specs=[VM] * len(outs),
        scratch_shapes=[pltpu.VMEM(shape, F32) for shape in scratch],
        compiler_params=pltpu.CompilerParams(vmem_limit_bytes=limit),
    )


def swap(value, axis, distance):
    return lax.ppermute(value, axis, [(i, i ^ distance) for i in range(lax.axis_size(axis))])


def swap_odd(value, axis):
    count = lax.axis_size(axis)
    return lax.ppermute(value, axis, [(i, (i + 1 if i % 2 else i - 1) % count) for i in range(count)])


def work(residual, fdm_vectors, fdm_eigen, coarse_basis, x_interior, x_separator):
    levels, unknowns, width = x_separator.shape[3:]
    x = residual.reshape(256, 256)
    vectors = fdm_vectors.reshape(3, 10, 10, 128).transpose(1, 2, 0, 3)
    eigen = fdm_eigen.reshape(3, 10, 1, 128)
    own = x_interior.reshape(unknowns, unknowns)
    sep = x_separator.reshape(levels, unknowns, width)
    gx = lax.axis_index("gx")
    level_of = lax.broadcasted_iota(jnp.int32, (16, 128), 0) & 7

    def climb(running, axis, bit, first):
        return running + jnp.where(level_of >= first, swap(running, axis, 1 << bit), 0.0)

    def climb_two(running, axis, bit, first):
        one, two, three = (swap(running, axis, d << bit) for d in (1, 2, 3))
        return running + jnp.where(level_of > first, one + (two + three), jnp.where(level_of == first, one, 0.0))

    xface = swap(jnp.where(gx == 0, residual[15], residual[0]), "gx", 1)
    e, za, zb, partial, ownsol = call(
        pre_kernel, [(10, 8, 8, 128), (24, 128), (8, 128), (16, 128), (16, 128)], [(2, 256, 128), (256, 128)], 5
    )(x, xface, coarse_basis, own, sep)
    za, zb = swap(za, "gz", 1), swap_odd(zb, "gz")
    e2 = e.reshape(640, 128)
    ya, yb, running = call(yface_kernel, [(72, 128), (56, 128), (16, 128)], [(256, 128)], 5)(e, e2, za, zb, partial)
    ya, yb = swap(ya, "gy", 1), swap_odd(yb, "gy")
    running = running + jnp.where(level_of >= 4, ya[56:72], 0.0)
    running = climb_two(running, "gy", 1, 5)
    local, edge_l, edge_h, xs = call(
        solve_kernel,
        [(10, 10, 8, 128), (10, 16, 128), (10, 16, 128), (56, 128)],
        [(800, 128), (112, 128), (112, 128), (1696, 128), (848, 128), (16, 128), (256, 128)],
        8,
    )(e, e2, za, zb, ya, yb, vectors, eigen)
    xr = swap(xs, "gx", 1)
    running = climb(running, "gx", 0, 7)
    ya, yb = call(yfold_send_kernel, [(64, 128)] * 2, [], 3)(edge_l, edge_h, xr)
    ya, yb = swap(ya, "gy", 1), swap_odd(yb, "gy")
    running = climb_two(running, "gz", 1, 1)
    za, zb = call(zfold_send_kernel, [(8, 128)] * 2, [(128, 128)] * 2, 6)(local, edge_l, edge_h, xr, ya, yb)
    za, zb = swap(za, "gz", 1), swap_odd(zb, "gz")
    running = climb(running, "gz", 3, 3)
    (out,) = call(
        post_kernel, [(256, 256)], [(128, 128), (128, 128), (2, 256, 128), (8, 8, 8, 128)], 12
    )(local, edge_l, edge_h, xr, ya, yb, za, zb, coarse_basis, sep, running, ownsol)
    return out.reshape(residual.shape)


def solution(mesh):
    in_specs = (
        P("gx", "gy", "gz"),
        P("gx", "gy", "gz", None, None, None, None),
        P("gx", "gy", "gz", None, None, None),
        P(),
        P("gx", "gy", "gz", None, None),
        P("gx", "gy", "gz", None, None, None),
    )
    return jax.shard_map(work, mesh=mesh, in_specs=in_specs, out_specs=P("gx", "gy", "gz"), check_vma=False)
```

```python
import functools

import jax
import jax.numpy as jnp
from jax import lax
from jax.experimental import pallas as pl
from jax.experimental.pallas import tpu as pltpu
from jax.sharding import PartitionSpec as P


F32 = jnp.float32
VM = pl.BlockSpec(memory_space=pltpu.VMEM)


def iotas(rows=8):
    lane = lax.broadcasted_iota(jnp.int32, (rows, 128), 1)
    sub = lax.broadcasted_iota(jnp.int32, (rows, 128), 0)
    return lane, sub


def roll(value, shift):
    shift = shift % 128
    return value if shift == 0 else pltpu.roll(value, shift, value.ndim - 1)


def row(ref, index, rows=8):
    return jnp.broadcast_to(ref[pl.ds(index, 1), :], (rows, 128))


def total(terms):
    terms = list(terms)
    while len(terms) > 1:
        terms = [a + b for a, b in zip(terms[::2], terms[1::2])] + terms[len(terms) & ~1 :]
    return terms[0]


def chain(pairs):
    acc = None
    for a, b in pairs:
        acc = a * b if acc is None else acc + a * b
    return acc


def pre_kernel(
    x_ref, sep_ref, basis_ref, own_ref, core_ref, xs_ref, run_ref, ownsol_ref, xv, xt, sepv, basisv, ownv, xsem, sems
):
    copies = [pltpu.make_async_copy(x_ref.at[pl.ds(p * 128, 128), :], xv.at[p], xsem.at[p]) for p in range(2)]
    small = [
        pltpu.make_async_copy(a, b, sems.at[n])
        for n, (a, b) in enumerate(((basis_ref, basisv), (own_ref, ownv), (sep_ref, sepv)))
    ]
    for copy in copies + small:
        copy.start()
    gx = lax.axis_index("gx")
    lane, _ = iotas()
    low_q = (lane & 32) == 0
    high_p = lane >= 64
    for p in range(2):
        copies[p].wait()
        xt[p] = xv[p].T
    for pair in range(4):
        k0, k1 = 2 * pair, 2 * pair + 1
        pieces = [xt[p, pl.ds(k, 32, stride=8), :] for p in range(2) for k in (k0, k1)]
        block = jnp.concatenate(pieces, 0).T
        for i in range(8):
            a = block[i * 16 : i * 16 + 8]
            b = block[i * 16 + 8 : i * 16 + 16]
            core_ref[i, k0] = jnp.where(low_q, a, roll(b, 32))
            core_ref[i, k1] = jnp.where(low_q, roll(a, 96), b)

    def outgoing(k):
        return jnp.where(gx == 0, core_ref[7, k], roll(core_ref[0, k], 64))

    for k in range(4):
        xs_ref[k * 8 : k * 8 + 8] = jnp.where(high_p, outgoing(k), roll(outgoing(k + 4), 64))
    small[0].wait()
    sums = []
    for i in range(8):
        weights = basisv[i]
        sums.append(chain((core_ref[i, k], jnp.broadcast_to(weights[:, k : k + 1], (8, 128))) for k in range(8)))
    lanes = jnp.sum(total(sums), axis=0, keepdims=True)
    lane16, sub16 = iotas(16)
    spread = jnp.where(((lane16 & 31) >> 1) == sub16, jnp.broadcast_to(lanes, (16, 128)), 0.0)
    rhs = jnp.sum(spread, axis=1, keepdims=True)
    small[1].wait()
    own = ownv[...]
    coef = jnp.sum(own * rhs, axis=0, keepdims=True)
    ownsol_ref[...] = jnp.broadcast_to(jnp.sum(own * coef, axis=1, keepdims=True), (16, 128))
    small[2].wait()
    for level in range(sep_ref.shape[0]):
        part = jnp.sum(sepv[level] * rhs, axis=0, keepdims=True)
        for h in range(2):
            run_ref[8 * h + level : 8 * h + level + 1, :] = part[:, h * 128 : h * 128 + 128]


def zface_kernel(core_ref, xr_ref, ends_ref, za_ref, zb_ref):
    gx = lax.axis_index("gx")
    even = lax.rem(lax.axis_index("gz"), 2) == 0
    lane, _ = iotas()
    high_p = lane >= 64
    slot = lane & 31
    for k in range(8):
        at = (k % 4) * 8
        got = xr_ref[at : at + 8]
        if k >= 4:
            got = roll(got, 64)
        ends_ref[0, k] = jnp.where(high_p, roll(core_ref[7, k], 64), jnp.where(gx == 1, roll(got, 64), 0.0))
        ends_ref[1, k] = jnp.where(high_p, jnp.where(gx == 0, got, 0.0), roll(core_ref[0, k], 64))
    upper = jnp.zeros((8, 128), F32)
    lower = jnp.zeros((8, 128), F32)
    for i in range(10):
        upper = jnp.where(slot == i, roll(plane(core_ref, ends_ref, i, 7), i - 31), upper)
        lower = jnp.where(slot == i, roll(plane(core_ref, ends_ref, i, 0), i), lower)
    za_ref[...] = jnp.where(even, upper, lower)
    zb_ref[...] = jnp.where(even, lower, upper)


def plane(core_ref, ends_ref, i, k):
    return core_ref[i - 1, k] if 1 <= i <= 8 else ends_ref[i // 9, k]


def sides(a, b, axis):
    index = lax.axis_index(axis)
    even = lax.rem(index, 2) == 0
    above = jnp.where(index == lax.axis_size(axis) - 1, 0.0, jnp.where(even, a, b))
    below = jnp.where(index == 0, 0.0, jnp.where(even, b, a))
    return above, below


def z_halo(core_ref, ends_ref, za_ref, zb_ref, slot):
    from_above, from_below = sides(za_ref[...], zb_ref[...], "gz")
    first, last = [], []
    for i in range(10):
        first.append(jnp.where(slot == 0, roll(from_below, -i), roll(plane(core_ref, ends_ref, i, 7), 1)))
        last.append(jnp.where(slot == 31, roll(from_above, 31 - i), roll(plane(core_ref, ends_ref, i, 0), -1)))
    return first, last


def y_rows(first, last, core2_ref, ends2_ref, scr):
    for i in range(10):
        scr[pl.ds(i * 8, 8), :] = first[i]
        scr[pl.ds(128 + i * 8, 8), :] = last[i]
    low, high = [], []
    for i in range(10):
        ref, at = (core2_ref, (i - 1) * 64) if 1 <= i <= 8 else (ends2_ref, (i // 9) * 64)
        low.append(ref[pl.ds(at, 8, stride=8), :])
        high.append(ref[pl.ds(at + 7, 8, stride=8), :])
    low_ends = [scr[pl.ds(b, 16, stride=8), :] for b in (0, 128)]
    high_ends = [scr[pl.ds(b + 7, 16, stride=8), :] for b in (0, 128)]
    return low, high, low_ends, high_ends


def yface_kernel(core_ref, core2_ref, ends_ref, ends2_ref, za_ref, zb_ref, run_ref, ya_ref, yb_ref, scr):
    ya_ref[56:72] = run_ref[...]
    even_y = lax.rem(lax.axis_index("gy"), 2) == 0
    lane, _ = iotas()
    low_q = (lane & 32) == 0
    first, last = z_halo(core_ref, ends_ref, za_ref, zb_ref, lane & 31)
    low, high, low_ends, high_ends = y_rows(first, last, core2_ref, ends2_ref, scr)
    for i in range(5):
        down = jnp.where(low_q, low[i], roll(low[i + 5], 32))
        up = jnp.where(low_q, roll(high[i + 5], 96), high[i])
        ya_ref[i * 8 : i * 8 + 8] = jnp.where(even_y, up, down)
        yb_ref[i * 8 : i * 8 + 8] = jnp.where(even_y, down, up)
    low_q = (iotas(16)[0] & 32) == 0
    down = jnp.where(low_q, low_ends[0], roll(low_ends[1], 32))
    up = jnp.where(low_q, roll(high_ends[1], 96), high_ends[0])
    ya_ref[40:56] = jnp.where(even_y, up, down)
    yb_ref[40:56] = jnp.where(even_y, down, up)


def load_factors(vec_ref, s):
    for a in range(10):
        for i in range(10):
            s[(i * 10 + a) * 8 : (i * 10 + a) * 8 + 3] = vec_ref[i, a].astype(F32)

    def factor(d, i, a):
        return row(s, (i * 10 + a) * 8 + d)

    return factor


def along_x(source, target, factor, transposed):
    def step(k, _):
        for h in range(2):
            at = k * 16 + 8 * h
            held = [source[pl.ds(i * 160 + at, 8), :] for i in range(10)]
            for a in range(10):
                target[pl.ds(a * 160 + at, 8), :] = chain(
                    (factor(0, a, i) if transposed else factor(0, i, a), held[i]) for i in range(10)
                )
        return 0

    lax.fori_loop(0, 10, step, 0)


def modes_kernel(
    core_ref, core2_ref, ends_ref, ends2_ref, za_ref, zb_ref, ya_ref, yb_ref, vec_ref, eig_ref,
    u, block, jl, jh, s, eg, scr,
):
    lane, _ = iotas()
    low_q = (lane & 32) == 0
    first, last = z_halo(core_ref, ends_ref, za_ref, zb_ref, lane & 31)
    low, high, low_ends, high_ends = y_rows(first, last, core2_ref, ends2_ref, scr)
    for i in range(10):
        block[pl.ds(i * 80, 8), :] = first[i]
        block[pl.ds(i * 80 + 72, 8), :] = last[i]
        for k in range(8):
            block[pl.ds(i * 80 + 8 + k * 8, 8), :] = plane(core_ref, ends_ref, i, k)
    for i in range(10):
        at = (i % 5) * 8
        above, below = sides(ya_ref[at : at + 8], yb_ref[at : at + 8], "gy")
        if i < 5:
            above, below = roll(above, 32), roll(below, 96)
        jl[pl.ds(i * 8, 8), :] = jnp.where(low_q, below, roll(high[i], 32))
        jh[pl.ds(i * 8, 8), :] = jnp.where(low_q, roll(low[i], 96), above)
    low_q16 = (iotas(16)[0] & 32) == 0
    above, below = sides(ya_ref[40:56], yb_ref[40:56], "gy")
    jl[80:96] = jnp.where(low_q16, roll(below, 96), roll(high_ends[0], 32))
    jl[96:112] = jnp.where(low_q16, below, roll(high_ends[1], 32))
    jh[80:96] = jnp.where(low_q16, roll(low_ends[0], 96), roll(above, 32))
    jh[96:112] = jnp.where(low_q16, roll(low_ends[1], 96), above)
    eg[...] = jnp.ones((16, 128), F32)
    for a in range(10):
        eg[a : a + 1] = eig_ref[1, a]
    factor = load_factors(vec_ref, s)

    def wide(value):
        return jnp.broadcast_to(value, (8, 128))

    front = [[s[pl.ds((j * 10 + 8 * h) * 8 + 1, 8, stride=8), :] for j in range(10)] for h in range(2)]

    def fwd_y(i, _):
        for k in range(10):
            edge = i * 8 + k - 1 if 1 <= k <= 8 else (80 + i if k == 0 else 96 + i)
            at = (i * 10 + k) * 8
            rows = [row(jl, edge)] + [row(block, at + j) for j in range(8)] + [row(jh, edge)]
            for h in range(2):
                out = chain((front[h][j], rows[j]) for j in range(10))
                u[pl.ds((i * 10 + k) * 16 + 8 * h, 8), :] = out
        return 0

    lax.fori_loop(0, 10, fwd_y, 0)

    along_x(u, u, factor, False)

    def along_z(a, _):
        for h in range(2):
            at = a * 160 + 8 * h
            held = [u[pl.ds(at + k * 16, 8), :] for k in range(10)]
            base = wide(eig_ref[0, a]) + eg[8 * h : 8 * h + 8]
            modes = []
            for c in range(10):
                modes.append(chain((factor(2, k, c), held[k]) for k in range(10)) / (base + wide(eig_ref[2, c])))
            for k in range(10):
                u[pl.ds(at + k * 16, 8), :] = chain((factor(2, k, c), modes[c]) for c in range(10))
        return 0

    lax.fori_loop(0, 10, along_z, 0)


def points_kernel(u_ref, vec_ref, l_ref, hl_ref, hh_ref, xs_ref, u, s):
    gx = lax.axis_index("gx")
    lane, _ = iotas()
    factor = load_factors(vec_ref, s)
    along_x(u_ref, u, factor, True)
    back = [s[pl.ds((10 + b) * 8 + 1, 8, stride=80), :] for b in range(10)]

    def back_y(i, _):
        for k in range(10):
            at = (i * 10 + k) * 16
            l_ref[i, k] = chain((back[b], row(u, at + b)) for b in range(10))
        for h in range(2):
            cut = [u[pl.ds(i * 160 + 128 * h + b, 8, stride=16), :] for b in range(10)]
            hl_ref[i, 8 * h : 8 * h + 8] = chain((factor(1, 0, b), cut[b]) for b in range(10))
            hh_ref[i, 8 * h : 8 * h + 8] = chain((factor(1, 9, b), cut[b]) for b in range(10))
        return 0

    lax.fori_loop(0, 10, back_y, 0)
    high_p = lane >= 64

    def outgoing(ref, k):
        return jnp.where(gx == 0, ref[9, k], roll(ref[0, k], 64))

    for k in range(5):
        xs_ref[k * 8 : k * 8 + 8] = jnp.where(high_p, outgoing(l_ref, k), roll(outgoing(l_ref, k + 5), 64))
    high_p = iotas(16)[0] >= 64
    edge_l = jnp.where(gx == 0, hl_ref[9], roll(hl_ref[0], 64))
    edge_h = jnp.where(gx == 0, hh_ref[9], roll(hh_ref[0], 64))
    xs_ref[40:56] = jnp.where(high_p, edge_l, roll(edge_h, 64))


def fold_x(value, i, opposite, received, gx, high_p):
    if i == 8:
        return value + jnp.where(high_p, jnp.where(gx == 0, received, 0.0), roll(opposite, 64))
    if i == 1:
        return value + jnp.where(high_p, roll(opposite, 64), jnp.where(gx == 1, roll(received, 64), 0.0))
    return value


def edge_rows(hl_ref, hh_ref, xr_ref, gx):
    high_p = iotas(16)[0] >= 64
    packed = xr_ref[40:56]
    low, high = [], []
    for i in range(1, 9):
        j = {1: 9, 8: 0}.get(i, i)
        low.append(fold_x(hl_ref[i], i, hl_ref[j], packed, gx, high_p))
        high.append(fold_x(hh_ref[i], i, hh_ref[j], roll(packed, 64), gx, high_p))
    return low, high


def yfold_send_kernel(hl_ref, hh_ref, xr_ref, ya_ref, yb_ref):
    gx = lax.axis_index("gx")
    even_y = lax.rem(lax.axis_index("gy"), 2) == 0
    low_q = (iotas(16)[0] & 32) == 0
    low, high = edge_rows(hl_ref, hh_ref, xr_ref, gx)
    for i in range(4):
        down = jnp.where(low_q, low[i], roll(low[i + 4], 32))
        up = jnp.where(low_q, roll(high[i + 4], 96), high[i])
        ya_ref[i * 16 : i * 16 + 16] = jnp.where(even_y, up, down)
        yb_ref[i * 16 : i * 16 + 16] = jnp.where(even_y, down, up)


def fold_rows(hl_ref, hh_ref, xr_ref, ya_ref, yb_ref, rows_first, rows_last, gx):
    low_q = (iotas(16)[0] & 32) == 0
    low, high = edge_rows(hl_ref, hh_ref, xr_ref, gx)
    for i in range(8):
        at = (i % 4) * 16
        above, below = sides(ya_ref[at : at + 16], yb_ref[at : at + 16], "gy")
        if i < 4:
            above, below = roll(above, 32), roll(below, 96)
        rows_last[pl.ds(i * 16, 16), :] = jnp.where(low_q, roll(low[i], 96), above)
        rows_first[pl.ds(i * 16, 16), :] = jnp.where(low_q, below, roll(high[i], 32))


def folded_xy(l_ref, xr_ref, rows_first, rows_last, i, k, gx, lane, sub):
    high_p = lane >= 64
    value = l_ref[i, k]
    if i in (1, 8):
        packed = xr_ref[(k % 5) * 8 : (k % 5) * 8 + 8]
        received = packed if k < 5 else roll(packed, 64)
        value = fold_x(value, i, l_ref[9 if i == 1 else 0, k], received, gx, high_p)
    at = (i - 1) * 16 + k
    return value + jnp.where(sub == 0, row(rows_first, at), jnp.where(sub == 7, row(rows_last, at), 0.0))


def zfold_send_kernel(l_ref, hl_ref, hh_ref, xr_ref, ya_ref, yb_ref, run_ref, za_ref, zb_ref, rows_first, rows_last):
    za_ref[8:24] = run_ref[...]
    gx = lax.axis_index("gx")
    even_z = lax.rem(lax.axis_index("gz"), 2) == 0
    lane, sub = iotas()
    slot = lane & 31
    fold_rows(hl_ref, hh_ref, xr_ref, ya_ref, yb_ref, rows_first, rows_last, gx)
    down = jnp.zeros((8, 128), F32)
    up = jnp.zeros((8, 128), F32)
    for i in range(8):
        down = jnp.where(slot == i, roll(folded_xy(l_ref, xr_ref, rows_first, rows_last, i + 1, 0, gx, lane, sub), i), down)
        up = jnp.where(slot == i, roll(folded_xy(l_ref, xr_ref, rows_first, rows_last, i + 1, 9, gx, lane, sub), i - 31), up)
    za_ref[:8] = jnp.where(even_z, up, down)
    zb_ref[...] = jnp.where(even_z, down, up)


def post_kernel(
    l_ref, hl_ref, hh_ref, xr_ref, ya_ref, yb_ref, za_ref, zb_ref, basis_ref, sep_ref, run_ref, ownsol_ref,
    out_ref, rows_first, rows_last, xt, grid,
):
    gx = lax.axis_index("gx")
    lane, sub = iotas()
    slot = lane & 31
    low_q = (lane & 32) == 0
    fold_rows(hl_ref, hh_ref, xr_ref, ya_ref, yb_ref, rows_first, rows_last, gx)
    running = run_ref[...] + za_ref[8:24]
    weighted = total(
        sep_ref[level][:, h * 128 : h * 128 + 128] * running[8 * h + level : 8 * h + level + 1, :]
        for h in range(2)
        for level in range(sep_ref.shape[0])
    )
    solution_col = ownsol_ref[:, :1] + jnp.sum(weighted, axis=1, keepdims=True)
    lane16, sub16 = iotas(16)
    spread = jnp.where(((lane16 & 31) >> 1) == sub16, jnp.broadcast_to(solution_col, (16, 128)), 0.0)
    per_element = jnp.broadcast_to(jnp.sum(spread, axis=0, keepdims=True), (8, 128))
    from_above, from_below = sides(za_ref[:8], zb_ref[...], "gz")
    for i in range(8):
        weights = basis_ref[i]
        get = functools.partial(folded_xy, l_ref, xr_ref, rows_first, rows_last, i + 1, gx=gx, lane=lane, sub=sub)
        before, after = get(0), get(9)
        for k in range(8):
            value = get(k + 1) + jnp.broadcast_to(weights[:, k : k + 1], (8, 128)) * per_element
            if k == 0:
                value = value + jnp.where(slot == 0, roll(from_below, -i), roll(after, 1))
            if k == 7:
                value = value + jnp.where(slot == 31, roll(from_above, 31 - i), roll(before, -1))
            grid[i, k] = value
    for pair in range(4):
        k0, k1 = 2 * pair, 2 * pair + 1
        pieces = []
        for i in range(8):
            c0, c1 = grid[i, k0], grid[i, k1]
            pieces.append(jnp.where(low_q, c0, roll(c1, 32)))
            pieces.append(jnp.where(low_q, roll(c0, 96), c1))
        block = jnp.concatenate(pieces, 0).T
        for p in range(2):
            for t, k in enumerate((k0, k1)):
                at = p * 64 + t * 32
                xt[p, pl.ds(k, 32, stride=8), :] = block[at : at + 32]
    out_ref[...] = jnp.concatenate([xt[0], xt[1]], 1).T


def call(kernel, outs, scratch, n_in, limit=4 << 20, far=0, semaphores=()):
    return pl.pallas_call(
        kernel,
        out_shape=[jax.ShapeDtypeStruct(shape, F32) for shape in outs],
        in_specs=[pl.BlockSpec(memory_space=pltpu.HBM)] * far + [VM] * (n_in - far),
        out_specs=[VM] * len(outs),
        scratch_shapes=[pltpu.VMEM(shape, F32) for shape in scratch] + list(semaphores),
        compiler_params=pltpu.CompilerParams(vmem_limit_bytes=limit),
    )


def far(value):
    return pltpu.with_memory_space_constraint(value, pltpu.HBM)


def swap(value, axis, distance):
    return lax.ppermute(value, axis, [(i, i ^ distance) for i in range(lax.axis_size(axis))])


def swap_odd(value, axis):
    count = lax.axis_size(axis)
    return lax.ppermute(value, axis, [(i, (i + 1 if i % 2 else i - 1) % count) for i in range(count)])


def work(residual, fdm_vectors, fdm_eigen, coarse_basis, x_interior, x_separator):
    levels, unknowns, width = x_separator.shape[3:]
    x = residual.reshape(256, 256)
    vectors = fdm_vectors.reshape(3, 10, 10, 128).transpose(1, 2, 0, 3)
    eigen = fdm_eigen.reshape(3, 10, 1, 128)
    own = x_interior.reshape(unknowns, unknowns)
    sep = x_separator.reshape(levels, unknowns, width)
    level_of = lax.broadcasted_iota(jnp.int32, (16, 128), 0) & 7

    def climb(running, axis, distance, first):
        return running + jnp.where(level_of >= first, swap(running, axis, distance), 0.0)

    core, xs, running, ownsol = call(
        pre_kernel,
        [(8, 8, 8, 128), (32, 128), (16, 128), (16, 128)],
        [(2, 128, 256), (2, 256, 128), (levels, unknowns, width), (8, 8, 8), (unknowns, unknowns)],
        4,
        far=4,
        semaphores=(pltpu.SemaphoreType.DMA((2,)), pltpu.SemaphoreType.DMA((3,))),
    )(far(x), far(sep), far(coarse_basis), far(own))
    xr = swap(xs, "gx", 1)
    running = climb(running, "gz", 2, 1)
    ends, za, zb = call(zface_kernel, [(2, 8, 8, 128), (8, 128), (8, 128)], [], 2)(core, xr)
    za, zb = swap(za, "gz", 1), swap_odd(zb, "gz")
    running = climb(running, "gy", 2, 5)
    block = (core, core.reshape(512, 128), ends, ends.reshape(128, 128), za, zb)
    ya, yb = call(yface_kernel, [(72, 128), (56, 128)], [(256, 128)], 7)(*block, running)
    ya, yb = swap(ya, "gy", 1), swap_odd(yb, "gy")
    running = running + jnp.where(level_of >= 4, ya[56:72], 0.0)
    running = climb(running, "gy", 6, 6)
    (modes,) = call(
        modes_kernel, [(1696, 128)], [(800, 128), (112, 128), (112, 128), (848, 128), (16, 128), (256, 128)], 10
    )(*block, ya, yb, vectors, eigen)
    running = climb(running, "gz", 4, 2)
    local, edge_l, edge_h, xs = call(
        points_kernel, [(10, 10, 8, 128), (10, 16, 128), (10, 16, 128), (56, 128)], [(1696, 128), (848, 128)], 2
    )(modes, vectors)
    xr = swap(xs, "gx", 1)
    running = climb(running, "gx", 1, 7)
    ya, yb = call(yfold_send_kernel, [(64, 128)] * 2, [], 3)(edge_l, edge_h, xr)
    ya, yb = swap(ya, "gy", 1), swap_odd(yb, "gy")
    running = climb(running, "gz", 8, 3)
    parts = (local, edge_l, edge_h, xr, ya, yb)
    za, zb = call(zfold_send_kernel, [(24, 128), (8, 128)], [(128, 128)] * 2, 7)(*parts, running)
    za, zb = swap(za, "gz", 1), swap_odd(zb, "gz")
    (out,) = call(
        post_kernel, [(256, 256)], [(128, 128), (128, 128), (2, 256, 128), (8, 8, 8, 128)], 12
    )(*parts, za, zb, coarse_basis, sep, running, ownsol)
    return out.reshape(residual.shape)


def solution(mesh):
    in_specs = (
        P("gx", "gy", "gz"),
        P("gx", "gy", "gz", None, None, None, None),
        P("gx", "gy", "gz", None, None, None),
        P(),
        P("gx", "gy", "gz", None, None),
        P("gx", "gy", "gz", None, None, None),
    )
    return jax.shard_map(work, mesh=mesh, in_specs=in_specs, out_specs=P("gx", "gy", "gz"), check_vma=False)
```

```python
import functools

import jax
import jax.numpy as jnp
from jax import lax
from jax.experimental import pallas as pl
from jax.experimental.pallas import tpu as pltpu
from jax.sharding import PartitionSpec as P


F32 = jnp.float32
VM = pl.BlockSpec(memory_space=pltpu.VMEM)


def iotas(rows=8):
    lane = lax.broadcasted_iota(jnp.int32, (rows, 128), 1)
    sub = lax.broadcasted_iota(jnp.int32, (rows, 128), 0)
    return lane, sub


def roll(value, shift):
    shift = shift % 128
    return value if shift == 0 else pltpu.roll(value, shift, value.ndim - 1)


def row(ref, index, rows=8):
    return jnp.broadcast_to(ref[pl.ds(index, 1), :], (rows, 128))


def total(terms):
    terms = list(terms)
    while len(terms) > 1:
        terms = [a + b for a, b in zip(terms[::2], terms[1::2])] + terms[len(terms) & ~1 :]
    return terms[0]


def chain(pairs):
    acc = None
    for a, b in pairs:
        acc = a * b if acc is None else acc + a * b
    return acc


def pre_kernel(
    x_ref, sep_ref, basis_ref, own_ref, core_ref, xs_ref, run_ref, ownsol_ref, xv, xt, sepv, basisv, ownv, xsem, sems
):
    copies = [pltpu.make_async_copy(x_ref.at[pl.ds(p * 128, 128), :], xv.at[p], xsem.at[p]) for p in range(2)]
    small = [
        pltpu.make_async_copy(a, b, sems.at[n])
        for n, (a, b) in enumerate(((basis_ref, basisv), (own_ref, ownv), (sep_ref, sepv)))
    ]
    for copy in copies + small:
        copy.start()
    gx = lax.axis_index("gx")
    lane, _ = iotas()
    low_q = (lane & 32) == 0
    high_p = lane >= 64
    for p in range(2):
        copies[p].wait()
        xt[p] = xv[p].T
    for pair in range(4):
        k0, k1 = 2 * pair, 2 * pair + 1
        pieces = [xt[p, pl.ds(k, 32, stride=8), :] for p in range(2) for k in (k0, k1)]
        block = jnp.concatenate(pieces, 0).T
        for i in range(8):
            a = block[i * 16 : i * 16 + 8]
            b = block[i * 16 + 8 : i * 16 + 16]
            core_ref[i, k0] = jnp.where(low_q, a, roll(b, 32))
            core_ref[i, k1] = jnp.where(low_q, roll(a, 96), b)

    def outgoing(k):
        return jnp.where(gx == 0, core_ref[7, k], roll(core_ref[0, k], 64))

    for k in range(4):
        xs_ref[k * 8 : k * 8 + 8] = jnp.where(high_p, outgoing(k), roll(outgoing(k + 4), 64))
    small[0].wait()
    sums = []
    for i in range(8):
        weights = basisv[i]
        sums.append(chain((core_ref[i, k], jnp.broadcast_to(weights[:, k : k + 1], (8, 128))) for k in range(8)))
    lanes = jnp.sum(total(sums), axis=0, keepdims=True)
    lane16, sub16 = iotas(16)
    spread = jnp.where(((lane16 & 31) >> 1) == sub16, jnp.broadcast_to(lanes, (16, 128)), 0.0)
    rhs = jnp.sum(spread, axis=1, keepdims=True)
    small[1].wait()
    own = ownv[...]
    coef = jnp.sum(own * rhs, axis=0, keepdims=True)
    ownsol_ref[...] = jnp.broadcast_to(jnp.sum(own * coef, axis=1, keepdims=True), (16, 128))
    small[2].wait()
    for level in range(sep_ref.shape[0]):
        part = jnp.sum(sepv[level] * rhs, axis=0, keepdims=True)
        for h in range(2):
            run_ref[8 * h + level : 8 * h + level + 1, :] = part[:, h * 128 : h * 128 + 128]


def zface_kernel(core_ref, xr_ref, ends_ref, za_ref, zb_ref):
    gx = lax.axis_index("gx")
    even = lax.rem(lax.axis_index("gz"), 2) == 0
    lane, _ = iotas()
    high_p = lane >= 64
    slot = lane & 31
    for k in range(8):
        at = (k % 4) * 8
        got = xr_ref[at : at + 8]
        if k >= 4:
            got = roll(got, 64)
        ends_ref[0, k] = jnp.where(high_p, roll(core_ref[7, k], 64), jnp.where(gx == 1, roll(got, 64), 0.0))
        ends_ref[1, k] = jnp.where(high_p, jnp.where(gx == 0, got, 0.0), roll(core_ref[0, k], 64))
    upper = jnp.zeros((8, 128), F32)
    lower = jnp.zeros((8, 128), F32)
    for i in range(10):
        upper = jnp.where(slot == i, roll(plane(core_ref, ends_ref, i, 7), i - 31), upper)
        lower = jnp.where(slot == i, roll(plane(core_ref, ends_ref, i, 0), i), lower)
    za_ref[...] = jnp.where(even, upper, lower)
    zb_ref[...] = jnp.where(even, lower, upper)


def plane(core_ref, ends_ref, i, k):
    return core_ref[i - 1, k] if 1 <= i <= 8 else ends_ref[i // 9, k]


def sides(a, b, axis):
    index = lax.axis_index(axis)
    even = lax.rem(index, 2) == 0
    above = jnp.where(index == lax.axis_size(axis) - 1, 0.0, jnp.where(even, a, b))
    below = jnp.where(index == 0, 0.0, jnp.where(even, b, a))
    return above, below


def z_halo(core_ref, ends_ref, za_ref, zb_ref, slot):
    from_above, from_below = sides(za_ref[...], zb_ref[...], "gz")
    first, last = [], []
    for i in range(10):
        first.append(jnp.where(slot == 0, roll(from_below, -i), roll(plane(core_ref, ends_ref, i, 7), 1)))
        last.append(jnp.where(slot == 31, roll(from_above, 31 - i), roll(plane(core_ref, ends_ref, i, 0), -1)))
    return first, last


def y_rows(first, last, core2_ref, ends2_ref, scr):
    for i in range(10):
        scr[pl.ds(i * 8, 8), :] = first[i]
        scr[pl.ds(128 + i * 8, 8), :] = last[i]
    low, high = [], []
    for i in range(10):
        ref, at = (core2_ref, (i - 1) * 64) if 1 <= i <= 8 else (ends2_ref, (i // 9) * 64)
        low.append(ref[pl.ds(at, 8, stride=8), :])
        high.append(ref[pl.ds(at + 7, 8, stride=8), :])
    low_ends = [scr[pl.ds(b, 16, stride=8), :] for b in (0, 128)]
    high_ends = [scr[pl.ds(b + 7, 16, stride=8), :] for b in (0, 128)]
    return low, high, low_ends, high_ends


def yface_kernel(core_ref, core2_ref, ends_ref, ends2_ref, za_ref, zb_ref, ya_ref, yb_ref, scr):
    even_y = lax.rem(lax.axis_index("gy"), 2) == 0
    lane, _ = iotas()
    low_q = (lane & 32) == 0
    first, last = z_halo(core_ref, ends_ref, za_ref, zb_ref, lane & 31)
    low, high, low_ends, high_ends = y_rows(first, last, core2_ref, ends2_ref, scr)
    for i in range(5):
        down = jnp.where(low_q, low[i], roll(low[i + 5], 32))
        up = jnp.where(low_q, roll(high[i + 5], 96), high[i])
        ya_ref[i * 8 : i * 8 + 8] = jnp.where(even_y, up, down)
        yb_ref[i * 8 : i * 8 + 8] = jnp.where(even_y, down, up)
    low_q = (iotas(16)[0] & 32) == 0
    down = jnp.where(low_q, low_ends[0], roll(low_ends[1], 32))
    up = jnp.where(low_q, roll(high_ends[1], 96), high_ends[0])
    ya_ref[40:56] = jnp.where(even_y, up, down)
    yb_ref[40:56] = jnp.where(even_y, down, up)


def load_factors(vec_ref, s):
    for a in range(10):
        for i in range(10):
            s[(i * 10 + a) * 8 : (i * 10 + a) * 8 + 3] = vec_ref[i, a].astype(F32)

    def factor(d, i, a):
        return row(s, (i * 10 + a) * 8 + d)

    return factor


def along_x(source, target, factor, transposed):
    def step(k, _):
        for h in range(2):
            at = k * 16 + 8 * h
            held = [source[pl.ds(i * 160 + at, 8), :] for i in range(10)]
            for a in range(10):
                target[pl.ds(a * 160 + at, 8), :] = chain(
                    (factor(0, a, i) if transposed else factor(0, i, a), held[i]) for i in range(10)
                )
        return 0

    lax.fori_loop(0, 10, step, 0)


def modes_kernel(
    core_ref, core2_ref, ends_ref, ends2_ref, za_ref, zb_ref, ya_ref, yb_ref, vec_ref, u, block, jl, jh, s, scr
):
    lane, _ = iotas()
    low_q = (lane & 32) == 0
    first, last = z_halo(core_ref, ends_ref, za_ref, zb_ref, lane & 31)
    low, high, low_ends, high_ends = y_rows(first, last, core2_ref, ends2_ref, scr)
    for i in range(10):
        block[pl.ds(i * 80, 8), :] = first[i]
        block[pl.ds(i * 80 + 72, 8), :] = last[i]
        for k in range(8):
            block[pl.ds(i * 80 + 8 + k * 8, 8), :] = plane(core_ref, ends_ref, i, k)
    for i in range(10):
        at = (i % 5) * 8
        above, below = sides(ya_ref[at : at + 8], yb_ref[at : at + 8], "gy")
        if i < 5:
            above, below = roll(above, 32), roll(below, 96)
        jl[pl.ds(i * 8, 8), :] = jnp.where(low_q, below, roll(high[i], 32))
        jh[pl.ds(i * 8, 8), :] = jnp.where(low_q, roll(low[i], 96), above)
    low_q16 = (iotas(16)[0] & 32) == 0
    above, below = sides(ya_ref[40:56], yb_ref[40:56], "gy")
    jl[80:96] = jnp.where(low_q16, roll(below, 96), roll(high_ends[0], 32))
    jl[96:112] = jnp.where(low_q16, below, roll(high_ends[1], 32))
    jh[80:96] = jnp.where(low_q16, roll(low_ends[0], 96), roll(above, 32))
    jh[96:112] = jnp.where(low_q16, roll(low_ends[1], 96), above)
    factor = load_factors(vec_ref, s)
    front = [[s[pl.ds((j * 10 + 8 * h) * 8 + 1, 8, stride=8), :] for j in range(10)] for h in range(2)]

    def fwd_y(i, _):
        for k in range(10):
            edge = i * 8 + k - 1 if 1 <= k <= 8 else (80 + i if k == 0 else 96 + i)
            at = (i * 10 + k) * 8
            rows = [row(jl, edge)] + [row(block, at + j) for j in range(8)] + [row(jh, edge)]
            for h in range(2):
                out = chain((front[h][j], rows[j]) for j in range(10))
                u[pl.ds((i * 10 + k) * 16 + 8 * h, 8), :] = out
        return 0

    lax.fori_loop(0, 10, fwd_y, 0)

    along_x(u, u, factor, False)


def middle_kernel(u_ref, vec_ref, eig_ref, u, s, eg):
    eg[...] = jnp.ones((16, 128), F32)
    for a in range(10):
        eg[a : a + 1] = eig_ref[1, a]
    factor = load_factors(vec_ref, s)

    def wide(value):
        return jnp.broadcast_to(value, (8, 128))

    def along_z(a, _):
        for h in range(2):
            at = a * 160 + 8 * h
            held = [u_ref[pl.ds(at + k * 16, 8), :] for k in range(10)]
            base = wide(eig_ref[0, a]) + eg[8 * h : 8 * h + 8]
            modes = []
            for c in range(10):
                modes.append(chain((factor(2, k, c), held[k]) for k in range(10)) / (base + wide(eig_ref[2, c])))
            for k in range(10):
                u[pl.ds(at + k * 16, 8), :] = chain((factor(2, k, c), modes[c]) for c in range(10))
        return 0

    lax.fori_loop(0, 10, along_z, 0)


def points_kernel(u_ref, vec_ref, l_ref, hl_ref, hh_ref, xs_ref, u, s):
    gx = lax.axis_index("gx")
    lane, _ = iotas()
    factor = load_factors(vec_ref, s)
    along_x(u_ref, u, factor, True)
    back = [s[pl.ds((10 + b) * 8 + 1, 8, stride=80), :] for b in range(10)]

    def back_y(i, _):
        for k in range(10):
            at = (i * 10 + k) * 16
            l_ref[i, k] = chain((back[b], row(u, at + b)) for b in range(10))
        for h in range(2):
            cut = [u[pl.ds(i * 160 + 128 * h + b, 8, stride=16), :] for b in range(10)]
            hl_ref[i, 8 * h : 8 * h + 8] = chain((factor(1, 0, b), cut[b]) for b in range(10))
            hh_ref[i, 8 * h : 8 * h + 8] = chain((factor(1, 9, b), cut[b]) for b in range(10))
        return 0

    lax.fori_loop(0, 10, back_y, 0)
    high_p = lane >= 64

    def outgoing(ref, k):
        return jnp.where(gx == 0, ref[9, k], roll(ref[0, k], 64))

    for k in range(5):
        xs_ref[k * 8 : k * 8 + 8] = jnp.where(high_p, outgoing(l_ref, k), roll(outgoing(l_ref, k + 5), 64))
    high_p = iotas(16)[0] >= 64
    edge_l = jnp.where(gx == 0, hl_ref[9], roll(hl_ref[0], 64))
    edge_h = jnp.where(gx == 0, hh_ref[9], roll(hh_ref[0], 64))
    xs_ref[40:56] = jnp.where(high_p, edge_l, roll(edge_h, 64))


def fold_x(value, i, opposite, received, gx, high_p):
    if i == 8:
        return value + jnp.where(high_p, jnp.where(gx == 0, received, 0.0), roll(opposite, 64))
    if i == 1:
        return value + jnp.where(high_p, roll(opposite, 64), jnp.where(gx == 1, roll(received, 64), 0.0))
    return value


def edge_rows(hl_ref, hh_ref, xr_ref, gx):
    high_p = iotas(16)[0] >= 64
    packed = xr_ref[40:56]
    low, high = [], []
    for i in range(1, 9):
        j = {1: 9, 8: 0}.get(i, i)
        low.append(fold_x(hl_ref[i], i, hl_ref[j], packed, gx, high_p))
        high.append(fold_x(hh_ref[i], i, hh_ref[j], roll(packed, 64), gx, high_p))
    return low, high


def yfold_send_kernel(hl_ref, hh_ref, xr_ref, run_ref, ya_ref, yb_ref):
    ya_ref[64:80] = run_ref[...]
    gx = lax.axis_index("gx")
    even_y = lax.rem(lax.axis_index("gy"), 2) == 0
    low_q = (iotas(16)[0] & 32) == 0
    low, high = edge_rows(hl_ref, hh_ref, xr_ref, gx)
    for i in range(4):
        down = jnp.where(low_q, low[i], roll(low[i + 4], 32))
        up = jnp.where(low_q, roll(high[i + 4], 96), high[i])
        ya_ref[i * 16 : i * 16 + 16] = jnp.where(even_y, up, down)
        yb_ref[i * 16 : i * 16 + 16] = jnp.where(even_y, down, up)


def fold_rows(hl_ref, hh_ref, xr_ref, ya_ref, yb_ref, rows_first, rows_last, gx):
    low_q = (iotas(16)[0] & 32) == 0
    low, high = edge_rows(hl_ref, hh_ref, xr_ref, gx)
    for i in range(8):
        at = (i % 4) * 16
        above, below = sides(ya_ref[at : at + 16], yb_ref[at : at + 16], "gy")
        if i < 4:
            above, below = roll(above, 32), roll(below, 96)
        rows_last[pl.ds(i * 16, 16), :] = jnp.where(low_q, roll(low[i], 96), above)
        rows_first[pl.ds(i * 16, 16), :] = jnp.where(low_q, below, roll(high[i], 32))


def folded_xy(l_ref, xr_ref, rows_first, rows_last, i, k, gx, lane, sub):
    high_p = lane >= 64
    value = l_ref[i, k]
    if i in (1, 8):
        packed = xr_ref[(k % 5) * 8 : (k % 5) * 8 + 8]
        received = packed if k < 5 else roll(packed, 64)
        value = fold_x(value, i, l_ref[9 if i == 1 else 0, k], received, gx, high_p)
    at = (i - 1) * 16 + k
    return value + jnp.where(sub == 0, row(rows_first, at), jnp.where(sub == 7, row(rows_last, at), 0.0))


def zfold_send_kernel(l_ref, hl_ref, hh_ref, xr_ref, ya_ref, yb_ref, run_ref, za_ref, zb_ref, sum_ref, rows_first, rows_last):
    level = iotas(16)[1] & 7
    sum_ref[...] = run_ref[...] + jnp.where(level >= 4, ya_ref[64:80], 0.0)
    za_ref[8:24] = sum_ref[...]
    gx = lax.axis_index("gx")
    even_z = lax.rem(lax.axis_index("gz"), 2) == 0
    lane, sub = iotas()
    slot = lane & 31
    fold_rows(hl_ref, hh_ref, xr_ref, ya_ref, yb_ref, rows_first, rows_last, gx)
    down = jnp.zeros((8, 128), F32)
    up = jnp.zeros((8, 128), F32)
    for i in range(8):
        down = jnp.where(slot == i, roll(folded_xy(l_ref, xr_ref, rows_first, rows_last, i + 1, 0, gx, lane, sub), i), down)
        up = jnp.where(slot == i, roll(folded_xy(l_ref, xr_ref, rows_first, rows_last, i + 1, 9, gx, lane, sub), i - 31), up)
    za_ref[:8] = jnp.where(even_z, up, down)
    zb_ref[...] = jnp.where(even_z, down, up)


def post_kernel(
    l_ref, hl_ref, hh_ref, xr_ref, ya_ref, yb_ref, za_ref, zb_ref, basis_ref, sep_ref, run_ref, ownsol_ref,
    out_ref, rows_first, rows_last, xt, grid,
):
    gx = lax.axis_index("gx")
    lane, sub = iotas()
    slot = lane & 31
    low_q = (lane & 32) == 0
    fold_rows(hl_ref, hh_ref, xr_ref, ya_ref, yb_ref, rows_first, rows_last, gx)
    running = run_ref[...] + za_ref[8:24]
    weighted = total(
        sep_ref[level][:, h * 128 : h * 128 + 128] * running[8 * h + level : 8 * h + level + 1, :]
        for h in range(2)
        for level in range(sep_ref.shape[0])
    )
    solution_col = ownsol_ref[:, :1] + jnp.sum(weighted, axis=1, keepdims=True)
    lane16, sub16 = iotas(16)
    spread = jnp.where(((lane16 & 31) >> 1) == sub16, jnp.broadcast_to(solution_col, (16, 128)), 0.0)
    per_element = jnp.broadcast_to(jnp.sum(spread, axis=0, keepdims=True), (8, 128))
    from_above, from_below = sides(za_ref[:8], zb_ref[...], "gz")
    for i in range(8):
        weights = basis_ref[i]
        get = functools.partial(folded_xy, l_ref, xr_ref, rows_first, rows_last, i + 1, gx=gx, lane=lane, sub=sub)
        before, after = get(0), get(9)
        for k in range(8):
            value = get(k + 1) + jnp.broadcast_to(weights[:, k : k + 1], (8, 128)) * per_element
            if k == 0:
                value = value + jnp.where(slot == 0, roll(from_below, -i), roll(after, 1))
            if k == 7:
                value = value + jnp.where(slot == 31, roll(from_above, 31 - i), roll(before, -1))
            grid[i, k] = value
    for pair in range(4):
        k0, k1 = 2 * pair, 2 * pair + 1
        pieces = []
        for i in range(8):
            c0, c1 = grid[i, k0], grid[i, k1]
            pieces.append(jnp.where(low_q, c0, roll(c1, 32)))
            pieces.append(jnp.where(low_q, roll(c0, 96), c1))
        block = jnp.concatenate(pieces, 0).T
        for p in range(2):
            for t, k in enumerate((k0, k1)):
                at = p * 64 + t * 32
                xt[p, pl.ds(k, 32, stride=8), :] = block[at : at + 32]
    out_ref[...] = jnp.concatenate([xt[0], xt[1]], 1).T


def call(kernel, outs, scratch, n_in, limit=4 << 20, far=0, semaphores=()):
    return pl.pallas_call(
        kernel,
        out_shape=[jax.ShapeDtypeStruct(shape, F32) for shape in outs],
        in_specs=[pl.BlockSpec(memory_space=pltpu.HBM)] * far + [VM] * (n_in - far),
        out_specs=[VM] * len(outs),
        scratch_shapes=[pltpu.VMEM(shape, F32) for shape in scratch] + list(semaphores),
        compiler_params=pltpu.CompilerParams(vmem_limit_bytes=limit),
    )


def far(value):
    return pltpu.with_memory_space_constraint(value, pltpu.HBM)


def swap(value, axis, distance):
    return lax.ppermute(value, axis, [(i, i ^ distance) for i in range(lax.axis_size(axis))])


def swap_odd(value, axis):
    count = lax.axis_size(axis)
    return lax.ppermute(value, axis, [(i, (i + 1 if i % 2 else i - 1) % count) for i in range(count)])


def work(residual, fdm_vectors, fdm_eigen, coarse_basis, x_interior, x_separator):
    levels, unknowns, width = x_separator.shape[3:]
    x = residual.reshape(256, 256)
    vectors = fdm_vectors.reshape(3, 10, 10, 128).transpose(1, 2, 0, 3)
    eigen = fdm_eigen.reshape(3, 10, 1, 128)
    own = x_interior.reshape(unknowns, unknowns)
    sep = x_separator.reshape(levels, unknowns, width)
    level_of = lax.broadcasted_iota(jnp.int32, (16, 128), 0) & 7

    def climb(running, axis, distance, first):
        return running + jnp.where(level_of >= first, swap(running, axis, distance), 0.0)

    core, xs, running, ownsol = call(
        pre_kernel,
        [(8, 8, 8, 128), (32, 128), (16, 128), (16, 128)],
        [(2, 128, 256), (2, 256, 128), (levels, unknowns, width), (8, 8, 8), (unknowns, unknowns)],
        4,
        far=4,
        semaphores=(pltpu.SemaphoreType.DMA((2,)), pltpu.SemaphoreType.DMA((3,))),
    )(far(x), far(sep), far(coarse_basis), far(own))
    xr = swap(xs, "gx", 1)
    running = climb(running, "gx", 1, 7)
    ends, za, zb = call(zface_kernel, [(2, 8, 8, 128), (8, 128), (8, 128)], [], 2)(core, xr)
    running = climb(running, "gy", 2, 5)
    za, zb = swap(za, "gz", 1), swap_odd(zb, "gz")
    running = climb(running, "gy", 6, 6)
    block = (core, core.reshape(512, 128), ends, ends.reshape(128, 128), za, zb)
    ya, yb = call(yface_kernel, [(56, 128), (56, 128)], [(256, 128)], 6)(*block)
    ya, yb = swap(ya, "gy", 1), swap_odd(yb, "gy")
    running = climb(running, "gz", 4, 2)
    (modes,) = call(
        modes_kernel, [(1696, 128)], [(800, 128), (112, 128), (112, 128), (848, 128), (256, 128)], 9
    )(*block, ya, yb, vectors)
    running = climb(running, "gz", 12, 3)
    (modes,) = call(middle_kernel, [(1696, 128)], [(848, 128), (16, 128)], 3)(modes, vectors, eigen)
    running = climb(running, "gz", 3, 1)
    local, edge_l, edge_h, xs = call(
        points_kernel, [(10, 10, 8, 128), (10, 16, 128), (10, 16, 128), (56, 128)], [(1696, 128), (848, 128)], 2
    )(modes, vectors)
    xr = swap(xs, "gx", 1)
    ya, yb = call(yfold_send_kernel, [(80, 128), (64, 128)], [], 4)(edge_l, edge_h, xr, running)
    ya, yb = swap(ya, "gy", 1), swap_odd(yb, "gy")
    parts = (local, edge_l, edge_h, xr, ya, yb)
    za, zb, running = call(zfold_send_kernel, [(24, 128), (8, 128), (16, 128)], [(128, 128)] * 2, 7)(*parts, running)
    za, zb = swap(za, "gz", 1), swap_odd(zb, "gz")
    (out,) = call(
        post_kernel, [(256, 256)], [(128, 128), (128, 128), (2, 256, 128), (8, 8, 8, 128)], 12
    )(*parts, za, zb, coarse_basis, sep, running, ownsol)
    return out.reshape(residual.shape)


def solution(mesh):
    in_specs = (
        P("gx", "gy", "gz"),
        P("gx", "gy", "gz", None, None, None, None),
        P("gx", "gy", "gz", None, None, None),
        P(),
        P("gx", "gy", "gz", None, None),
        P("gx", "gy", "gz", None, None, None),
    )
    return jax.shard_map(work, mesh=mesh, in_specs=in_specs, out_specs=P("gx", "gy", "gz"), check_vma=False)
```

```python
import functools

import jax
import jax.numpy as jnp
from jax import lax
from jax.experimental import pallas as pl
from jax.experimental.pallas import tpu as pltpu
from jax.sharding import PartitionSpec as P


F32 = jnp.float32
VM = pl.BlockSpec(memory_space=pltpu.VMEM)


def iotas(rows=8):
    lane = lax.broadcasted_iota(jnp.int32, (rows, 128), 1)
    sub = lax.broadcasted_iota(jnp.int32, (rows, 128), 0)
    return lane, sub


def roll(value, shift):
    shift = shift % 128
    return value if shift == 0 else pltpu.roll(value, shift, value.ndim - 1)


def row(ref, index, rows=8):
    return jnp.broadcast_to(ref[pl.ds(index, 1), :], (rows, 128))


def total(terms):
    terms = list(terms)
    while len(terms) > 1:
        terms = [a + b for a, b in zip(terms[::2], terms[1::2])] + terms[len(terms) & ~1 :]
    return terms[0]


def chain(pairs):
    acc = None
    for a, b in pairs:
        acc = a * b if acc is None else acc + a * b
    return acc


def pre_kernel(
    x_ref, sep_ref, basis_ref, own_ref, core_ref, xs_ref, run_ref, ownsol_ref, xv, xt, sepv, basisv, ownv, xsem, sems
):
    copies = [pltpu.make_async_copy(x_ref.at[pl.ds(p * 128, 128), :], xv.at[p], xsem.at[p]) for p in range(2)]
    small = [
        pltpu.make_async_copy(a, b, sems.at[n])
        for n, (a, b) in enumerate(((basis_ref, basisv), (own_ref, ownv), (sep_ref, sepv)))
    ]
    for copy in copies + small:
        copy.start()
    gx = lax.axis_index("gx")
    lane, _ = iotas()
    low_q = (lane & 32) == 0
    high_p = lane >= 64
    for p in range(2):
        copies[p].wait()
        xt[p] = xv[p].T
    for pair in range(4):
        k0, k1 = 2 * pair, 2 * pair + 1
        pieces = [xt[p, pl.ds(k, 32, stride=8), :] for p in range(2) for k in (k0, k1)]
        block = jnp.concatenate(pieces, 0).T
        for i in range(8):
            a = block[i * 16 : i * 16 + 8]
            b = block[i * 16 + 8 : i * 16 + 16]
            core_ref[i, k0] = jnp.where(low_q, a, roll(b, 32))
            core_ref[i, k1] = jnp.where(low_q, roll(a, 96), b)

    def outgoing(k):
        return jnp.where(gx == 0, core_ref[7, k], roll(core_ref[0, k], 64))

    for k in range(4):
        xs_ref[k * 8 : k * 8 + 8] = jnp.where(high_p, outgoing(k), roll(outgoing(k + 4), 64))
    small[0].wait()
    sums = []
    for i in range(8):
        weights = basisv[i]
        sums.append(chain((core_ref[i, k], jnp.broadcast_to(weights[:, k : k + 1], (8, 128))) for k in range(8)))
    lanes = jnp.sum(total(sums), axis=0, keepdims=True)
    lane16, sub16 = iotas(16)
    spread = jnp.where(((lane16 & 31) >> 1) == sub16, jnp.broadcast_to(lanes, (16, 128)), 0.0)
    rhs = jnp.sum(spread, axis=1, keepdims=True)
    small[1].wait()
    own = ownv[...]
    coef = jnp.sum(own * rhs, axis=0, keepdims=True)
    ownsol_ref[...] = jnp.broadcast_to(jnp.sum(own * coef, axis=1, keepdims=True), (16, 128))
    small[2].wait()
    for level in range(sep_ref.shape[0]):
        part = jnp.sum(sepv[level] * rhs, axis=0, keepdims=True)
        for h in range(2):
            run_ref[8 * h + level : 8 * h + level + 1, :] = part[:, h * 128 : h * 128 + 128]


def zface_kernel(core_ref, xr_ref, ends_ref, za_ref, zb_ref):
    gx = lax.axis_index("gx")
    even = lax.rem(lax.axis_index("gz"), 2) == 0
    lane, _ = iotas()
    high_p = lane >= 64
    slot = lane & 31
    for k in range(8):
        at = (k % 4) * 8
        got = xr_ref[at : at + 8]
        if k >= 4:
            got = roll(got, 64)
        ends_ref[0, k] = jnp.where(high_p, roll(core_ref[7, k], 64), jnp.where(gx == 1, roll(got, 64), 0.0))
        ends_ref[1, k] = jnp.where(high_p, jnp.where(gx == 0, got, 0.0), roll(core_ref[0, k], 64))
    upper = jnp.zeros((8, 128), F32)
    lower = jnp.zeros((8, 128), F32)
    for i in range(10):
        upper = jnp.where(slot == i, roll(plane(core_ref, ends_ref, i, 7), i - 31), upper)
        lower = jnp.where(slot == i, roll(plane(core_ref, ends_ref, i, 0), i), lower)
    za_ref[...] = jnp.where(even, upper, lower)
    zb_ref[...] = jnp.where(even, lower, upper)


def plane(core_ref, ends_ref, i, k):
    return core_ref[i - 1, k] if 1 <= i <= 8 else ends_ref[i // 9, k]


def sides(a, b, axis):
    index = lax.axis_index(axis)
    even = lax.rem(index, 2) == 0
    above = jnp.where(index == lax.axis_size(axis) - 1, 0.0, jnp.where(even, a, b))
    below = jnp.where(index == 0, 0.0, jnp.where(even, b, a))
    return above, below


def z_halo(core_ref, ends_ref, za_ref, zb_ref, slot):
    from_above, from_below = sides(za_ref[...], zb_ref[...], "gz")
    first, last = [], []
    for i in range(10):
        first.append(jnp.where(slot == 0, roll(from_below, -i), roll(plane(core_ref, ends_ref, i, 7), 1)))
        last.append(jnp.where(slot == 31, roll(from_above, 31 - i), roll(plane(core_ref, ends_ref, i, 0), -1)))
    return first, last


def y_rows(first, last, core2_ref, ends2_ref, scr):
    for i in range(10):
        scr[pl.ds(i * 8, 8), :] = first[i]
        scr[pl.ds(128 + i * 8, 8), :] = last[i]
    low, high = [], []
    for i in range(10):
        ref, at = (core2_ref, (i - 1) * 64) if 1 <= i <= 8 else (ends2_ref, (i // 9) * 64)
        low.append(ref[pl.ds(at, 8, stride=8), :])
        high.append(ref[pl.ds(at + 7, 8, stride=8), :])
    low_ends = [scr[pl.ds(b, 16, stride=8), :] for b in (0, 128)]
    high_ends = [scr[pl.ds(b + 7, 16, stride=8), :] for b in (0, 128)]
    return low, high, low_ends, high_ends


def yface_kernel(core_ref, core2_ref, ends_ref, ends2_ref, za_ref, zb_ref, run_ref, ya_ref, yb_ref, scr):
    ya_ref[56:72] = run_ref[...]
    even_y = lax.rem(lax.axis_index("gy"), 2) == 0
    lane, _ = iotas()
    low_q = (lane & 32) == 0
    first, last = z_halo(core_ref, ends_ref, za_ref, zb_ref, lane & 31)
    low, high, low_ends, high_ends = y_rows(first, last, core2_ref, ends2_ref, scr)
    for i in range(5):
        down = jnp.where(low_q, low[i], roll(low[i + 5], 32))
        up = jnp.where(low_q, roll(high[i + 5], 96), high[i])
        ya_ref[i * 8 : i * 8 + 8] = jnp.where(even_y, up, down)
        yb_ref[i * 8 : i * 8 + 8] = jnp.where(even_y, down, up)
    low_q = (iotas(16)[0] & 32) == 0
    down = jnp.where(low_q, low_ends[0], roll(low_ends[1], 32))
    up = jnp.where(low_q, roll(high_ends[1], 96), high_ends[0])
    ya_ref[40:56] = jnp.where(even_y, up, down)
    yb_ref[40:56] = jnp.where(even_y, down, up)


def load_factors(vec_ref, s):
    for a in range(10):
        for i in range(10):
            s[(i * 10 + a) * 8 : (i * 10 + a) * 8 + 3] = vec_ref[i, a].astype(F32)

    def factor(d, i, a):
        return row(s, (i * 10 + a) * 8 + d)

    return factor


def along_x(source, target, factor, transposed):
    def step(k, _):
        for h in range(2):
            at = k * 16 + 8 * h
            held = [source[pl.ds(i * 160 + at, 8), :] for i in range(10)]
            for a in range(10):
                target[pl.ds(a * 160 + at, 8), :] = chain(
                    (factor(0, a, i) if transposed else factor(0, i, a), held[i]) for i in range(10)
                )
        return 0

    lax.fori_loop(0, 10, step, 0)


def modes_kernel(
    core_ref, core2_ref, ends_ref, ends2_ref, za_ref, zb_ref, ya_ref, yb_ref, vec_ref, u, block, jl, jh, s, scr
):
    lane, _ = iotas()
    low_q = (lane & 32) == 0
    first, last = z_halo(core_ref, ends_ref, za_ref, zb_ref, lane & 31)
    low, high, low_ends, high_ends = y_rows(first, last, core2_ref, ends2_ref, scr)
    for i in range(10):
        block[pl.ds(i * 80, 8), :] = first[i]
        block[pl.ds(i * 80 + 72, 8), :] = last[i]
        for k in range(8):
            block[pl.ds(i * 80 + 8 + k * 8, 8), :] = plane(core_ref, ends_ref, i, k)
    for i in range(10):
        at = (i % 5) * 8
        above, below = sides(ya_ref[at : at + 8], yb_ref[at : at + 8], "gy")
        if i < 5:
            above, below = roll(above, 32), roll(below, 96)
        jl[pl.ds(i * 8, 8), :] = jnp.where(low_q, below, roll(high[i], 32))
        jh[pl.ds(i * 8, 8), :] = jnp.where(low_q, roll(low[i], 96), above)
    low_q16 = (iotas(16)[0] & 32) == 0
    above, below = sides(ya_ref[40:56], yb_ref[40:56], "gy")
    jl[80:96] = jnp.where(low_q16, roll(below, 96), roll(high_ends[0], 32))
    jl[96:112] = jnp.where(low_q16, below, roll(high_ends[1], 32))
    jh[80:96] = jnp.where(low_q16, roll(low_ends[0], 96), roll(above, 32))
    jh[96:112] = jnp.where(low_q16, roll(low_ends[1], 96), above)
    factor = load_factors(vec_ref, s)
    front = [[s[pl.ds((j * 10 + 8 * h) * 8 + 1, 8, stride=8), :] for j in range(10)] for h in range(2)]

    def fwd_y(i, _):
        for k in range(10):
            edge = i * 8 + k - 1 if 1 <= k <= 8 else (80 + i if k == 0 else 96 + i)
            at = (i * 10 + k) * 8
            rows = [row(jl, edge)] + [row(block, at + j) for j in range(8)] + [row(jh, edge)]
            for h in range(2):
                out = chain((front[h][j], rows[j]) for j in range(10))
                u[pl.ds((i * 10 + k) * 16 + 8 * h, 8), :] = out
        return 0

    lax.fori_loop(0, 10, fwd_y, 0)

    along_x(u, u, factor, False)


def middle_kernel(u_ref, vec_ref, eig_ref, u, s, eg):
    eg[...] = jnp.ones((16, 128), F32)
    for a in range(10):
        eg[a : a + 1] = eig_ref[1, a]
    factor = load_factors(vec_ref, s)

    def wide(value):
        return jnp.broadcast_to(value, (8, 128))

    def along_z(a, _):
        for h in range(2):
            at = a * 160 + 8 * h
            held = [u_ref[pl.ds(at + k * 16, 8), :] for k in range(10)]
            base = wide(eig_ref[0, a]) + eg[8 * h : 8 * h + 8]
            modes = []
            for c in range(10):
                modes.append(chain((factor(2, k, c), held[k]) for k in range(10)) / (base + wide(eig_ref[2, c])))
            for k in range(10):
                u[pl.ds(at + k * 16, 8), :] = chain((factor(2, k, c), modes[c]) for c in range(10))
        return 0

    lax.fori_loop(0, 10, along_z, 0)


def points_kernel(u_ref, vec_ref, l_ref, hl_ref, hh_ref, xs_ref, u, s):
    gx = lax.axis_index("gx")
    lane, _ = iotas()
    factor = load_factors(vec_ref, s)
    along_x(u_ref, u, factor, True)
    back = [s[pl.ds((10 + b) * 8 + 1, 8, stride=80), :] for b in range(10)]

    def back_y(i, _):
        for k in range(10):
            at = (i * 10 + k) * 16
            l_ref[i, k] = chain((back[b], row(u, at + b)) for b in range(10))
        for h in range(2):
            cut = [u[pl.ds(i * 160 + 128 * h + b, 8, stride=16), :] for b in range(10)]
            hl_ref[i, 8 * h : 8 * h + 8] = chain((factor(1, 0, b), cut[b]) for b in range(10))
            hh_ref[i, 8 * h : 8 * h + 8] = chain((factor(1, 9, b), cut[b]) for b in range(10))
        return 0

    lax.fori_loop(0, 10, back_y, 0)
    high_p = lane >= 64

    def outgoing(ref, k):
        return jnp.where(gx == 0, ref[9, k], roll(ref[0, k], 64))

    for k in range(5):
        xs_ref[k * 8 : k * 8 + 8] = jnp.where(high_p, outgoing(l_ref, k), roll(outgoing(l_ref, k + 5), 64))
    high_p = iotas(16)[0] >= 64
    edge_l = jnp.where(gx == 0, hl_ref[9], roll(hl_ref[0], 64))
    edge_h = jnp.where(gx == 0, hh_ref[9], roll(hh_ref[0], 64))
    xs_ref[40:56] = jnp.where(high_p, edge_l, roll(edge_h, 64))


def fold_x(value, i, opposite, received, gx, high_p):
    if i == 8:
        return value + jnp.where(high_p, jnp.where(gx == 0, received, 0.0), roll(opposite, 64))
    if i == 1:
        return value + jnp.where(high_p, roll(opposite, 64), jnp.where(gx == 1, roll(received, 64), 0.0))
    return value


def edge_rows(hl_ref, hh_ref, xr_ref, gx):
    high_p = iotas(16)[0] >= 64
    packed = xr_ref[40:56]
    low, high = [], []
    for i in range(1, 9):
        j = {1: 9, 8: 0}.get(i, i)
        low.append(fold_x(hl_ref[i], i, hl_ref[j], packed, gx, high_p))
        high.append(fold_x(hh_ref[i], i, hh_ref[j], roll(packed, 64), gx, high_p))
    return low, high


def yfold_send_kernel(hl_ref, hh_ref, xr_ref, ya_ref, yb_ref):
    gx = lax.axis_index("gx")
    even_y = lax.rem(lax.axis_index("gy"), 2) == 0
    low_q = (iotas(16)[0] & 32) == 0
    low, high = edge_rows(hl_ref, hh_ref, xr_ref, gx)
    for i in range(4):
        down = jnp.where(low_q, low[i], roll(low[i + 4], 32))
        up = jnp.where(low_q, roll(high[i + 4], 96), high[i])
        ya_ref[i * 16 : i * 16 + 16] = jnp.where(even_y, up, down)
        yb_ref[i * 16 : i * 16 + 16] = jnp.where(even_y, down, up)


def fold_rows(hl_ref, hh_ref, xr_ref, ya_ref, yb_ref, rows_first, rows_last, gx):
    low_q = (iotas(16)[0] & 32) == 0
    low, high = edge_rows(hl_ref, hh_ref, xr_ref, gx)
    for i in range(8):
        at = (i % 4) * 16
        above, below = sides(ya_ref[at : at + 16], yb_ref[at : at + 16], "gy")
        if i < 4:
            above, below = roll(above, 32), roll(below, 96)
        rows_last[pl.ds(i * 16, 16), :] = jnp.where(low_q, roll(low[i], 96), above)
        rows_first[pl.ds(i * 16, 16), :] = jnp.where(low_q, below, roll(high[i], 32))


def folded_xy(l_ref, xr_ref, rows_first, rows_last, i, k, gx, lane, sub):
    high_p = lane >= 64
    value = l_ref[i, k]
    if i in (1, 8):
        packed = xr_ref[(k % 5) * 8 : (k % 5) * 8 + 8]
        received = packed if k < 5 else roll(packed, 64)
        value = fold_x(value, i, l_ref[9 if i == 1 else 0, k], received, gx, high_p)
    at = (i - 1) * 16 + k
    return value + jnp.where(sub == 0, row(rows_first, at), jnp.where(sub == 7, row(rows_last, at), 0.0))


def zfold_send_kernel(l_ref, hl_ref, hh_ref, xr_ref, ya_ref, yb_ref, run_ref, za_ref, zb_ref, rows_first, rows_last):
    za_ref[8:24] = run_ref[...]
    gx = lax.axis_index("gx")
    even_z = lax.rem(lax.axis_index("gz"), 2) == 0
    lane, sub = iotas()
    slot = lane & 31
    fold_rows(hl_ref, hh_ref, xr_ref, ya_ref, yb_ref, rows_first, rows_last, gx)
    down = jnp.zeros((8, 128), F32)
    up = jnp.zeros((8, 128), F32)
    for i in range(8):
        down = jnp.where(slot == i, roll(folded_xy(l_ref, xr_ref, rows_first, rows_last, i + 1, 0, gx, lane, sub), i), down)
        up = jnp.where(slot == i, roll(folded_xy(l_ref, xr_ref, rows_first, rows_last, i + 1, 9, gx, lane, sub), i - 31), up)
    za_ref[:8] = jnp.where(even_z, up, down)
    zb_ref[...] = jnp.where(even_z, down, up)


def post_kernel(
    l_ref, hl_ref, hh_ref, xr_ref, ya_ref, yb_ref, za_ref, zb_ref, basis_ref, sep_ref, run_ref, ownsol_ref,
    out_ref, rows_first, rows_last, xt, grid,
):
    gx = lax.axis_index("gx")
    lane, sub = iotas()
    slot = lane & 31
    low_q = (lane & 32) == 0
    fold_rows(hl_ref, hh_ref, xr_ref, ya_ref, yb_ref, rows_first, rows_last, gx)
    running = run_ref[...] + za_ref[8:24]
    weighted = total(
        sep_ref[level][:, h * 128 : h * 128 + 128] * running[8 * h + level : 8 * h + level + 1, :]
        for h in range(2)
        for level in range(sep_ref.shape[0])
    )
    solution_col = ownsol_ref[:, :1] + jnp.sum(weighted, axis=1, keepdims=True)
    lane16, sub16 = iotas(16)
    spread = jnp.where(((lane16 & 31) >> 1) == sub16, jnp.broadcast_to(solution_col, (16, 128)), 0.0)
    per_element = jnp.broadcast_to(jnp.sum(spread, axis=0, keepdims=True), (8, 128))
    from_above, from_below = sides(za_ref[:8], zb_ref[...], "gz")
    for i in range(8):
        weights = basis_ref[i]
        get = functools.partial(folded_xy, l_ref, xr_ref, rows_first, rows_last, i + 1, gx=gx, lane=lane, sub=sub)
        before, after = get(0), get(9)
        for k in range(8):
            value = get(k + 1) + jnp.broadcast_to(weights[:, k : k + 1], (8, 128)) * per_element
            if k == 0:
                value = value + jnp.where(slot == 0, roll(from_below, -i), roll(after, 1))
            if k == 7:
                value = value + jnp.where(slot == 31, roll(from_above, 31 - i), roll(before, -1))
            grid[i, k] = value
    for pair in range(4):
        k0, k1 = 2 * pair, 2 * pair + 1
        pieces = []
        for i in range(8):
            c0, c1 = grid[i, k0], grid[i, k1]
            pieces.append(jnp.where(low_q, c0, roll(c1, 32)))
            pieces.append(jnp.where(low_q, roll(c0, 96), c1))
        block = jnp.concatenate(pieces, 0).T
        for p in range(2):
            for t, k in enumerate((k0, k1)):
                at = p * 64 + t * 32
                xt[p, pl.ds(k, 32, stride=8), :] = block[at : at + 32]
    out_ref[...] = jnp.concatenate([xt[0], xt[1]], 1).T


def call(kernel, outs, scratch, n_in, limit=4 << 20, far=0, semaphores=()):
    return pl.pallas_call(
        kernel,
        out_shape=[jax.ShapeDtypeStruct(shape, F32) for shape in outs],
        in_specs=[pl.BlockSpec(memory_space=pltpu.HBM)] * far + [VM] * (n_in - far),
        out_specs=[VM] * len(outs),
        scratch_shapes=[pltpu.VMEM(shape, F32) for shape in scratch] + list(semaphores),
        compiler_params=pltpu.CompilerParams(vmem_limit_bytes=limit),
    )


def far(value):
    return pltpu.with_memory_space_constraint(value, pltpu.HBM)


def swap(value, axis, distance):
    return lax.ppermute(value, axis, [(i, i ^ distance) for i in range(lax.axis_size(axis))])


def swap_odd(value, axis):
    count = lax.axis_size(axis)
    return lax.ppermute(value, axis, [(i, (i + 1 if i % 2 else i - 1) % count) for i in range(count)])


def work(residual, fdm_vectors, fdm_eigen, coarse_basis, x_interior, x_separator):
    levels, unknowns, width = x_separator.shape[3:]
    x = residual.reshape(256, 256)
    vectors = fdm_vectors.reshape(3, 10, 10, 128).transpose(1, 2, 0, 3)
    eigen = fdm_eigen.reshape(3, 10, 1, 128)
    own = x_interior.reshape(unknowns, unknowns)
    sep = x_separator.reshape(levels, unknowns, width)
    level_of = lax.broadcasted_iota(jnp.int32, (16, 128), 0) & 7

    def climb(running, axis, distance, first):
        return running + jnp.where(level_of >= first, swap(running, axis, distance), 0.0)

    core, xs, running, ownsol = call(
        pre_kernel,
        [(8, 8, 8, 128), (32, 128), (16, 128), (16, 128)],
        [(2, 128, 256), (2, 256, 128), (levels, unknowns, width), (8, 8, 8), (unknowns, unknowns)],
        4,
        far=4,
        semaphores=(pltpu.SemaphoreType.DMA((2,)), pltpu.SemaphoreType.DMA((3,))),
    )(far(x), far(sep), far(coarse_basis), far(own))
    xr = swap(xs, "gx", 1)
    running = climb(running, "gx", 1, 7)
    ends, za, zb = call(zface_kernel, [(2, 8, 8, 128), (8, 128), (8, 128)], [], 2)(core, xr)
    running = climb(running, "gy", 2, 5)
    za, zb = swap(za, "gz", 1), swap_odd(zb, "gz")
    running = climb(running, "gz", 4, 2)
    block = (core, core.reshape(512, 128), ends, ends.reshape(128, 128), za, zb)
    ya, yb = call(yface_kernel, [(72, 128), (56, 128)], [(256, 128)], 7)(*block, running)
    ya, yb = swap(ya, "gy", 1), swap_odd(yb, "gy")
    running = running + jnp.where(level_of >= 4, ya[56:72], 0.0)
    running = climb(running, "gz", 3, 1)
    (modes,) = call(
        modes_kernel, [(1696, 128)], [(800, 128), (112, 128), (112, 128), (848, 128), (256, 128)], 9
    )(*block, ya, yb, vectors)
    running = climb(running, "gy", 6, 6)
    (modes,) = call(middle_kernel, [(1696, 128)], [(848, 128), (16, 128)], 3)(modes, vectors, eigen)
    local, edge_l, edge_h, xs = call(
        points_kernel, [(10, 10, 8, 128), (10, 16, 128), (10, 16, 128), (56, 128)], [(1696, 128), (848, 128)], 2
    )(modes, vectors)
    xr = swap(xs, "gx", 1)
    ya, yb = call(yfold_send_kernel, [(64, 128), (64, 128)], [], 3)(edge_l, edge_h, xr)
    ya, yb = swap(ya, "gy", 1), swap_odd(yb, "gy")
    running = climb(running, "gz", 12, 3)
    parts = (local, edge_l, edge_h, xr, ya, yb)
    za, zb = call(zfold_send_kernel, [(24, 128), (8, 128)], [(128, 128)] * 2, 7)(*parts, running)
    za, zb = swap(za, "gz", 1), swap_odd(zb, "gz")
    (out,) = call(
        post_kernel, [(256, 256)], [(128, 128), (128, 128), (2, 256, 128), (8, 8, 8, 128)], 12
    )(*parts, za, zb, coarse_basis, sep, running, ownsol)
    return out.reshape(residual.shape)


def solution(mesh):
    in_specs = (
        P("gx", "gy", "gz"),
        P("gx", "gy", "gz", None, None, None, None),
        P("gx", "gy", "gz", None, None, None),
        P(),
        P("gx", "gy", "gz", None, None),
        P("gx", "gy", "gz", None, None, None),
    )
    return jax.shard_map(work, mesh=mesh, in_specs=in_specs, out_specs=P("gx", "gy", "gz"), check_vma=False)
```

```python
import functools

import jax
import jax.numpy as jnp
from jax import lax
from jax.experimental import pallas as pl
from jax.experimental.pallas import tpu as pltpu
from jax.sharding import PartitionSpec as P


F32 = jnp.float32
VM = pl.BlockSpec(memory_space=pltpu.VMEM)


def iotas(rows=8):
    lane = lax.broadcasted_iota(jnp.int32, (rows, 128), 1)
    sub = lax.broadcasted_iota(jnp.int32, (rows, 128), 0)
    return lane, sub


def roll(value, shift):
    shift = shift % 128
    return value if shift == 0 else pltpu.roll(value, shift, value.ndim - 1)


def row(ref, index, rows=8):
    return jnp.broadcast_to(ref[pl.ds(index, 1), :], (rows, 128))


def total(terms):
    terms = list(terms)
    while len(terms) > 1:
        terms = [a + b for a, b in zip(terms[::2], terms[1::2])] + terms[len(terms) & ~1 :]
    return terms[0]


def chain(pairs):
    acc = None
    for a, b in pairs:
        acc = a * b if acc is None else acc + a * b
    return acc


def pre_kernel(
    x_ref, sep_ref, basis_ref, own_ref, core_ref, xs_ref, run_ref, ownsol_ref, xv, xt, sepv, basisv, ownv, xsem, sems
):
    copies = [pltpu.make_async_copy(x_ref.at[pl.ds(p * 128, 128), :], xv.at[p], xsem.at[p]) for p in range(2)]
    small = [
        pltpu.make_async_copy(a, b, sems.at[n])
        for n, (a, b) in enumerate(((basis_ref, basisv), (own_ref, ownv), (sep_ref, sepv)))
    ]
    for copy in copies + small:
        copy.start()
    gx = lax.axis_index("gx")
    lane, _ = iotas()
    low_q = (lane & 32) == 0
    high_p = lane >= 64
    for p in range(2):
        copies[p].wait()
        xt[p] = xv[p].T
    for pair in range(4):
        k0, k1 = 2 * pair, 2 * pair + 1
        pieces = [xt[p, pl.ds(k, 32, stride=8), :] for p in range(2) for k in (k0, k1)]
        block = jnp.concatenate(pieces, 0).T
        for i in range(8):
            a = block[i * 16 : i * 16 + 8]
            b = block[i * 16 + 8 : i * 16 + 16]
            core_ref[i, k0] = jnp.where(low_q, a, roll(b, 32))
            core_ref[i, k1] = jnp.where(low_q, roll(a, 96), b)

    def outgoing(k):
        return jnp.where(gx == 0, core_ref[7, k], roll(core_ref[0, k], 64))

    for k in range(4):
        xs_ref[k * 8 : k * 8 + 8] = jnp.where(high_p, outgoing(k), roll(outgoing(k + 4), 64))
    small[0].wait()
    sums = []
    for i in range(8):
        weights = basisv[i]
        sums.append(chain((core_ref[i, k], jnp.broadcast_to(weights[:, k : k + 1], (8, 128))) for k in range(8)))
    lanes = jnp.sum(total(sums), axis=0, keepdims=True)
    lane16, sub16 = iotas(16)
    spread = jnp.where(((lane16 & 31) >> 1) == sub16, jnp.broadcast_to(lanes, (16, 128)), 0.0)
    rhs = jnp.sum(spread, axis=1, keepdims=True)
    small[1].wait()
    own = ownv[...]
    coef = jnp.sum(own * rhs, axis=0, keepdims=True)
    ownsol_ref[...] = jnp.broadcast_to(jnp.sum(own * coef, axis=1, keepdims=True), (16, 128))
    small[2].wait()
    for level in range(sep_ref.shape[0]):
        part = jnp.sum(sepv[level] * rhs, axis=0, keepdims=True)
        for h in range(2):
            run_ref[8 * h + level : 8 * h + level + 1, :] = part[:, h * 128 : h * 128 + 128]


def zface_kernel(core_ref, xr_ref, ends_ref, za_ref, zb_ref):
    gx = lax.axis_index("gx")
    even = lax.rem(lax.axis_index("gz"), 2) == 0
    lane, _ = iotas()
    high_p = lane >= 64
    slot = lane & 31
    for k in range(8):
        at = (k % 4) * 8
        got = xr_ref[at : at + 8]
        if k >= 4:
            got = roll(got, 64)
        ends_ref[0, k] = jnp.where(high_p, roll(core_ref[7, k], 64), jnp.where(gx == 1, roll(got, 64), 0.0))
        ends_ref[1, k] = jnp.where(high_p, jnp.where(gx == 0, got, 0.0), roll(core_ref[0, k], 64))
    upper = jnp.zeros((8, 128), F32)
    lower = jnp.zeros((8, 128), F32)
    for i in range(10):
        upper = jnp.where(slot == i, roll(plane(core_ref, ends_ref, i, 7), i - 31), upper)
        lower = jnp.where(slot == i, roll(plane(core_ref, ends_ref, i, 0), i), lower)
    za_ref[...] = jnp.where(even, upper, lower)
    zb_ref[...] = jnp.where(even, lower, upper)


def plane(core_ref, ends_ref, i, k):
    return core_ref[i - 1, k] if 1 <= i <= 8 else ends_ref[i // 9, k]


def sides(a, b, axis):
    index = lax.axis_index(axis)
    even = lax.rem(index, 2) == 0
    above = jnp.where(index == lax.axis_size(axis) - 1, 0.0, jnp.where(even, a, b))
    below = jnp.where(index == 0, 0.0, jnp.where(even, b, a))
    return above, below


def z_halo(core_ref, ends_ref, za_ref, zb_ref, slot):
    from_above, from_below = sides(za_ref[...], zb_ref[...], "gz")
    first, last = [], []
    for i in range(10):
        first.append(jnp.where(slot == 0, roll(from_below, -i), roll(plane(core_ref, ends_ref, i, 7), 1)))
        last.append(jnp.where(slot == 31, roll(from_above, 31 - i), roll(plane(core_ref, ends_ref, i, 0), -1)))
    return first, last


def y_rows(first, last, core2_ref, ends2_ref, scr):
    for i in range(10):
        scr[pl.ds(i * 8, 8), :] = first[i]
        scr[pl.ds(128 + i * 8, 8), :] = last[i]
    low, high = [], []
    for i in range(10):
        ref, at = (core2_ref, (i - 1) * 64) if 1 <= i <= 8 else (ends2_ref, (i // 9) * 64)
        low.append(ref[pl.ds(at, 8, stride=8), :])
        high.append(ref[pl.ds(at + 7, 8, stride=8), :])
    low_ends = [scr[pl.ds(b, 16, stride=8), :] for b in (0, 128)]
    high_ends = [scr[pl.ds(b + 7, 16, stride=8), :] for b in (0, 128)]
    return low, high, low_ends, high_ends


def yface_kernel(core_ref, core2_ref, ends_ref, ends2_ref, za_ref, zb_ref, ya_ref, yb_ref, scr):
    even_y = lax.rem(lax.axis_index("gy"), 2) == 0
    lane, _ = iotas()
    low_q = (lane & 32) == 0
    first, last = z_halo(core_ref, ends_ref, za_ref, zb_ref, lane & 31)
    low, high, low_ends, high_ends = y_rows(first, last, core2_ref, ends2_ref, scr)
    for i in range(5):
        down = jnp.where(low_q, low[i], roll(low[i + 5], 32))
        up = jnp.where(low_q, roll(high[i + 5], 96), high[i])
        ya_ref[i * 8 : i * 8 + 8] = jnp.where(even_y, up, down)
        yb_ref[i * 8 : i * 8 + 8] = jnp.where(even_y, down, up)
    low_q = (iotas(16)[0] & 32) == 0
    down = jnp.where(low_q, low_ends[0], roll(low_ends[1], 32))
    up = jnp.where(low_q, roll(high_ends[1], 96), high_ends[0])
    ya_ref[40:56] = jnp.where(even_y, up, down)
    yb_ref[40:56] = jnp.where(even_y, down, up)


def factors_kernel(vec_ref, s_ref):
    for a in range(10):
        for i in range(10):
            s_ref[(i * 10 + a) * 8 : (i * 10 + a) * 8 + 3] = vec_ref[i, a].astype(F32)


def factor_of(s):
    return lambda d, i, a: row(s, (i * 10 + a) * 8 + d)


def along_x(source, target, factor, transposed):
    def step(k, _):
        for h in range(2):
            at = k * 16 + 8 * h
            held = [source[pl.ds(i * 160 + at, 8), :] for i in range(10)]
            for a in range(10):
                target[pl.ds(a * 160 + at, 8), :] = chain(
                    (factor(0, a, i) if transposed else factor(0, i, a), held[i]) for i in range(10)
                )
        return 0

    lax.fori_loop(0, 10, step, 0)


def modes_kernel(
    core_ref, core2_ref, ends_ref, ends2_ref, za_ref, zb_ref, ya_ref, yb_ref, s, u, block, jl, jh, scr
):
    lane, _ = iotas()
    low_q = (lane & 32) == 0
    first, last = z_halo(core_ref, ends_ref, za_ref, zb_ref, lane & 31)
    low, high, low_ends, high_ends = y_rows(first, last, core2_ref, ends2_ref, scr)
    for i in range(10):
        block[pl.ds(i * 80, 8), :] = first[i]
        block[pl.ds(i * 80 + 72, 8), :] = last[i]
        for k in range(8):
            block[pl.ds(i * 80 + 8 + k * 8, 8), :] = plane(core_ref, ends_ref, i, k)
    for i in range(10):
        at = (i % 5) * 8
        above, below = sides(ya_ref[at : at + 8], yb_ref[at : at + 8], "gy")
        if i < 5:
            above, below = roll(above, 32), roll(below, 96)
        jl[pl.ds(i * 8, 8), :] = jnp.where(low_q, below, roll(high[i], 32))
        jh[pl.ds(i * 8, 8), :] = jnp.where(low_q, roll(low[i], 96), above)
    low_q16 = (iotas(16)[0] & 32) == 0
    above, below = sides(ya_ref[40:56], yb_ref[40:56], "gy")
    jl[80:96] = jnp.where(low_q16, roll(below, 96), roll(high_ends[0], 32))
    jl[96:112] = jnp.where(low_q16, below, roll(high_ends[1], 32))
    jh[80:96] = jnp.where(low_q16, roll(low_ends[0], 96), roll(above, 32))
    jh[96:112] = jnp.where(low_q16, roll(low_ends[1], 96), above)
    factor = factor_of(s)
    front = [[s[pl.ds((j * 10 + 8 * h) * 8 + 1, 8, stride=8), :] for j in range(10)] for h in range(2)]

    def fwd_y(i, _):
        for k in range(10):
            edge = i * 8 + k - 1 if 1 <= k <= 8 else (80 + i if k == 0 else 96 + i)
            at = (i * 10 + k) * 8
            rows = [row(jl, edge)] + [row(block, at + j) for j in range(8)] + [row(jh, edge)]
            for h in range(2):
                out = chain((front[h][j], rows[j]) for j in range(10))
                u[pl.ds((i * 10 + k) * 16 + 8 * h, 8), :] = out
        return 0

    lax.fori_loop(0, 10, fwd_y, 0)

    along_x(u, u, factor, False)


def middle_kernel(u_ref, s, eig_ref, u, eg):
    eg[...] = jnp.ones((16, 128), F32)
    for a in range(10):
        eg[a : a + 1] = eig_ref[1, a]
    factor = factor_of(s)

    def wide(value):
        return jnp.broadcast_to(value, (8, 128))

    def along_z(a, _):
        for h in range(2):
            at = a * 160 + 8 * h
            held = [u_ref[pl.ds(at + k * 16, 8), :] for k in range(10)]
            base = wide(eig_ref[0, a]) + eg[8 * h : 8 * h + 8]
            modes = []
            for c in range(10):
                modes.append(chain((factor(2, k, c), held[k]) for k in range(10)) / (base + wide(eig_ref[2, c])))
            for k in range(10):
                u[pl.ds(at + k * 16, 8), :] = chain((factor(2, k, c), modes[c]) for c in range(10))
        return 0

    lax.fori_loop(0, 10, along_z, 0)


def points_kernel(u_ref, s, l_ref, hl_ref, hh_ref, xs_ref, u):
    gx = lax.axis_index("gx")
    lane, _ = iotas()
    factor = factor_of(s)
    along_x(u_ref, u, factor, True)
    back = [s[pl.ds((10 + b) * 8 + 1, 8, stride=80), :] for b in range(10)]

    def back_y(i, _):
        for k in range(10):
            at = (i * 10 + k) * 16
            l_ref[i, k] = chain((back[b], row(u, at + b)) for b in range(10))
        for h in range(2):
            cut = [u[pl.ds(i * 160 + 128 * h + b, 8, stride=16), :] for b in range(10)]
            hl_ref[i, 8 * h : 8 * h + 8] = chain((factor(1, 0, b), cut[b]) for b in range(10))
            hh_ref[i, 8 * h : 8 * h + 8] = chain((factor(1, 9, b), cut[b]) for b in range(10))
        return 0

    lax.fori_loop(0, 10, back_y, 0)
    high_p = lane >= 64

    def outgoing(ref, k):
        return jnp.where(gx == 0, ref[9, k], roll(ref[0, k], 64))

    for k in range(5):
        xs_ref[k * 8 : k * 8 + 8] = jnp.where(high_p, outgoing(l_ref, k), roll(outgoing(l_ref, k + 5), 64))
    high_p = iotas(16)[0] >= 64
    edge_l = jnp.where(gx == 0, hl_ref[9], roll(hl_ref[0], 64))
    edge_h = jnp.where(gx == 0, hh_ref[9], roll(hh_ref[0], 64))
    xs_ref[40:56] = jnp.where(high_p, edge_l, roll(edge_h, 64))


def fold_x(value, i, opposite, received, gx, high_p):
    if i == 8:
        return value + jnp.where(high_p, jnp.where(gx == 0, received, 0.0), roll(opposite, 64))
    if i == 1:
        return value + jnp.where(high_p, roll(opposite, 64), jnp.where(gx == 1, roll(received, 64), 0.0))
    return value


def edge_rows(hl_ref, hh_ref, xr_ref, gx):
    high_p = iotas(16)[0] >= 64
    packed = xr_ref[40:56]
    low, high = [], []
    for i in range(1, 9):
        j = {1: 9, 8: 0}.get(i, i)
        low.append(fold_x(hl_ref[i], i, hl_ref[j], packed, gx, high_p))
        high.append(fold_x(hh_ref[i], i, hh_ref[j], roll(packed, 64), gx, high_p))
    return low, high


def yfold_send_kernel(hl_ref, hh_ref, xr_ref, run_ref, ya_ref, yb_ref):
    ya_ref[64:80] = run_ref[...]
    gx = lax.axis_index("gx")
    even_y = lax.rem(lax.axis_index("gy"), 2) == 0
    low_q = (iotas(16)[0] & 32) == 0
    low, high = edge_rows(hl_ref, hh_ref, xr_ref, gx)
    for i in range(4):
        down = jnp.where(low_q, low[i], roll(low[i + 4], 32))
        up = jnp.where(low_q, roll(high[i + 4], 96), high[i])
        ya_ref[i * 16 : i * 16 + 16] = jnp.where(even_y, up, down)
        yb_ref[i * 16 : i * 16 + 16] = jnp.where(even_y, down, up)


def fold_rows(hl_ref, hh_ref, xr_ref, ya_ref, yb_ref, rows_first, rows_last, gx):
    low_q = (iotas(16)[0] & 32) == 0
    low, high = edge_rows(hl_ref, hh_ref, xr_ref, gx)
    for i in range(8):
        at = (i % 4) * 16
        above, below = sides(ya_ref[at : at + 16], yb_ref[at : at + 16], "gy")
        if i < 4:
            above, below = roll(above, 32), roll(below, 96)
        rows_last[pl.ds(i * 16, 16), :] = jnp.where(low_q, roll(low[i], 96), above)
        rows_first[pl.ds(i * 16, 16), :] = jnp.where(low_q, below, roll(high[i], 32))


def folded_xy(l_ref, xr_ref, rows_first, rows_last, i, k, gx, lane, sub):
    high_p = lane >= 64
    value = l_ref[i, k]
    if i in (1, 8):
        packed = xr_ref[(k % 5) * 8 : (k % 5) * 8 + 8]
        received = packed if k < 5 else roll(packed, 64)
        value = fold_x(value, i, l_ref[9 if i == 1 else 0, k], received, gx, high_p)
    at = (i - 1) * 16 + k
    return value + jnp.where(sub == 0, row(rows_first, at), jnp.where(sub == 7, row(rows_last, at), 0.0))


def zfold_send_kernel(l_ref, hl_ref, hh_ref, xr_ref, ya_ref, yb_ref, run_ref, za_ref, zb_ref, rows_first, rows_last):
    za_ref[8:24] = run_ref[...]
    gx = lax.axis_index("gx")
    even_z = lax.rem(lax.axis_index("gz"), 2) == 0
    lane, sub = iotas()
    slot = lane & 31
    fold_rows(hl_ref, hh_ref, xr_ref, ya_ref, yb_ref, rows_first, rows_last, gx)
    down = jnp.zeros((8, 128), F32)
    up = jnp.zeros((8, 128), F32)
    for i in range(8):
        down = jnp.where(slot == i, roll(folded_xy(l_ref, xr_ref, rows_first, rows_last, i + 1, 0, gx, lane, sub), i), down)
        up = jnp.where(slot == i, roll(folded_xy(l_ref, xr_ref, rows_first, rows_last, i + 1, 9, gx, lane, sub), i - 31), up)
    za_ref[:8] = jnp.where(even_z, up, down)
    zb_ref[...] = jnp.where(even_z, down, up)


def gather_kernel(
    l_ref, hl_ref, hh_ref, xr_ref, ya_ref, yb_ref, basis_ref, sum_ref, tile_ref, rows_first, rows_last, xt, grid
):
    gx = lax.axis_index("gx")
    lane, sub = iotas()
    slot = lane & 31
    low_q = (lane & 32) == 0
    fold_rows(hl_ref, hh_ref, xr_ref, ya_ref, yb_ref, rows_first, rows_last, gx)
    for i in range(8):
        get = functools.partial(folded_xy, l_ref, xr_ref, rows_first, rows_last, i + 1, gx=gx, lane=lane, sub=sub)
        before, after = get(0), get(9)
        for k in range(8):
            value = get(k + 1)
            if k == 0:
                value = value + jnp.where(slot == 0, 0.0, roll(after, 1))
            if k == 7:
                value = value + jnp.where(slot == 31, 0.0, roll(before, -1))
            grid[i, k] = value
        weights = jnp.concatenate([basis_ref[i]] * 16, 1)
        tile_ref[i * 8 : i * 8 + 8] = weights
    for pair in range(4):
        k0, k1 = 2 * pair, 2 * pair + 1
        pieces = []
        for i in range(8):
            c0, c1 = grid[i, k0], grid[i, k1]
            pieces.append(jnp.where(low_q, c0, roll(c1, 32)))
            pieces.append(jnp.where(low_q, roll(c0, 96), c1))
        block = jnp.concatenate(pieces, 0).T
        for p in range(2):
            for t, k in enumerate((k0, k1)):
                at = p * 64 + t * 32
                xt[p, pl.ds(k, 32, stride=8), :] = block[at : at + 32]
    sum_ref[...] = jnp.concatenate([xt[0], xt[1]], 1).T


def post_kernel(sum_ref, tile_ref, za_ref, zb_ref, sep_ref, run_ref, ownsol_ref, out_ref, total_ref, sems):
    lane, _ = iotas()
    running = run_ref[...] + za_ref[8:24]
    weighted = total(
        sep_ref[level][:, h * 128 : h * 128 + 128] * running[8 * h + level : 8 * h + level + 1, :]
        for h in range(2)
        for level in range(sep_ref.shape[0])
    )
    solution_col = ownsol_ref[:, :1] + jnp.sum(weighted, axis=1, keepdims=True)
    lane16, sub16 = iotas(16)
    along_z = []
    for t in range(2):
        spread = jnp.where((lane16 >> 4) + 8 * t == sub16, jnp.broadcast_to(solution_col, (16, 128)), 0.0)
        along_z.append(jnp.broadcast_to(jnp.sum(spread, axis=0, keepdims=True), (8, 128)))
    from_above, from_below = sides(za_ref[:8], zb_ref[...], "gz")
    copies = []
    for p in range(2):
        for i in range(8):
            weights = tile_ref[i * 8 : i * 8 + 8]
            low, high = weights * along_z[0], weights * along_z[1]
            for q in range(2):
                at = ((p * 8 + i) * 2 + q) * 8
                source = p * 64 + q * 32 + i
                first = sum_ref[at : at + 8, :128] + low
                last = sum_ref[at : at + 8, 128:] + high
                total_ref[at : at + 8, :128] = first + jnp.where(lane == 0, roll(from_below, -source), 0.0)
                total_ref[at : at + 8, 128:] = last + jnp.where(lane == 127, roll(from_above, 127 - source), 0.0)
        rows = pl.ds(p * 128, 128)
        copies.append(pltpu.make_async_copy(total_ref.at[rows, :], out_ref.at[rows, :], sems.at[p]))
        copies[p].start()
    for copy in copies:
        copy.wait()


def call(kernel, outs, scratch, n_in, limit=4 << 20, far=0, semaphores=(), out_space=pltpu.VMEM):
    return pl.pallas_call(
        kernel,
        out_shape=[jax.ShapeDtypeStruct(shape, F32) for shape in outs],
        in_specs=[pl.BlockSpec(memory_space=pltpu.HBM)] * far + [VM] * (n_in - far),
        out_specs=[pl.BlockSpec(memory_space=out_space)] * len(outs),
        scratch_shapes=[pltpu.VMEM(shape, F32) for shape in scratch] + list(semaphores),
        compiler_params=pltpu.CompilerParams(vmem_limit_bytes=limit),
    )


def far(value):
    return pltpu.with_memory_space_constraint(value, pltpu.HBM)


def swap(value, axis, distance):
    return lax.ppermute(value, axis, [(i, i ^ distance) for i in range(lax.axis_size(axis))])


def swap_odd(value, axis):
    count = lax.axis_size(axis)
    return lax.ppermute(value, axis, [(i, (i + 1 if i % 2 else i - 1) % count) for i in range(count)])


def work(residual, fdm_vectors, fdm_eigen, coarse_basis, x_interior, x_separator):
    levels, unknowns, width = x_separator.shape[3:]
    x = residual.reshape(256, 256)
    vectors = fdm_vectors.reshape(3, 10, 10, 128).transpose(1, 2, 0, 3)
    eigen = fdm_eigen.reshape(3, 10, 1, 128)
    own = x_interior.reshape(unknowns, unknowns)
    sep = x_separator.reshape(levels, unknowns, width)
    level_of = lax.broadcasted_iota(jnp.int32, (16, 128), 0) & 7

    def climb(running, axis, distance, first):
        return running + jnp.where(level_of >= first, swap(running, axis, distance), 0.0)

    core, xs, running, ownsol = call(
        pre_kernel,
        [(8, 8, 8, 128), (32, 128), (16, 128), (16, 128)],
        [(2, 128, 256), (2, 256, 128), (levels, unknowns, width), (8, 8, 8), (unknowns, unknowns)],
        4,
        far=4,
        semaphores=(pltpu.SemaphoreType.DMA((2,)), pltpu.SemaphoreType.DMA((3,))),
    )(far(x), far(sep), far(coarse_basis), far(own))
    xr = swap(xs, "gx", 1)
    ends, za, zb = call(zface_kernel, [(2, 8, 8, 128), (8, 128), (8, 128)], [], 2)(core, xr)
    running = climb(running, "gy", 2, 5)
    za, zb = swap(za, "gz", 1), swap_odd(zb, "gz")
    running = climb(running, "gy", 6, 6)
    (factors,) = call(factors_kernel, [(848, 128)], [], 1)(vectors)
    block = (core, core.reshape(512, 128), ends, ends.reshape(128, 128), za, zb)
    ya, yb = call(yface_kernel, [(56, 128), (56, 128)], [(256, 128)], 6)(*block)
    ya, yb = swap(ya, "gy", 1), swap_odd(yb, "gy")
    running = climb(running, "gz", 4, 2)
    (modes,) = call(
        modes_kernel, [(1696, 128)], [(800, 128), (112, 128), (112, 128), (256, 128)], 9
    )(*block, ya, yb, factors)
    running = climb(running, "gz", 12, 3)
    (modes,) = call(middle_kernel, [(1696, 128)], [(16, 128)], 3)(modes, factors, eigen)
    running = climb(running, "gz", 3, 1)
    local, edge_l, edge_h, xs = call(
        points_kernel, [(10, 10, 8, 128), (10, 16, 128), (10, 16, 128), (56, 128)], [(1696, 128)], 2
    )(modes, factors)
    xr = swap(xs, "gx", 1)
    ya, yb = call(yfold_send_kernel, [(80, 128), (64, 128)], [], 4)(edge_l, edge_h, xr, running)
    ya, yb = swap(ya, "gy", 1), swap_odd(yb, "gy")
    running = running + jnp.where(level_of >= 4, ya[64:80], 0.0)
    running = climb(running, "gx", 1, 7)
    parts = (local, edge_l, edge_h, xr, ya, yb)
    za, zb = call(zfold_send_kernel, [(24, 128), (8, 128)], [(128, 128)] * 2, 7)(*parts, running)
    za, zb = swap(za, "gz", 1), swap_odd(zb, "gz")
    smooth, tile = call(
        gather_kernel, [(256, 256), (64, 128)], [(128, 128), (128, 128), (2, 256, 128), (8, 8, 8, 128)], 7
    )(*parts, coarse_basis)
    (out,) = call(
        post_kernel, [(256, 256)], [(256, 256)], 7, semaphores=(pltpu.SemaphoreType.DMA((2,)),), out_space=pltpu.HBM
    )(smooth, tile, za, zb, sep, running, ownsol)
    return out.reshape(residual.shape)


def solution(mesh):
    in_specs = (
        P("gx", "gy", "gz"),
        P("gx", "gy", "gz", None, None, None, None),
        P("gx", "gy", "gz", None, None, None),
        P(),
        P("gx", "gy", "gz", None, None),
        P("gx", "gy", "gz", None, None, None),
    )
    return jax.shard_map(work, mesh=mesh, in_specs=in_specs, out_specs=P("gx", "gy", "gz"), check_vma=False)
```

```python
import functools

import jax
import jax.numpy as jnp
from jax import lax
from jax.experimental import pallas as pl
from jax.experimental.pallas import tpu as pltpu
from jax.sharding import PartitionSpec as P


F32 = jnp.float32
VM = pl.BlockSpec(memory_space=pltpu.VMEM)


def iotas(rows=8):
    lane = lax.broadcasted_iota(jnp.int32, (rows, 128), 1)
    sub = lax.broadcasted_iota(jnp.int32, (rows, 128), 0)
    return lane, sub


def roll(value, shift):
    shift = shift % 128
    return value if shift == 0 else pltpu.roll(value, shift, value.ndim - 1)


def row(ref, index, rows=8):
    return jnp.broadcast_to(ref[pl.ds(index, 1), :], (rows, 128))


def total(terms):
    terms = list(terms)
    while len(terms) > 1:
        terms = [a + b for a, b in zip(terms[::2], terms[1::2])] + terms[len(terms) & ~1 :]
    return terms[0]


def chain(pairs):
    acc = None
    for a, b in pairs:
        acc = a * b if acc is None else acc + a * b
    return acc


def pre_kernel(
    x_ref, sep_ref, basis_ref, own_ref, core_ref, xs_ref, run_ref, ownsol_ref, xv, xt, sepv, basisv, ownv, xsem, sems
):
    copies = [pltpu.make_async_copy(x_ref.at[pl.ds(p * 128, 128), :], xv.at[p], xsem.at[p]) for p in range(2)]
    small = [
        pltpu.make_async_copy(a, b, sems.at[n])
        for n, (a, b) in enumerate(((basis_ref, basisv), (own_ref, ownv), (sep_ref, sepv)))
    ]
    for copy in copies + small:
        copy.start()
    gx = lax.axis_index("gx")
    lane, _ = iotas()
    low_q = (lane & 32) == 0
    high_p = lane >= 64
    for p in range(2):
        copies[p].wait()
        xt[p] = xv[p].T
    for pair in range(4):
        k0, k1 = 2 * pair, 2 * pair + 1
        pieces = [xt[p, pl.ds(k, 32, stride=8), :] for p in range(2) for k in (k0, k1)]
        block = jnp.concatenate(pieces, 0).T
        for i in range(8):
            a = block[i * 16 : i * 16 + 8]
            b = block[i * 16 + 8 : i * 16 + 16]
            core_ref[i, k0] = jnp.where(low_q, a, roll(b, 32))
            core_ref[i, k1] = jnp.where(low_q, roll(a, 96), b)

    def outgoing(k):
        return jnp.where(gx == 0, core_ref[7, k], roll(core_ref[0, k], 64))

    for k in range(4):
        xs_ref[k * 8 : k * 8 + 8] = jnp.where(high_p, outgoing(k), roll(outgoing(k + 4), 64))
    small[0].wait()
    sums = []
    for i in range(8):
        weights = basisv[i]
        sums.append(chain((core_ref[i, k], jnp.broadcast_to(weights[:, k : k + 1], (8, 128))) for k in range(8)))
    lanes = jnp.sum(total(sums), axis=0, keepdims=True)
    lane16, sub16 = iotas(16)
    spread = jnp.where(((lane16 & 31) >> 1) == sub16, jnp.broadcast_to(lanes, (16, 128)), 0.0)
    rhs = jnp.sum(spread, axis=1, keepdims=True)
    small[1].wait()
    own = ownv[...]
    coef = jnp.sum(own * rhs, axis=0, keepdims=True)
    ownsol_ref[...] = jnp.broadcast_to(jnp.sum(own * coef, axis=1, keepdims=True), (16, 128))
    small[2].wait()
    for level in range(sep_ref.shape[0]):
        part = jnp.sum(sepv[level] * rhs, axis=0, keepdims=True)
        for h in range(2):
            run_ref[8 * h + level : 8 * h + level + 1, :] = part[:, h * 128 : h * 128 + 128]


def zface_kernel(core_ref, xr_ref, ends_ref, za_ref, zb_ref):
    gx = lax.axis_index("gx")
    even = lax.rem(lax.axis_index("gz"), 2) == 0
    lane, _ = iotas()
    high_p = lane >= 64
    slot = lane & 31
    for k in range(8):
        at = (k % 4) * 8
        got = xr_ref[at : at + 8]
        if k >= 4:
            got = roll(got, 64)
        ends_ref[0, k] = jnp.where(high_p, roll(core_ref[7, k], 64), jnp.where(gx == 1, roll(got, 64), 0.0))
        ends_ref[1, k] = jnp.where(high_p, jnp.where(gx == 0, got, 0.0), roll(core_ref[0, k], 64))
    upper = jnp.zeros((8, 128), F32)
    lower = jnp.zeros((8, 128), F32)
    for i in range(10):
        upper = jnp.where(slot == i, roll(plane(core_ref, ends_ref, i, 7), i - 31), upper)
        lower = jnp.where(slot == i, roll(plane(core_ref, ends_ref, i, 0), i), lower)
    za_ref[...] = jnp.where(even, upper, lower)
    zb_ref[...] = jnp.where(even, lower, upper)


def plane(core_ref, ends_ref, i, k):
    return core_ref[i - 1, k] if 1 <= i <= 8 else ends_ref[i // 9, k]


def sides(a, b, axis):
    index = lax.axis_index(axis)
    even = lax.rem(index, 2) == 0
    above = jnp.where(index == lax.axis_size(axis) - 1, 0.0, jnp.where(even, a, b))
    below = jnp.where(index == 0, 0.0, jnp.where(even, b, a))
    return above, below


def z_halo(core_ref, ends_ref, za_ref, zb_ref, slot):
    from_above, from_below = sides(za_ref[...], zb_ref[...], "gz")
    first, last = [], []
    for i in range(10):
        first.append(jnp.where(slot == 0, roll(from_below, -i), roll(plane(core_ref, ends_ref, i, 7), 1)))
        last.append(jnp.where(slot == 31, roll(from_above, 31 - i), roll(plane(core_ref, ends_ref, i, 0), -1)))
    return first, last


def y_rows(first, last, core2_ref, ends2_ref, scr):
    for i in range(10):
        scr[pl.ds(i * 8, 8), :] = first[i]
        scr[pl.ds(128 + i * 8, 8), :] = last[i]
    low, high = [], []
    for i in range(10):
        ref, at = (core2_ref, (i - 1) * 64) if 1 <= i <= 8 else (ends2_ref, (i // 9) * 64)
        low.append(ref[pl.ds(at, 8, stride=8), :])
        high.append(ref[pl.ds(at + 7, 8, stride=8), :])
    low_ends = [scr[pl.ds(b, 16, stride=8), :] for b in (0, 128)]
    high_ends = [scr[pl.ds(b + 7, 16, stride=8), :] for b in (0, 128)]
    return low, high, low_ends, high_ends


def yface_kernel(core_ref, core2_ref, ends_ref, ends2_ref, za_ref, zb_ref, ya_ref, yb_ref, scr):
    even_y = lax.rem(lax.axis_index("gy"), 2) == 0
    lane, _ = iotas()
    low_q = (lane & 32) == 0
    first, last = z_halo(core_ref, ends_ref, za_ref, zb_ref, lane & 31)
    low, high, low_ends, high_ends = y_rows(first, last, core2_ref, ends2_ref, scr)
    for i in range(5):
        down = jnp.where(low_q, low[i], roll(low[i + 5], 32))
        up = jnp.where(low_q, roll(high[i + 5], 96), high[i])
        ya_ref[i * 8 : i * 8 + 8] = jnp.where(even_y, up, down)
        yb_ref[i * 8 : i * 8 + 8] = jnp.where(even_y, down, up)
    low_q = (iotas(16)[0] & 32) == 0
    down = jnp.where(low_q, low_ends[0], roll(low_ends[1], 32))
    up = jnp.where(low_q, roll(high_ends[1], 96), high_ends[0])
    ya_ref[40:56] = jnp.where(even_y, up, down)
    yb_ref[40:56] = jnp.where(even_y, down, up)


def factors_kernel(vec_ref, s_ref):
    for a in range(10):
        for i in range(10):
            s_ref[(i * 10 + a) * 8 : (i * 10 + a) * 8 + 3] = vec_ref[i, a].astype(F32)


def factor_of(s):
    return lambda d, i, a: row(s, (i * 10 + a) * 8 + d)


def along_x(source, target, factor, transposed):
    def step(k, _):
        for h in range(2):
            at = k * 16 + 8 * h
            held = [source[pl.ds(i * 160 + at, 8), :] for i in range(10)]
            for a in range(10):
                target[pl.ds(a * 160 + at, 8), :] = chain(
                    (factor(0, a, i) if transposed else factor(0, i, a), held[i]) for i in range(10)
                )
        return 0

    lax.fori_loop(0, 10, step, 0)


def modes_kernel(
    core_ref, core2_ref, ends_ref, ends2_ref, za_ref, zb_ref, ya_ref, yb_ref, s, u, block, jl, jh, scr
):
    lane, _ = iotas()
    low_q = (lane & 32) == 0
    first, last = z_halo(core_ref, ends_ref, za_ref, zb_ref, lane & 31)
    low, high, low_ends, high_ends = y_rows(first, last, core2_ref, ends2_ref, scr)
    for i in range(10):
        block[pl.ds(i * 80, 8), :] = first[i]
        block[pl.ds(i * 80 + 72, 8), :] = last[i]
        for k in range(8):
            block[pl.ds(i * 80 + 8 + k * 8, 8), :] = plane(core_ref, ends_ref, i, k)
    for i in range(10):
        at = (i % 5) * 8
        above, below = sides(ya_ref[at : at + 8], yb_ref[at : at + 8], "gy")
        if i < 5:
            above, below = roll(above, 32), roll(below, 96)
        jl[pl.ds(i * 8, 8), :] = jnp.where(low_q, below, roll(high[i], 32))
        jh[pl.ds(i * 8, 8), :] = jnp.where(low_q, roll(low[i], 96), above)
    low_q16 = (iotas(16)[0] & 32) == 0
    above, below = sides(ya_ref[40:56], yb_ref[40:56], "gy")
    jl[80:96] = jnp.where(low_q16, roll(below, 96), roll(high_ends[0], 32))
    jl[96:112] = jnp.where(low_q16, below, roll(high_ends[1], 32))
    jh[80:96] = jnp.where(low_q16, roll(low_ends[0], 96), roll(above, 32))
    jh[96:112] = jnp.where(low_q16, roll(low_ends[1], 96), above)
    factor = factor_of(s)
    front = [[s[pl.ds((j * 10 + 8 * h) * 8 + 1, 8, stride=8), :] for j in range(10)] for h in range(2)]

    def fwd_y(i, _):
        for k in range(10):
            edge = i * 8 + k - 1 if 1 <= k <= 8 else (80 + i if k == 0 else 96 + i)
            at = (i * 10 + k) * 8
            rows = [row(jl, edge)] + [row(block, at + j) for j in range(8)] + [row(jh, edge)]
            for h in range(2):
                out = chain((front[h][j], rows[j]) for j in range(10))
                u[pl.ds((i * 10 + k) * 16 + 8 * h, 8), :] = out
        return 0

    lax.fori_loop(0, 10, fwd_y, 0)

    along_x(u, u, factor, False)


def middle_kernel(u_ref, s, eig_ref, u, eg):
    eg[...] = jnp.ones((16, 128), F32)
    for a in range(10):
        eg[a : a + 1] = eig_ref[1, a]
    factor = factor_of(s)

    def wide(value):
        return jnp.broadcast_to(value, (8, 128))

    def along_z(a, _):
        for h in range(2):
            at = a * 160 + 8 * h
            held = [u_ref[pl.ds(at + k * 16, 8), :] for k in range(10)]
            base = wide(eig_ref[0, a]) + eg[8 * h : 8 * h + 8]
            modes = []
            for c in range(10):
                modes.append(chain((factor(2, k, c), held[k]) for k in range(10)) / (base + wide(eig_ref[2, c])))
            for k in range(10):
                u[pl.ds(at + k * 16, 8), :] = chain((factor(2, k, c), modes[c]) for c in range(10))
        return 0

    lax.fori_loop(0, 10, along_z, 0)


def points_kernel(u_ref, s, l_ref, hl_ref, hh_ref, xs_ref, u):
    gx = lax.axis_index("gx")
    lane, _ = iotas()
    factor = factor_of(s)
    along_x(u_ref, u, factor, True)
    back = [s[pl.ds((10 + b) * 8 + 1, 8, stride=80), :] for b in range(10)]

    def back_y(i, _):
        for k in range(10):
            at = (i * 10 + k) * 16
            l_ref[i, k] = chain((back[b], row(u, at + b)) for b in range(10))
        for h in range(2):
            cut = [u[pl.ds(i * 160 + 128 * h + b, 8, stride=16), :] for b in range(10)]
            hl_ref[i, 8 * h : 8 * h + 8] = chain((factor(1, 0, b), cut[b]) for b in range(10))
            hh_ref[i, 8 * h : 8 * h + 8] = chain((factor(1, 9, b), cut[b]) for b in range(10))
        return 0

    lax.fori_loop(0, 10, back_y, 0)
    high_p = lane >= 64

    def outgoing(ref, k):
        return jnp.where(gx == 0, ref[9, k], roll(ref[0, k], 64))

    for k in range(5):
        xs_ref[k * 8 : k * 8 + 8] = jnp.where(high_p, outgoing(l_ref, k), roll(outgoing(l_ref, k + 5), 64))
    high_p = iotas(16)[0] >= 64
    edge_l = jnp.where(gx == 0, hl_ref[9], roll(hl_ref[0], 64))
    edge_h = jnp.where(gx == 0, hh_ref[9], roll(hh_ref[0], 64))
    xs_ref[40:56] = jnp.where(high_p, edge_l, roll(edge_h, 64))


def fold_x(value, i, opposite, received, gx, high_p):
    if i == 8:
        return value + jnp.where(high_p, jnp.where(gx == 0, received, 0.0), roll(opposite, 64))
    if i == 1:
        return value + jnp.where(high_p, roll(opposite, 64), jnp.where(gx == 1, roll(received, 64), 0.0))
    return value


def edge_rows(hl_ref, hh_ref, xr_ref, gx):
    high_p = iotas(16)[0] >= 64
    packed = xr_ref[40:56]
    low, high = [], []
    for i in range(1, 9):
        j = {1: 9, 8: 0}.get(i, i)
        low.append(fold_x(hl_ref[i], i, hl_ref[j], packed, gx, high_p))
        high.append(fold_x(hh_ref[i], i, hh_ref[j], roll(packed, 64), gx, high_p))
    return low, high


def yfold_send_kernel(hl_ref, hh_ref, xr_ref, run_ref, ya_ref, yb_ref):
    ya_ref[64:80] = run_ref[...]
    gx = lax.axis_index("gx")
    even_y = lax.rem(lax.axis_index("gy"), 2) == 0
    low_q = (iotas(16)[0] & 32) == 0
    low, high = edge_rows(hl_ref, hh_ref, xr_ref, gx)
    for i in range(4):
        down = jnp.where(low_q, low[i], roll(low[i + 4], 32))
        up = jnp.where(low_q, roll(high[i + 4], 96), high[i])
        ya_ref[i * 16 : i * 16 + 16] = jnp.where(even_y, up, down)
        yb_ref[i * 16 : i * 16 + 16] = jnp.where(even_y, down, up)


def fold_rows(hl_ref, hh_ref, xr_ref, ya_ref, yb_ref, rows_first, rows_last, gx):
    low_q = (iotas(16)[0] & 32) == 0
    low, high = edge_rows(hl_ref, hh_ref, xr_ref, gx)
    for i in range(8):
        at = (i % 4) * 16
        above, below = sides(ya_ref[at : at + 16], yb_ref[at : at + 16], "gy")
        if i < 4:
            above, below = roll(above, 32), roll(below, 96)
        rows_last[pl.ds(i * 16, 16), :] = jnp.where(low_q, roll(low[i], 96), above)
        rows_first[pl.ds(i * 16, 16), :] = jnp.where(low_q, below, roll(high[i], 32))


def folded_xy(l_ref, xr_ref, rows_first, rows_last, i, k, gx, lane, sub):
    high_p = lane >= 64
    value = l_ref[i, k]
    if i in (1, 8):
        packed = xr_ref[(k % 5) * 8 : (k % 5) * 8 + 8]
        received = packed if k < 5 else roll(packed, 64)
        value = fold_x(value, i, l_ref[9 if i == 1 else 0, k], received, gx, high_p)
    at = (i - 1) * 16 + k
    return value + jnp.where(sub == 0, row(rows_first, at), jnp.where(sub == 7, row(rows_last, at), 0.0))


def zfold_send_kernel(l_ref, hl_ref, hh_ref, xr_ref, ya_ref, yb_ref, run_ref, za_ref, zb_ref, rows_first, rows_last):
    za_ref[8:24] = run_ref[...]
    gx = lax.axis_index("gx")
    even_z = lax.rem(lax.axis_index("gz"), 2) == 0
    lane, sub = iotas()
    slot = lane & 31
    fold_rows(hl_ref, hh_ref, xr_ref, ya_ref, yb_ref, rows_first, rows_last, gx)
    down = jnp.zeros((8, 128), F32)
    up = jnp.zeros((8, 128), F32)
    for i in range(8):
        down = jnp.where(slot == i, roll(folded_xy(l_ref, xr_ref, rows_first, rows_last, i + 1, 0, gx, lane, sub), i), down)
        up = jnp.where(slot == i, roll(folded_xy(l_ref, xr_ref, rows_first, rows_last, i + 1, 9, gx, lane, sub), i - 31), up)
    za_ref[:8] = jnp.where(even_z, up, down)
    zb_ref[...] = jnp.where(even_z, down, up)


def gather_kernel(
    l_ref, hl_ref, hh_ref, xr_ref, ya_ref, yb_ref, basis_ref, sum_ref, tile_ref, rows_first, rows_last, xt, grid
):
    gx = lax.axis_index("gx")
    lane, sub = iotas()
    slot = lane & 31
    low_q = (lane & 32) == 0
    fold_rows(hl_ref, hh_ref, xr_ref, ya_ref, yb_ref, rows_first, rows_last, gx)
    for i in range(8):
        get = functools.partial(folded_xy, l_ref, xr_ref, rows_first, rows_last, i + 1, gx=gx, lane=lane, sub=sub)
        before, after = get(0), get(9)
        for k in range(8):
            value = get(k + 1)
            if k == 0:
                value = value + jnp.where(slot == 0, 0.0, roll(after, 1))
            if k == 7:
                value = value + jnp.where(slot == 31, 0.0, roll(before, -1))
            grid[i, k] = value
        weights = jnp.concatenate([basis_ref[i]] * 16, 1)
        tile_ref[i * 8 : i * 8 + 8] = weights
    for pair in range(4):
        k0, k1 = 2 * pair, 2 * pair + 1
        pieces = []
        for i in range(8):
            c0, c1 = grid[i, k0], grid[i, k1]
            pieces.append(jnp.where(low_q, c0, roll(c1, 32)))
            pieces.append(jnp.where(low_q, roll(c0, 96), c1))
        block = jnp.concatenate(pieces, 0).T
        for p in range(2):
            for t, k in enumerate((k0, k1)):
                at = p * 64 + t * 32
                xt[p, pl.ds(k, 32, stride=8), :] = block[at : at + 32]
    sum_ref[...] = jnp.concatenate([xt[0], xt[1]], 1).T


def post_kernel(sum_ref, tile_ref, za_ref, zb_ref, sep_ref, run_ref, ownsol_ref, out_ref, total_ref, sems):
    lane, _ = iotas()
    running = run_ref[...] + za_ref[8:24]
    weighted = total(
        sep_ref[level][:, h * 128 : h * 128 + 128] * running[8 * h + level : 8 * h + level + 1, :]
        for h in range(2)
        for level in range(sep_ref.shape[0])
    )
    solution_col = ownsol_ref[:, :1] + jnp.sum(weighted, axis=1, keepdims=True)
    lane16, sub16 = iotas(16)
    along_z = []
    for t in range(2):
        spread = jnp.where((lane16 >> 4) + 8 * t == sub16, jnp.broadcast_to(solution_col, (16, 128)), 0.0)
        along_z.append(jnp.broadcast_to(jnp.sum(spread, axis=0, keepdims=True), (8, 128)))
    from_above, from_below = sides(za_ref[:8], zb_ref[...], "gz")
    copies = []
    for p in range(2):
        for i in range(8):
            weights = tile_ref[i * 8 : i * 8 + 8]
            low, high = weights * along_z[0], weights * along_z[1]
            for q in range(2):
                at = ((p * 8 + i) * 2 + q) * 8
                source = p * 64 + q * 32 + i
                first = sum_ref[at : at + 8, :128] + low
                last = sum_ref[at : at + 8, 128:] + high
                total_ref[at : at + 8, :128] = first + jnp.where(lane == 0, roll(from_below, -source), 0.0)
                total_ref[at : at + 8, 128:] = last + jnp.where(lane == 127, roll(from_above, 127 - source), 0.0)
        rows = pl.ds(p * 128, 128)
        copies.append(pltpu.make_async_copy(total_ref.at[rows, :], out_ref.at[rows, :], sems.at[p]))
        copies[p].start()
    for copy in copies:
        copy.wait()


def call(kernel, outs, scratch, n_in, limit=4 << 20, far=0, semaphores=(), out_space=pltpu.VMEM):
    return pl.pallas_call(
        kernel,
        out_shape=[jax.ShapeDtypeStruct(shape, F32) for shape in outs],
        in_specs=[pl.BlockSpec(memory_space=pltpu.HBM)] * far + [VM] * (n_in - far),
        out_specs=[pl.BlockSpec(memory_space=out_space)] * len(outs),
        scratch_shapes=[pltpu.VMEM(shape, F32) for shape in scratch] + list(semaphores),
        compiler_params=pltpu.CompilerParams(vmem_limit_bytes=limit),
    )


def far(value):
    return pltpu.with_memory_space_constraint(value, pltpu.HBM)


def swap(value, axis, distance):
    return lax.ppermute(value, axis, [(i, i ^ distance) for i in range(lax.axis_size(axis))])


def swap_odd(value, axis):
    count = lax.axis_size(axis)
    return lax.ppermute(value, axis, [(i, (i + 1 if i % 2 else i - 1) % count) for i in range(count)])


def work(residual, fdm_vectors, fdm_eigen, coarse_basis, x_interior, x_separator):
    levels, unknowns, width = x_separator.shape[3:]
    x = residual.reshape(256, 256)
    vectors = fdm_vectors.reshape(3, 10, 10, 128).transpose(1, 2, 0, 3)
    eigen = fdm_eigen.reshape(3, 10, 1, 128)
    own = x_interior.reshape(unknowns, unknowns)
    sep = x_separator.reshape(levels, unknowns, width)
    level_of = lax.broadcasted_iota(jnp.int32, (16, 128), 0) & 7

    def climb(running, axis, distance, first):
        return running + jnp.where(level_of >= first, swap(running, axis, distance), 0.0)

    core, xs, running, ownsol = call(
        pre_kernel,
        [(8, 8, 8, 128), (32, 128), (16, 128), (16, 128)],
        [(2, 128, 256), (2, 256, 128), (levels, unknowns, width), (8, 8, 8), (unknowns, unknowns)],
        4,
        far=4,
        semaphores=(pltpu.SemaphoreType.DMA((2,)), pltpu.SemaphoreType.DMA((3,))),
    )(far(x), far(sep), far(coarse_basis), far(own))
    xr = swap(xs, "gx", 1)
    ends, za, zb = call(zface_kernel, [(2, 8, 8, 128), (8, 128), (8, 128)], [], 2)(core, xr)
    running = climb(running, "gy", 2, 5)
    za, zb = swap(za, "gz", 1), swap_odd(zb, "gz")
    running = climb(running, "gy", 6, 6)
    (factors,) = call(factors_kernel, [(848, 128)], [], 1)(vectors)
    block = (core, core.reshape(512, 128), ends, ends.reshape(128, 128), za, zb)
    ya, yb = call(yface_kernel, [(56, 128), (56, 128)], [(256, 128)], 6)(*block)
    ya, yb = swap(ya, "gy", 1), swap_odd(yb, "gy")
    running = climb(running, "gz", 4, 2)
    (modes,) = call(
        modes_kernel, [(1696, 128)], [(800, 128), (112, 128), (112, 128), (256, 128)], 9
    )(*block, ya, yb, factors)
    three, twelve, fifteen = (swap(running, "gz", d) for d in (3, 12, 15))
    (modes,) = call(middle_kernel, [(1696, 128)], [(16, 128)], 3)(modes, factors, eigen)
    both = jnp.where(level_of >= 3, three + (twelve + fifteen), three)
    running = running + jnp.where(level_of >= 1, both, 0.0)
    local, edge_l, edge_h, xs = call(
        points_kernel, [(10, 10, 8, 128), (10, 16, 128), (10, 16, 128), (56, 128)], [(1696, 128)], 2
    )(modes, factors)
    xr = swap(xs, "gx", 1)
    ya, yb = call(yfold_send_kernel, [(80, 128), (64, 128)], [], 4)(edge_l, edge_h, xr, running)
    ya, yb = swap(ya, "gy", 1), swap_odd(yb, "gy")
    running = running + jnp.where(level_of >= 4, ya[64:80], 0.0)
    running = climb(running, "gx", 1, 7)
    parts = (local, edge_l, edge_h, xr, ya, yb)
    za, zb = call(zfold_send_kernel, [(24, 128), (8, 128)], [(128, 128)] * 2, 7)(*parts, running)
    za, zb = swap(za, "gz", 1), swap_odd(zb, "gz")
    smooth, tile = call(
        gather_kernel, [(256, 256), (64, 128)], [(128, 128), (128, 128), (2, 256, 128), (8, 8, 8, 128)], 7
    )(*parts, coarse_basis)
    (out,) = call(
        post_kernel, [(256, 256)], [(256, 256)], 7, semaphores=(pltpu.SemaphoreType.DMA((2,)),), out_space=pltpu.HBM
    )(smooth, tile, za, zb, sep, running, ownsol)
    return out.reshape(residual.shape)


def solution(mesh):
    in_specs = (
        P("gx", "gy", "gz"),
        P("gx", "gy", "gz", None, None, None, None),
        P("gx", "gy", "gz", None, None, None),
        P(),
        P("gx", "gy", "gz", None, None),
        P("gx", "gy", "gz", None, None, None),
    )
    return jax.shard_map(work, mesh=mesh, in_specs=in_specs, out_specs=P("gx", "gy", "gz"), check_vma=False)
```

```python
import functools

import jax
import jax.numpy as jnp
from jax import lax
from jax.experimental import pallas as pl
from jax.experimental.pallas import tpu as pltpu
from jax.sharding import PartitionSpec as P


F32 = jnp.float32
VM = pl.BlockSpec(memory_space=pltpu.VMEM)


def iotas(rows=8):
    lane = lax.broadcasted_iota(jnp.int32, (rows, 128), 1)
    sub = lax.broadcasted_iota(jnp.int32, (rows, 128), 0)
    return lane, sub


def roll(value, shift):
    shift = shift % 128
    return value if shift == 0 else pltpu.roll(value, shift, value.ndim - 1)


def row(ref, index, rows=8):
    return jnp.broadcast_to(ref[pl.ds(index, 1), :], (rows, 128))


def total(terms):
    terms = list(terms)
    while len(terms) > 1:
        terms = [a + b for a, b in zip(terms[::2], terms[1::2])] + terms[len(terms) & ~1 :]
    return terms[0]


def chain(pairs):
    acc = None
    for a, b in pairs:
        acc = a * b if acc is None else acc + a * b
    return acc


def pre_kernel(
    x_ref, sep_ref, basis_ref, own_ref, core_ref, xs_ref, run_ref, ownsol_ref, xv, xt, sepv, basisv, ownv, xsem, sems
):
    copies = [pltpu.make_async_copy(x_ref.at[pl.ds(p * 128, 128), :], xv.at[p], xsem.at[p]) for p in range(2)]
    small = [
        pltpu.make_async_copy(a, b, sems.at[n])
        for n, (a, b) in enumerate(((basis_ref, basisv), (own_ref, ownv), (sep_ref, sepv)))
    ]
    for copy in copies + small:
        copy.start()
    gx = lax.axis_index("gx")
    lane, _ = iotas()
    low_q = (lane & 32) == 0
    high_p = lane >= 64
    for p in range(2):
        copies[p].wait()
        xt[p] = xv[p].T
    for pair in range(4):
        k0, k1 = 2 * pair, 2 * pair + 1
        pieces = [xt[p, pl.ds(k, 32, stride=8), :] for p in range(2) for k in (k0, k1)]
        block = jnp.concatenate(pieces, 0).T
        for i in range(8):
            a = block[i * 16 : i * 16 + 8]
            b = block[i * 16 + 8 : i * 16 + 16]
            core_ref[i, k0] = jnp.where(low_q, a, roll(b, 32))
            core_ref[i, k1] = jnp.where(low_q, roll(a, 96), b)

    def outgoing(k):
        return jnp.where(gx == 0, core_ref[7, k], roll(core_ref[0, k], 64))

    for k in range(4):
        xs_ref[k * 8 : k * 8 + 8] = jnp.where(high_p, outgoing(k), roll(outgoing(k + 4), 64))
    small[0].wait()
    sums = []
    for i in range(8):
        weights = basisv[i]
        sums.append(chain((core_ref[i, k], jnp.broadcast_to(weights[:, k : k + 1], (8, 128))) for k in range(8)))
    lanes = jnp.sum(total(sums), axis=0, keepdims=True)
    lane16, sub16 = iotas(16)
    spread = jnp.where(((lane16 & 31) >> 1) == sub16, jnp.broadcast_to(lanes, (16, 128)), 0.0)
    rhs = jnp.sum(spread, axis=1, keepdims=True)
    small[1].wait()
    own = ownv[...]
    coef = jnp.sum(own * rhs, axis=0, keepdims=True)
    ownsol_ref[...] = jnp.broadcast_to(jnp.sum(own * coef, axis=1, keepdims=True), (16, 128))
    small[2].wait()
    for level in range(sep_ref.shape[0]):
        part = jnp.sum(sepv[level] * rhs, axis=0, keepdims=True)
        for h in range(2):
            run_ref[8 * h + level : 8 * h + level + 1, :] = part[:, h * 128 : h * 128 + 128]


def zface_kernel(core_ref, xr_ref, ends_ref, za_ref, zb_ref):
    gx = lax.axis_index("gx")
    even = lax.rem(lax.axis_index("gz"), 2) == 0
    lane, _ = iotas()
    high_p = lane >= 64
    slot = lane & 31
    for k in range(8):
        at = (k % 4) * 8
        got = xr_ref[at : at + 8]
        if k >= 4:
            got = roll(got, 64)
        ends_ref[0, k] = jnp.where(high_p, roll(core_ref[7, k], 64), jnp.where(gx == 1, roll(got, 64), 0.0))
        ends_ref[1, k] = jnp.where(high_p, jnp.where(gx == 0, got, 0.0), roll(core_ref[0, k], 64))
    upper = jnp.zeros((8, 128), F32)
    lower = jnp.zeros((8, 128), F32)
    for i in range(10):
        upper = jnp.where(slot == i, roll(plane(core_ref, ends_ref, i, 7), i - 31), upper)
        lower = jnp.where(slot == i, roll(plane(core_ref, ends_ref, i, 0), i), lower)
    za_ref[...] = jnp.where(even, upper, lower)
    zb_ref[...] = jnp.where(even, lower, upper)


def plane(core_ref, ends_ref, i, k):
    return core_ref[i - 1, k] if 1 <= i <= 8 else ends_ref[i // 9, k]


def sides(a, b, axis):
    index = lax.axis_index(axis)
    even = lax.rem(index, 2) == 0
    above = jnp.where(index == lax.axis_size(axis) - 1, 0.0, jnp.where(even, a, b))
    below = jnp.where(index == 0, 0.0, jnp.where(even, b, a))
    return above, below


def z_halo(core_ref, ends_ref, za_ref, zb_ref, slot):
    from_above, from_below = sides(za_ref[...], zb_ref[...], "gz")
    first, last = [], []
    for i in range(10):
        first.append(jnp.where(slot == 0, roll(from_below, -i), roll(plane(core_ref, ends_ref, i, 7), 1)))
        last.append(jnp.where(slot == 31, roll(from_above, 31 - i), roll(plane(core_ref, ends_ref, i, 0), -1)))
    return first, last


def y_rows(first, last, core2_ref, ends2_ref, scr):
    for i in range(10):
        scr[pl.ds(i * 8, 8), :] = first[i]
        scr[pl.ds(128 + i * 8, 8), :] = last[i]
    low, high = [], []
    for i in range(10):
        ref, at = (core2_ref, (i - 1) * 64) if 1 <= i <= 8 else (ends2_ref, (i // 9) * 64)
        low.append(ref[pl.ds(at, 8, stride=8), :])
        high.append(ref[pl.ds(at + 7, 8, stride=8), :])
    low_ends = [scr[pl.ds(b, 16, stride=8), :] for b in (0, 128)]
    high_ends = [scr[pl.ds(b + 7, 16, stride=8), :] for b in (0, 128)]
    return low, high, low_ends, high_ends


def yface_kernel(core_ref, core2_ref, ends_ref, ends2_ref, za_ref, zb_ref, ya_ref, yb_ref, scr):
    even_y = lax.rem(lax.axis_index("gy"), 2) == 0
    lane, _ = iotas()
    low_q = (lane & 32) == 0
    first, last = z_halo(core_ref, ends_ref, za_ref, zb_ref, lane & 31)
    low, high, low_ends, high_ends = y_rows(first, last, core2_ref, ends2_ref, scr)
    for i in range(5):
        down = jnp.where(low_q, low[i], roll(low[i + 5], 32))
        up = jnp.where(low_q, roll(high[i + 5], 96), high[i])
        ya_ref[i * 8 : i * 8 + 8] = jnp.where(even_y, up, down)
        yb_ref[i * 8 : i * 8 + 8] = jnp.where(even_y, down, up)
    low_q = (iotas(16)[0] & 32) == 0
    down = jnp.where(low_q, low_ends[0], roll(low_ends[1], 32))
    up = jnp.where(low_q, roll(high_ends[1], 96), high_ends[0])
    ya_ref[40:56] = jnp.where(even_y, up, down)
    yb_ref[40:56] = jnp.where(even_y, down, up)


def factors_kernel(vec_ref, s_ref):
    for a in range(10):
        for i in range(10):
            s_ref[(i * 10 + a) * 8 : (i * 10 + a) * 8 + 3] = vec_ref[i, a].astype(F32)


def factor_of(s):
    return lambda d, i, a: row(s, (i * 10 + a) * 8 + d)


def along_x(source, target, factor, transposed):
    def step(k, _):
        for h in range(2):
            at = k * 16 + 8 * h
            held = [source[pl.ds(i * 160 + at, 8), :] for i in range(10)]
            for a in range(10):
                target[pl.ds(a * 160 + at, 8), :] = chain(
                    (factor(0, a, i) if transposed else factor(0, i, a), held[i]) for i in range(10)
                )
        return 0

    lax.fori_loop(0, 10, step, 0)


def y_factors(s):
    return [[s[pl.ds((j * 10 + 8 * h) * 8 + 1, 8, stride=8), :] for j in range(10)] for h in range(2)]


def front_kernel(core_ref, ends_ref, za_ref, zb_ref, s, u, edge_ref, block):
    lane, _ = iotas()
    first, last = z_halo(core_ref, ends_ref, za_ref, zb_ref, lane & 31)
    for i in range(10):
        block[pl.ds(i * 80, 8), :] = first[i]
        block[pl.ds(i * 80 + 72, 8), :] = last[i]
        for k in range(8):
            block[pl.ds(i * 80 + 8 + k * 8, 8), :] = plane(core_ref, ends_ref, i, k)
    for i in range(10):
        edge_ref[i * 16 : i * 16 + 16] = roll(block[pl.ds(i * 80 + 7, 16, stride=8), :], 32)
        edge_ref[160 + i * 16 : 176 + i * 16] = roll(block[pl.ds(i * 80, 16, stride=8), :], 96)
    factor = factor_of(s)
    front = y_factors(s)

    def along(k, _):
        held = [block[pl.ds(i * 80 + k * 8, 8), :] for i in range(10)]
        for a in range(10):
            block[pl.ds(a * 80 + k * 8, 8), :] = chain((factor(0, i, a), held[i]) for i in range(10))
        return 0

    lax.fori_loop(0, 10, along, 0)

    def own_rows(a, _):
        for k in range(10):
            at = (a * 10 + k) * 8
            rows = [row(block, at + j) for j in range(8)]
            for h in range(2):
                u[pl.ds(at * 2 + 8 * h, 8), :] = chain((front[h][j + 1], rows[j]) for j in range(8))
        return 0

    lax.fori_loop(0, 10, own_rows, 0)


def modes_kernel(u_ref, edge_ref, ya_ref, yb_ref, s, u, rows):
    low_q = (iotas(16)[0] & 32) == 0
    ends_above, ends_below = sides(ya_ref[40:56], yb_ref[40:56], "gy")
    for i in range(10):
        at = (i % 5) * 8
        above, below = sides(ya_ref[at : at + 8], yb_ref[at : at + 8], "gy")
        if i < 5:
            above, below = roll(above, 32), roll(below, 96)
        for base, middle, zero, nine in (
            (0, below, roll(ends_below, 96), ends_below),
            (160, above, roll(ends_above, 32), ends_above),
        ):
            rows[base + i * 16 + 1 : base + i * 16 + 9] = middle
            rows[base + i * 16 : base + i * 16 + 1] = zero[i : i + 1]
            rows[base + i * 16 + 9 : base + i * 16 + 10] = nine[i : i + 1]
    low = [jnp.where(low_q, rows[i * 16 : i * 16 + 16], edge_ref[i * 16 : i * 16 + 16]) for i in range(10)]
    high = [
        jnp.where(low_q, edge_ref[160 + i * 16 : 176 + i * 16], rows[160 + i * 16 : 176 + i * 16]) for i in range(10)
    ]
    front = y_factors(s)
    for a in range(10):
        weights = [row(s, (i * 10 + a) * 8, 16) for i in range(10)]
        rows[320 + a * 16 : 336 + a * 16] = chain((weights[i], low[i]) for i in range(10))
        rows[480 + a * 16 : 496 + a * 16] = chain((weights[i], high[i]) for i in range(10))

    def add_edges(a, _):
        for k in range(10):
            before, after = row(rows, 320 + a * 16 + k), row(rows, 480 + a * 16 + k)
            for h in range(2):
                at = (a * 10 + k) * 16 + 8 * h
                u[pl.ds(at, 8), :] = u_ref[pl.ds(at, 8), :] + (front[h][0] * before + front[h][9] * after)
        return 0

    lax.fori_loop(0, 10, add_edges, 0)


def middle_kernel(u_ref, s, eig_ref, u, eg):
    eg[...] = jnp.ones((16, 128), F32)
    for a in range(10):
        eg[a : a + 1] = eig_ref[1, a]
    factor = factor_of(s)

    def wide(value):
        return jnp.broadcast_to(value, (8, 128))

    def along_z(a, _):
        for h in range(2):
            at = a * 160 + 8 * h
            held = [u_ref[pl.ds(at + k * 16, 8), :] for k in range(10)]
            base = wide(eig_ref[0, a]) + eg[8 * h : 8 * h + 8]
            modes = []
            for c in range(10):
                modes.append(chain((factor(2, k, c), held[k]) for k in range(10)) / (base + wide(eig_ref[2, c])))
            for k in range(10):
                u[pl.ds(at + k * 16, 8), :] = chain((factor(2, k, c), modes[c]) for c in range(10))
        return 0

    lax.fori_loop(0, 10, along_z, 0)


def points_kernel(u_ref, s, l_ref, hl_ref, hh_ref, xs_ref, u):
    gx = lax.axis_index("gx")
    lane, _ = iotas()
    factor = factor_of(s)
    along_x(u_ref, u, factor, True)
    back = [s[pl.ds((10 + b) * 8 + 1, 8, stride=80), :] for b in range(10)]

    def back_y(i, _):
        for k in range(10):
            at = (i * 10 + k) * 16
            l_ref[i, k] = chain((back[b], row(u, at + b)) for b in range(10))
        for h in range(2):
            cut = [u[pl.ds(i * 160 + 128 * h + b, 8, stride=16), :] for b in range(10)]
            hl_ref[i, 8 * h : 8 * h + 8] = chain((factor(1, 0, b), cut[b]) for b in range(10))
            hh_ref[i, 8 * h : 8 * h + 8] = chain((factor(1, 9, b), cut[b]) for b in range(10))
        return 0

    lax.fori_loop(0, 10, back_y, 0)
    high_p = lane >= 64

    def outgoing(ref, k):
        return jnp.where(gx == 0, ref[9, k], roll(ref[0, k], 64))

    for k in range(5):
        xs_ref[k * 8 : k * 8 + 8] = jnp.where(high_p, outgoing(l_ref, k), roll(outgoing(l_ref, k + 5), 64))
    high_p = iotas(16)[0] >= 64
    edge_l = jnp.where(gx == 0, hl_ref[9], roll(hl_ref[0], 64))
    edge_h = jnp.where(gx == 0, hh_ref[9], roll(hh_ref[0], 64))
    xs_ref[40:56] = jnp.where(high_p, edge_l, roll(edge_h, 64))


def fold_x(value, i, opposite, received, gx, high_p):
    if i == 8:
        return value + jnp.where(high_p, jnp.where(gx == 0, received, 0.0), roll(opposite, 64))
    if i == 1:
        return value + jnp.where(high_p, roll(opposite, 64), jnp.where(gx == 1, roll(received, 64), 0.0))
    return value


def edge_rows(hl_ref, hh_ref, xr_ref, gx):
    high_p = iotas(16)[0] >= 64
    packed = xr_ref[40:56]
    low, high = [], []
    for i in range(1, 9):
        j = {1: 9, 8: 0}.get(i, i)
        low.append(fold_x(hl_ref[i], i, hl_ref[j], packed, gx, high_p))
        high.append(fold_x(hh_ref[i], i, hh_ref[j], roll(packed, 64), gx, high_p))
    return low, high


def yfold_send_kernel(hl_ref, hh_ref, xr_ref, run_ref, ya_ref, yb_ref):
    ya_ref[64:80] = run_ref[...]
    gx = lax.axis_index("gx")
    even_y = lax.rem(lax.axis_index("gy"), 2) == 0
    low_q = (iotas(16)[0] & 32) == 0
    low, high = edge_rows(hl_ref, hh_ref, xr_ref, gx)
    for i in range(4):
        down = jnp.where(low_q, low[i], roll(low[i + 4], 32))
        up = jnp.where(low_q, roll(high[i + 4], 96), high[i])
        ya_ref[i * 16 : i * 16 + 16] = jnp.where(even_y, up, down)
        yb_ref[i * 16 : i * 16 + 16] = jnp.where(even_y, down, up)


def fold_rows(hl_ref, hh_ref, xr_ref, ya_ref, yb_ref, rows_first, rows_last, gx):
    low_q = (iotas(16)[0] & 32) == 0
    low, high = edge_rows(hl_ref, hh_ref, xr_ref, gx)
    for i in range(8):
        at = (i % 4) * 16
        above, below = sides(ya_ref[at : at + 16], yb_ref[at : at + 16], "gy")
        if i < 4:
            above, below = roll(above, 32), roll(below, 96)
        rows_last[pl.ds(i * 16, 16), :] = jnp.where(low_q, roll(low[i], 96), above)
        rows_first[pl.ds(i * 16, 16), :] = jnp.where(low_q, below, roll(high[i], 32))


def folded_xy(l_ref, xr_ref, rows_first, rows_last, i, k, gx, lane, sub):
    high_p = lane >= 64
    value = l_ref[i, k]
    if i in (1, 8):
        packed = xr_ref[(k % 5) * 8 : (k % 5) * 8 + 8]
        received = packed if k < 5 else roll(packed, 64)
        value = fold_x(value, i, l_ref[9 if i == 1 else 0, k], received, gx, high_p)
    at = (i - 1) * 16 + k
    return value + jnp.where(sub == 0, row(rows_first, at), jnp.where(sub == 7, row(rows_last, at), 0.0))


def zfold_send_kernel(l_ref, hl_ref, hh_ref, xr_ref, ya_ref, yb_ref, run_ref, za_ref, zb_ref, rows_first, rows_last):
    za_ref[8:24] = run_ref[...]
    gx = lax.axis_index("gx")
    even_z = lax.rem(lax.axis_index("gz"), 2) == 0
    lane, sub = iotas()
    slot = lane & 31
    fold_rows(hl_ref, hh_ref, xr_ref, ya_ref, yb_ref, rows_first, rows_last, gx)
    down = jnp.zeros((8, 128), F32)
    up = jnp.zeros((8, 128), F32)
    for i in range(8):
        down = jnp.where(slot == i, roll(folded_xy(l_ref, xr_ref, rows_first, rows_last, i + 1, 0, gx, lane, sub), i), down)
        up = jnp.where(slot == i, roll(folded_xy(l_ref, xr_ref, rows_first, rows_last, i + 1, 9, gx, lane, sub), i - 31), up)
    za_ref[:8] = jnp.where(even_z, up, down)
    zb_ref[...] = jnp.where(even_z, down, up)


def gather_kernel(
    l_ref, hl_ref, hh_ref, xr_ref, ya_ref, yb_ref, basis_ref, sum_ref, tile_ref, rows_first, rows_last, xt, grid
):
    gx = lax.axis_index("gx")
    lane, sub = iotas()
    slot = lane & 31
    low_q = (lane & 32) == 0
    fold_rows(hl_ref, hh_ref, xr_ref, ya_ref, yb_ref, rows_first, rows_last, gx)
    for i in range(8):
        get = functools.partial(folded_xy, l_ref, xr_ref, rows_first, rows_last, i + 1, gx=gx, lane=lane, sub=sub)
        before, after = get(0), get(9)
        for k in range(8):
            value = get(k + 1)
            if k == 0:
                value = value + jnp.where(slot == 0, 0.0, roll(after, 1))
            if k == 7:
                value = value + jnp.where(slot == 31, 0.0, roll(before, -1))
            grid[i, k] = value
        weights = jnp.concatenate([basis_ref[i]] * 16, 1)
        tile_ref[i * 8 : i * 8 + 8] = weights
    for pair in range(4):
        k0, k1 = 2 * pair, 2 * pair + 1
        pieces = []
        for i in range(8):
            c0, c1 = grid[i, k0], grid[i, k1]
            pieces.append(jnp.where(low_q, c0, roll(c1, 32)))
            pieces.append(jnp.where(low_q, roll(c0, 96), c1))
        block = jnp.concatenate(pieces, 0).T
        for p in range(2):
            for t, k in enumerate((k0, k1)):
                at = p * 64 + t * 32
                xt[p, pl.ds(k, 32, stride=8), :] = block[at : at + 32]
    sum_ref[...] = jnp.concatenate([xt[0], xt[1]], 1).T


def post_kernel(sum_ref, tile_ref, za_ref, zb_ref, sep_ref, run_ref, ownsol_ref, out_ref, total_ref, sems):
    lane, _ = iotas()
    running = run_ref[...] + za_ref[8:24]
    weighted = total(
        sep_ref[level][:, h * 128 : h * 128 + 128] * running[8 * h + level : 8 * h + level + 1, :]
        for h in range(2)
        for level in range(sep_ref.shape[0])
    )
    solution_col = ownsol_ref[:, :1] + jnp.sum(weighted, axis=1, keepdims=True)
    lane16, sub16 = iotas(16)
    along_z = []
    for t in range(2):
        spread = jnp.where((lane16 >> 4) + 8 * t == sub16, jnp.broadcast_to(solution_col, (16, 128)), 0.0)
        along_z.append(jnp.broadcast_to(jnp.sum(spread, axis=0, keepdims=True), (8, 128)))
    from_above, from_below = sides(za_ref[:8], zb_ref[...], "gz")
    copies = []
    for p in range(2):
        for i in range(8):
            weights = tile_ref[i * 8 : i * 8 + 8]
            low, high = weights * along_z[0], weights * along_z[1]
            for q in range(2):
                at = ((p * 8 + i) * 2 + q) * 8
                source = p * 64 + q * 32 + i
                first = sum_ref[at : at + 8, :128] + low
                last = sum_ref[at : at + 8, 128:] + high
                total_ref[at : at + 8, :128] = first + jnp.where(lane == 0, roll(from_below, -source), 0.0)
                total_ref[at : at + 8, 128:] = last + jnp.where(lane == 127, roll(from_above, 127 - source), 0.0)
        rows = pl.ds(p * 128, 128)
        copies.append(pltpu.make_async_copy(total_ref.at[rows, :], out_ref.at[rows, :], sems.at[p]))
        copies[p].start()
    for copy in copies:
        copy.wait()


def call(kernel, outs, scratch, n_in, limit=4 << 20, far=0, semaphores=(), out_space=pltpu.VMEM):
    return pl.pallas_call(
        kernel,
        out_shape=[jax.ShapeDtypeStruct(shape, F32) for shape in outs],
        in_specs=[pl.BlockSpec(memory_space=pltpu.HBM)] * far + [VM] * (n_in - far),
        out_specs=[pl.BlockSpec(memory_space=out_space)] * len(outs),
        scratch_shapes=[pltpu.VMEM(shape, F32) for shape in scratch] + list(semaphores),
        compiler_params=pltpu.CompilerParams(vmem_limit_bytes=limit),
    )


def far(value):
    return pltpu.with_memory_space_constraint(value, pltpu.HBM)


def swap(value, axis, distance):
    return lax.ppermute(value, axis, [(i, i ^ distance) for i in range(lax.axis_size(axis))])


def swap_odd(value, axis):
    count = lax.axis_size(axis)
    return lax.ppermute(value, axis, [(i, (i + 1 if i % 2 else i - 1) % count) for i in range(count)])


def work(residual, fdm_vectors, fdm_eigen, coarse_basis, x_interior, x_separator):
    levels, unknowns, width = x_separator.shape[3:]
    x = residual.reshape(256, 256)
    vectors = fdm_vectors.reshape(3, 10, 10, 128).transpose(1, 2, 0, 3)
    eigen = fdm_eigen.reshape(3, 10, 1, 128)
    own = x_interior.reshape(unknowns, unknowns)
    sep = x_separator.reshape(levels, unknowns, width)
    level_of = lax.broadcasted_iota(jnp.int32, (16, 128), 0) & 7

    def climb(running, axis, distance, first):
        return running + jnp.where(level_of >= first, swap(running, axis, distance), 0.0)

    core, xs, running, ownsol = call(
        pre_kernel,
        [(8, 8, 8, 128), (32, 128), (16, 128), (16, 128)],
        [(2, 128, 256), (2, 256, 128), (levels, unknowns, width), (8, 8, 8), (unknowns, unknowns)],
        4,
        far=4,
        semaphores=(pltpu.SemaphoreType.DMA((2,)), pltpu.SemaphoreType.DMA((3,))),
    )(far(x), far(sep), far(coarse_basis), far(own))
    xr = swap(xs, "gx", 1)
    ends, za, zb = call(zface_kernel, [(2, 8, 8, 128), (8, 128), (8, 128)], [], 2)(core, xr)
    running = climb(running, "gy", 2, 5)
    za, zb = swap(za, "gz", 1), swap_odd(zb, "gz")
    running = climb(running, "gy", 6, 6)
    (factors,) = call(factors_kernel, [(848, 128)], [], 1)(vectors)
    block = (core, core.reshape(512, 128), ends, ends.reshape(128, 128), za, zb)
    ya, yb = call(yface_kernel, [(56, 128), (56, 128)], [(256, 128)], 6)(*block)
    ya, yb = swap(ya, "gy", 1), swap_odd(yb, "gy")
    running = climb(running, "gz", 4, 2)
    modes, edges = call(front_kernel, [(1696, 128), (320, 128)], [(848, 128)], 5)(core, ends, *block[4:], factors)
    (modes,) = call(modes_kernel, [(1696, 128)], [(640, 128)], 5)(modes, edges, ya, yb, factors)
    running = climb(running, "gz", 12, 3)
    (modes,) = call(middle_kernel, [(1696, 128)], [(16, 128)], 3)(modes, factors, eigen)
    running = climb(running, "gz", 3, 1)
    local, edge_l, edge_h, xs = call(
        points_kernel, [(10, 10, 8, 128), (10, 16, 128), (10, 16, 128), (56, 128)], [(1696, 128)], 2
    )(modes, factors)
    xr = swap(xs, "gx", 1)
    ya, yb = call(yfold_send_kernel, [(80, 128), (64, 128)], [], 4)(edge_l, edge_h, xr, running)
    ya, yb = swap(ya, "gy", 1), swap_odd(yb, "gy")
    running = running + jnp.where(level_of >= 4, ya[64:80], 0.0)
    running = climb(running, "gx", 1, 7)
    parts = (local, edge_l, edge_h, xr, ya, yb)
    za, zb = call(zfold_send_kernel, [(24, 128), (8, 128)], [(128, 128)] * 2, 7)(*parts, running)
    za, zb = swap(za, "gz", 1), swap_odd(zb, "gz")
    smooth, tile = call(
        gather_kernel, [(256, 256), (64, 128)], [(128, 128), (128, 128), (2, 256, 128), (8, 8, 8, 128)], 7
    )(*parts, coarse_basis)
    (out,) = call(
        post_kernel, [(256, 256)], [(256, 256)], 7, semaphores=(pltpu.SemaphoreType.DMA((2,)),), out_space=pltpu.HBM
    )(smooth, tile, za, zb, sep, running, ownsol)
    return out.reshape(residual.shape)


def solution(mesh):
    in_specs = (
        P("gx", "gy", "gz"),
        P("gx", "gy", "gz", None, None, None, None),
        P("gx", "gy", "gz", None, None, None),
        P(),
        P("gx", "gy", "gz", None, None),
        P("gx", "gy", "gz", None, None, None),
    )
    return jax.shard_map(work, mesh=mesh, in_specs=in_specs, out_specs=P("gx", "gy", "gz"), check_vma=False)
```

```python
import functools

import jax
import jax.numpy as jnp
from jax import lax
from jax.experimental import pallas as pl
from jax.experimental.pallas import tpu as pltpu
from jax.sharding import PartitionSpec as P


F32 = jnp.float32
VM = pl.BlockSpec(memory_space=pltpu.VMEM)


def iotas(rows=8):
    lane = lax.broadcasted_iota(jnp.int32, (rows, 128), 1)
    sub = lax.broadcasted_iota(jnp.int32, (rows, 128), 0)
    return lane, sub


def roll(value, shift):
    shift = shift % 128
    return value if shift == 0 else pltpu.roll(value, shift, value.ndim - 1)


def row(ref, index, rows=8):
    return jnp.broadcast_to(ref[pl.ds(index, 1), :], (rows, 128))


def total(terms):
    terms = list(terms)
    while len(terms) > 1:
        terms = [a + b for a, b in zip(terms[::2], terms[1::2])] + terms[len(terms) & ~1 :]
    return terms[0]


def chain(pairs):
    acc = None
    for a, b in pairs:
        acc = a * b if acc is None else acc + a * b
    return acc


def pre_kernel(
    x_ref, sep_ref, basis_ref, own_ref, core_ref, xs_ref, run_ref, ownsol_ref, xv, xt, sepv, basisv, ownv, xsem, sems
):
    copies = [pltpu.make_async_copy(x_ref.at[pl.ds(p * 128, 128), :], xv.at[p], xsem.at[p]) for p in range(2)]
    small = [
        pltpu.make_async_copy(a, b, sems.at[n])
        for n, (a, b) in enumerate(((basis_ref, basisv), (own_ref, ownv), (sep_ref, sepv)))
    ]
    for copy in copies + small:
        copy.start()
    gx = lax.axis_index("gx")
    lane, _ = iotas()
    low_q = (lane & 32) == 0
    high_p = lane >= 64
    for p in range(2):
        copies[p].wait()
        xt[p] = xv[p].T
    for pair in range(4):
        k0, k1 = 2 * pair, 2 * pair + 1
        pieces = [xt[p, pl.ds(k, 32, stride=8), :] for p in range(2) for k in (k0, k1)]
        block = jnp.concatenate(pieces, 0).T
        for i in range(8):
            a = block[i * 16 : i * 16 + 8]
            b = block[i * 16 + 8 : i * 16 + 16]
            core_ref[i, k0] = jnp.where(low_q, a, roll(b, 32))
            core_ref[i, k1] = jnp.where(low_q, roll(a, 96), b)

    def outgoing(k):
        return jnp.where(gx == 0, core_ref[7, k], roll(core_ref[0, k], 64))

    for k in range(4):
        xs_ref[k * 8 : k * 8 + 8] = jnp.where(high_p, outgoing(k), roll(outgoing(k + 4), 64))
    small[0].wait()
    sums = []
    for i in range(8):
        weights = basisv[i]
        sums.append(chain((core_ref[i, k], jnp.broadcast_to(weights[:, k : k + 1], (8, 128))) for k in range(8)))
    lanes = jnp.sum(total(sums), axis=0, keepdims=True)
    lane16, sub16 = iotas(16)
    spread = jnp.where(((lane16 & 31) >> 1) == sub16, jnp.broadcast_to(lanes, (16, 128)), 0.0)
    rhs = jnp.sum(spread, axis=1, keepdims=True)
    small[1].wait()
    own = ownv[...]
    coef = jnp.sum(own * rhs, axis=0, keepdims=True)
    ownsol_ref[...] = jnp.broadcast_to(jnp.sum(own * coef, axis=1, keepdims=True), (16, 128))
    small[2].wait()
    for level in range(sep_ref.shape[0]):
        part = jnp.sum(sepv[level] * rhs, axis=0, keepdims=True)
        for h in range(2):
            run_ref[8 * h + level : 8 * h + level + 1, :] = part[:, h * 128 : h * 128 + 128]


def zface_kernel(core_ref, xr_ref, ends_ref, za_ref, zb_ref):
    gx = lax.axis_index("gx")
    even = lax.rem(lax.axis_index("gz"), 2) == 0
    lane, _ = iotas()
    high_p = lane >= 64
    slot = lane & 31
    for k in range(8):
        at = (k % 4) * 8
        got = xr_ref[at : at + 8]
        if k >= 4:
            got = roll(got, 64)
        ends_ref[0, k] = jnp.where(high_p, roll(core_ref[7, k], 64), jnp.where(gx == 1, roll(got, 64), 0.0))
        ends_ref[1, k] = jnp.where(high_p, jnp.where(gx == 0, got, 0.0), roll(core_ref[0, k], 64))
    upper = jnp.zeros((8, 128), F32)
    lower = jnp.zeros((8, 128), F32)
    for i in range(10):
        upper = jnp.where(slot == i, roll(plane(core_ref, ends_ref, i, 7), i - 31), upper)
        lower = jnp.where(slot == i, roll(plane(core_ref, ends_ref, i, 0), i), lower)
    za_ref[...] = jnp.where(even, upper, lower)
    zb_ref[...] = jnp.where(even, lower, upper)


def plane(core_ref, ends_ref, i, k):
    return core_ref[i - 1, k] if 1 <= i <= 8 else ends_ref[i // 9, k]


def sides(a, b, axis):
    index = lax.axis_index(axis)
    even = lax.rem(index, 2) == 0
    above = jnp.where(index == lax.axis_size(axis) - 1, 0.0, jnp.where(even, a, b))
    below = jnp.where(index == 0, 0.0, jnp.where(even, b, a))
    return above, below


def z_halo(core_ref, ends_ref, za_ref, zb_ref, slot):
    from_above, from_below = sides(za_ref[...], zb_ref[...], "gz")
    first, last = [], []
    for i in range(10):
        first.append(jnp.where(slot == 0, roll(from_below, -i), roll(plane(core_ref, ends_ref, i, 7), 1)))
        last.append(jnp.where(slot == 31, roll(from_above, 31 - i), roll(plane(core_ref, ends_ref, i, 0), -1)))
    return first, last


def y_rows(first, last, core2_ref, ends2_ref, scr):
    for i in range(10):
        scr[pl.ds(i * 8, 8), :] = first[i]
        scr[pl.ds(128 + i * 8, 8), :] = last[i]
    low, high = [], []
    for i in range(10):
        ref, at = (core2_ref, (i - 1) * 64) if 1 <= i <= 8 else (ends2_ref, (i // 9) * 64)
        low.append(ref[pl.ds(at, 8, stride=8), :])
        high.append(ref[pl.ds(at + 7, 8, stride=8), :])
    low_ends = [scr[pl.ds(b, 16, stride=8), :] for b in (0, 128)]
    high_ends = [scr[pl.ds(b + 7, 16, stride=8), :] for b in (0, 128)]
    return low, high, low_ends, high_ends


def yface_kernel(core_ref, core2_ref, ends_ref, ends2_ref, za_ref, zb_ref, ya_ref, yb_ref, scr):
    even_y = lax.rem(lax.axis_index("gy"), 2) == 0
    lane, _ = iotas()
    low_q = (lane & 32) == 0
    first, last = z_halo(core_ref, ends_ref, za_ref, zb_ref, lane & 31)
    low, high, low_ends, high_ends = y_rows(first, last, core2_ref, ends2_ref, scr)
    for i in range(5):
        down = jnp.where(low_q, low[i], roll(low[i + 5], 32))
        up = jnp.where(low_q, roll(high[i + 5], 96), high[i])
        ya_ref[i * 8 : i * 8 + 8] = jnp.where(even_y, up, down)
        yb_ref[i * 8 : i * 8 + 8] = jnp.where(even_y, down, up)
    low_q = (iotas(16)[0] & 32) == 0
    down = jnp.where(low_q, low_ends[0], roll(low_ends[1], 32))
    up = jnp.where(low_q, roll(high_ends[1], 96), high_ends[0])
    ya_ref[40:56] = jnp.where(even_y, up, down)
    yb_ref[40:56] = jnp.where(even_y, down, up)


def factors_kernel(vec_ref, s_ref):
    for a in range(10):
        for i in range(10):
            s_ref[(i * 10 + a) * 8 : (i * 10 + a) * 8 + 3] = vec_ref[i, a].astype(F32)


def factor_of(s):
    return lambda d, i, a: row(s, (i * 10 + a) * 8 + d)


def along_x(source, target, factor, transposed):
    def step(k, _):
        for h in range(2):
            at = k * 16 + 8 * h
            held = [source[pl.ds(i * 160 + at, 8), :] for i in range(10)]
            for a in range(10):
                target[pl.ds(a * 160 + at, 8), :] = chain(
                    (factor(0, a, i) if transposed else factor(0, i, a), held[i]) for i in range(10)
                )
        return 0

    lax.fori_loop(0, 10, step, 0)


def y_factors(s):
    return [[s[pl.ds((j * 10 + 8 * h) * 8 + 1, 8, stride=8), :] for j in range(10)] for h in range(2)]


def front_kernel(core_ref, ends_ref, za_ref, zb_ref, s, u, edge_ref, block):
    lane, _ = iotas()
    first, last = z_halo(core_ref, ends_ref, za_ref, zb_ref, lane & 31)
    for i in range(10):
        block[pl.ds(i * 80, 8), :] = first[i]
        block[pl.ds(i * 80 + 72, 8), :] = last[i]
        for k in range(8):
            block[pl.ds(i * 80 + 8 + k * 8, 8), :] = plane(core_ref, ends_ref, i, k)
    for i in range(10):
        edge_ref[i * 16 : i * 16 + 16] = roll(block[pl.ds(i * 80 + 7, 16, stride=8), :], 32)
        edge_ref[160 + i * 16 : 176 + i * 16] = roll(block[pl.ds(i * 80, 16, stride=8), :], 96)
    factor = factor_of(s)
    front = y_factors(s)

    def along(k, _):
        held = [block[pl.ds(i * 80 + k * 8, 8), :] for i in range(10)]
        for a in range(10):
            block[pl.ds(a * 80 + k * 8, 8), :] = chain((factor(0, i, a), held[i]) for i in range(10))
        return 0

    lax.fori_loop(0, 10, along, 0)

    def own_rows(a, _):
        for k in range(10):
            at = (a * 10 + k) * 8
            rows = [row(block, at + j) for j in range(8)]
            for h in range(2):
                u[pl.ds(at * 2 + 8 * h, 8), :] = chain((front[h][j + 1], rows[j]) for j in range(8))
        return 0

    lax.fori_loop(0, 10, own_rows, 0)


def modes_kernel(u_ref, edge_ref, ya_ref, yb_ref, s, u, rows):
    low_q = (iotas(16)[0] & 32) == 0
    ends_above, ends_below = sides(ya_ref[40:56], yb_ref[40:56], "gy")
    for i in range(10):
        at = (i % 5) * 8
        above, below = sides(ya_ref[at : at + 8], yb_ref[at : at + 8], "gy")
        if i < 5:
            above, below = roll(above, 32), roll(below, 96)
        for base, middle, zero, nine in (
            (0, below, roll(ends_below, 96), ends_below),
            (160, above, roll(ends_above, 32), ends_above),
        ):
            rows[base + i * 16 + 1 : base + i * 16 + 9] = middle
            rows[base + i * 16 : base + i * 16 + 1] = zero[i : i + 1]
            rows[base + i * 16 + 9 : base + i * 16 + 10] = nine[i : i + 1]
    low = [jnp.where(low_q, rows[i * 16 : i * 16 + 16], edge_ref[i * 16 : i * 16 + 16]) for i in range(10)]
    high = [
        jnp.where(low_q, edge_ref[160 + i * 16 : 176 + i * 16], rows[160 + i * 16 : 176 + i * 16]) for i in range(10)
    ]
    front = y_factors(s)
    for a in range(10):
        weights = [row(s, (i * 10 + a) * 8, 16) for i in range(10)]
        rows[320 + a * 16 : 336 + a * 16] = chain((weights[i], low[i]) for i in range(10))
        rows[480 + a * 16 : 496 + a * 16] = chain((weights[i], high[i]) for i in range(10))

    def add_edges(a, _):
        for k in range(10):
            before, after = row(rows, 320 + a * 16 + k), row(rows, 480 + a * 16 + k)
            for h in range(2):
                at = (a * 10 + k) * 16 + 8 * h
                u[pl.ds(at, 8), :] = u_ref[pl.ds(at, 8), :] + (front[h][0] * before + front[h][9] * after)
        return 0

    lax.fori_loop(0, 10, add_edges, 0)


def middle_kernel(u_ref, s, eig_ref, u, eg):
    eg[...] = jnp.ones((16, 128), F32)
    for a in range(10):
        eg[a : a + 1] = eig_ref[1, a]
    factor = factor_of(s)

    def wide(value):
        return jnp.broadcast_to(value, (8, 128))

    def along_z(a, _):
        for h in range(2):
            at = a * 160 + 8 * h
            held = [u_ref[pl.ds(at + k * 16, 8), :] for k in range(10)]
            base = wide(eig_ref[0, a]) + eg[8 * h : 8 * h + 8]
            modes = []
            for c in range(10):
                modes.append(chain((factor(2, k, c), held[k]) for k in range(10)) / (base + wide(eig_ref[2, c])))
            for k in range(10):
                u[pl.ds(at + k * 16, 8), :] = chain((factor(2, k, c), modes[c]) for c in range(10))
        return 0

    lax.fori_loop(0, 10, along_z, 0)


def points_kernel(u_ref, s, l_ref, hl_ref, hh_ref, xs_ref, u):
    gx = lax.axis_index("gx")
    lane, _ = iotas()
    factor = factor_of(s)
    along_x(u_ref, u, factor, True)
    back = [s[pl.ds((10 + b) * 8 + 1, 8, stride=80), :] for b in range(10)]

    def back_y(i, _):
        for k in range(10):
            at = (i * 10 + k) * 16
            l_ref[i, k] = chain((back[b], row(u, at + b)) for b in range(10))
        for h in range(2):
            cut = [u[pl.ds(i * 160 + 128 * h + b, 8, stride=16), :] for b in range(10)]
            hl_ref[i, 8 * h : 8 * h + 8] = chain((factor(1, 0, b), cut[b]) for b in range(10))
            hh_ref[i, 8 * h : 8 * h + 8] = chain((factor(1, 9, b), cut[b]) for b in range(10))
        return 0

    lax.fori_loop(0, 10, back_y, 0)
    high_p = lane >= 64

    def outgoing(ref, k):
        return jnp.where(gx == 0, ref[9, k], roll(ref[0, k], 64))

    for k in range(5):
        xs_ref[k * 8 : k * 8 + 8] = jnp.where(high_p, outgoing(l_ref, k), roll(outgoing(l_ref, k + 5), 64))
    high_p = iotas(16)[0] >= 64
    edge_l = jnp.where(gx == 0, hl_ref[9], roll(hl_ref[0], 64))
    edge_h = jnp.where(gx == 0, hh_ref[9], roll(hh_ref[0], 64))
    xs_ref[40:56] = jnp.where(high_p, edge_l, roll(edge_h, 64))


def fold_x(value, i, opposite, received, gx, high_p):
    if i == 8:
        return value + jnp.where(high_p, jnp.where(gx == 0, received, 0.0), roll(opposite, 64))
    if i == 1:
        return value + jnp.where(high_p, roll(opposite, 64), jnp.where(gx == 1, roll(received, 64), 0.0))
    return value


def edge_rows(hl_ref, hh_ref, xr_ref, gx):
    high_p = iotas(16)[0] >= 64
    packed = xr_ref[40:56]
    low, high = [], []
    for i in range(1, 9):
        j = {1: 9, 8: 0}.get(i, i)
        low.append(fold_x(hl_ref[i], i, hl_ref[j], packed, gx, high_p))
        high.append(fold_x(hh_ref[i], i, hh_ref[j], roll(packed, 64), gx, high_p))
    return low, high


def yfold_send_kernel(hl_ref, hh_ref, xr_ref, run_ref, ya_ref, yb_ref):
    ya_ref[64:80] = run_ref[...]
    gx = lax.axis_index("gx")
    even_y = lax.rem(lax.axis_index("gy"), 2) == 0
    low_q = (iotas(16)[0] & 32) == 0
    low, high = edge_rows(hl_ref, hh_ref, xr_ref, gx)
    for i in range(4):
        down = jnp.where(low_q, low[i], roll(low[i + 4], 32))
        up = jnp.where(low_q, roll(high[i + 4], 96), high[i])
        ya_ref[i * 16 : i * 16 + 16] = jnp.where(even_y, up, down)
        yb_ref[i * 16 : i * 16 + 16] = jnp.where(even_y, down, up)


def fold_rows(hl_ref, hh_ref, xr_ref, ya_ref, yb_ref, rows_first, rows_last, gx):
    low_q = (iotas(16)[0] & 32) == 0
    low, high = edge_rows(hl_ref, hh_ref, xr_ref, gx)
    for i in range(8):
        at = (i % 4) * 16
        above, below = sides(ya_ref[at : at + 16], yb_ref[at : at + 16], "gy")
        if i < 4:
            above, below = roll(above, 32), roll(below, 96)
        rows_last[pl.ds(i * 16, 16), :] = jnp.where(low_q, roll(low[i], 96), above)
        rows_first[pl.ds(i * 16, 16), :] = jnp.where(low_q, below, roll(high[i], 32))


def folded_xy(l_ref, xr_ref, rows_first, rows_last, i, k, gx, lane, sub):
    high_p = lane >= 64
    value = l_ref[i, k]
    if i in (1, 8):
        packed = xr_ref[(k % 5) * 8 : (k % 5) * 8 + 8]
        received = packed if k < 5 else roll(packed, 64)
        value = fold_x(value, i, l_ref[9 if i == 1 else 0, k], received, gx, high_p)
    at = (i - 1) * 16 + k
    return value + jnp.where(sub == 0, row(rows_first, at), jnp.where(sub == 7, row(rows_last, at), 0.0))


def zfold_send_kernel(l_ref, hl_ref, hh_ref, xr_ref, ya_ref, yb_ref, run_ref, za_ref, zb_ref, rows_first, rows_last):
    za_ref[8:24] = run_ref[...]
    gx = lax.axis_index("gx")
    even_z = lax.rem(lax.axis_index("gz"), 2) == 0
    lane, sub = iotas()
    slot = lane & 31
    fold_rows(hl_ref, hh_ref, xr_ref, ya_ref, yb_ref, rows_first, rows_last, gx)
    down = jnp.zeros((8, 128), F32)
    up = jnp.zeros((8, 128), F32)
    for i in range(8):
        down = jnp.where(slot == i, roll(folded_xy(l_ref, xr_ref, rows_first, rows_last, i + 1, 0, gx, lane, sub), i), down)
        up = jnp.where(slot == i, roll(folded_xy(l_ref, xr_ref, rows_first, rows_last, i + 1, 9, gx, lane, sub), i - 31), up)
    za_ref[:8] = jnp.where(even_z, up, down)
    zb_ref[...] = jnp.where(even_z, down, up)


def gather_kernel(
    l_ref, hl_ref, hh_ref, xr_ref, ya_ref, yb_ref, basis_ref, sum_ref, tile_ref, rows_first, rows_last, xt, grid
):
    gx = lax.axis_index("gx")
    lane, sub = iotas()
    slot = lane & 31
    low_q = (lane & 32) == 0
    fold_rows(hl_ref, hh_ref, xr_ref, ya_ref, yb_ref, rows_first, rows_last, gx)
    for i in range(8):
        get = functools.partial(folded_xy, l_ref, xr_ref, rows_first, rows_last, i + 1, gx=gx, lane=lane, sub=sub)
        before, after = get(0), get(9)
        for k in range(8):
            value = get(k + 1)
            if k == 0:
                value = value + jnp.where(slot == 0, 0.0, roll(after, 1))
            if k == 7:
                value = value + jnp.where(slot == 31, 0.0, roll(before, -1))
            grid[i, k] = value
        weights = jnp.concatenate([basis_ref[i]] * 16, 1)
        tile_ref[i * 8 : i * 8 + 8] = weights
    for pair in range(4):
        k0, k1 = 2 * pair, 2 * pair + 1
        pieces = []
        for i in range(8):
            c0, c1 = grid[i, k0], grid[i, k1]
            pieces.append(jnp.where(low_q, c0, roll(c1, 32)))
            pieces.append(jnp.where(low_q, roll(c0, 96), c1))
        block = jnp.concatenate(pieces, 0).T
        for p in range(2):
            for t, k in enumerate((k0, k1)):
                at = p * 64 + t * 32
                xt[p, pl.ds(k, 32, stride=8), :] = block[at : at + 32]
    sum_ref[...] = jnp.concatenate([xt[0], xt[1]], 1).T


def post_kernel(sum_ref, tile_ref, za_ref, zb_ref, sep_ref, run_ref, ownsol_ref, out_ref, total_ref, sems):
    lane, _ = iotas()
    running = run_ref[...] + za_ref[8:24]
    weighted = total(
        sep_ref[level][:, h * 128 : h * 128 + 128] * running[8 * h + level : 8 * h + level + 1, :]
        for h in range(2)
        for level in range(sep_ref.shape[0])
    )
    solution_col = ownsol_ref[:, :1] + jnp.sum(weighted, axis=1, keepdims=True)
    lane16, sub16 = iotas(16)
    along_z = []
    for t in range(2):
        spread = jnp.where((lane16 >> 4) + 8 * t == sub16, jnp.broadcast_to(solution_col, (16, 128)), 0.0)
        along_z.append(jnp.broadcast_to(jnp.sum(spread, axis=0, keepdims=True), (8, 128)))
    from_above, from_below = sides(za_ref[:8], zb_ref[...], "gz")
    copies = []
    for p in range(2):
        for i in range(8):
            weights = tile_ref[i * 8 : i * 8 + 8]
            low, high = weights * along_z[0], weights * along_z[1]
            for q in range(2):
                at = ((p * 8 + i) * 2 + q) * 8
                source = p * 64 + q * 32 + i
                first = sum_ref[at : at + 8, :128] + low
                last = sum_ref[at : at + 8, 128:] + high
                total_ref[at : at + 8, :128] = first + jnp.where(lane == 0, roll(from_below, -source), 0.0)
                total_ref[at : at + 8, 128:] = last + jnp.where(lane == 127, roll(from_above, 127 - source), 0.0)
        rows = pl.ds(p * 128, 128)
        copies.append(pltpu.make_async_copy(total_ref.at[rows, :], out_ref.at[rows, :], sems.at[p]))
        copies[p].start()
    for copy in copies:
        copy.wait()


def call(kernel, outs, scratch, n_in, limit=4 << 20, far=0, semaphores=(), out_space=pltpu.VMEM):
    return pl.pallas_call(
        kernel,
        out_shape=[jax.ShapeDtypeStruct(shape, F32) for shape in outs],
        in_specs=[pl.BlockSpec(memory_space=pltpu.HBM)] * far + [VM] * (n_in - far),
        out_specs=[pl.BlockSpec(memory_space=out_space)] * len(outs),
        scratch_shapes=[pltpu.VMEM(shape, F32) for shape in scratch] + list(semaphores),
        compiler_params=pltpu.CompilerParams(vmem_limit_bytes=limit),
    )


def far(value):
    return pltpu.with_memory_space_constraint(value, pltpu.HBM)


def swap(value, axis, distance):
    return lax.ppermute(value, axis, [(i, i ^ distance) for i in range(lax.axis_size(axis))])


def swap_odd(value, axis):
    count = lax.axis_size(axis)
    return lax.ppermute(value, axis, [(i, (i + 1 if i % 2 else i - 1) % count) for i in range(count)])


def work(residual, fdm_vectors, fdm_eigen, coarse_basis, x_interior, x_separator):
    levels, unknowns, width = x_separator.shape[3:]
    x = residual.reshape(256, 256)
    vectors = fdm_vectors.reshape(3, 10, 10, 128).transpose(1, 2, 0, 3)
    eigen = fdm_eigen.reshape(3, 10, 1, 128)
    own = x_interior.reshape(unknowns, unknowns)
    sep = x_separator.reshape(levels, unknowns, width)
    level_of = lax.broadcasted_iota(jnp.int32, (16, 128), 0) & 7

    def climb(running, axis, distance, first):
        return running + jnp.where(level_of >= first, swap(running, axis, distance), 0.0)

    core, xs, running, ownsol = call(
        pre_kernel,
        [(8, 8, 8, 128), (32, 128), (16, 128), (16, 128)],
        [(2, 128, 256), (2, 256, 128), (levels, unknowns, width), (8, 8, 8), (unknowns, unknowns)],
        4,
        far=4,
        semaphores=(pltpu.SemaphoreType.DMA((2,)), pltpu.SemaphoreType.DMA((3,))),
    )(far(x), far(sep), far(coarse_basis), far(own))
    xr = swap(xs, "gx", 1)
    ends, za, zb = call(zface_kernel, [(2, 8, 8, 128), (8, 128), (8, 128)], [], 2)(core, xr)
    running = climb(running, "gy", 2, 5)
    za, zb = swap(za, "gz", 1), swap_odd(zb, "gz")
    running = climb(running, "gy", 6, 6)
    (factors,) = call(factors_kernel, [(848, 128)], [], 1)(vectors)
    block = (core, core.reshape(512, 128), ends, ends.reshape(128, 128), za, zb)
    ya, yb = call(yface_kernel, [(56, 128), (56, 128)], [(256, 128)], 6)(*block)
    ya, yb = swap(ya, "gy", 1), swap_odd(yb, "gy")
    four, twelve, eight = (swap(running, "gz", d) for d in (4, 12, 8))
    modes, edges = call(front_kernel, [(1696, 128), (320, 128)], [(848, 128)], 5)(core, ends, *block[4:], factors)
    (modes,) = call(modes_kernel, [(1696, 128)], [(640, 128)], 5)(modes, edges, ya, yb, factors)
    (modes,) = call(middle_kernel, [(1696, 128)], [(16, 128)], 3)(modes, factors, eigen)
    both = jnp.where(level_of >= 3, four + (twelve + eight), four)
    running = running + jnp.where(level_of >= 2, both, 0.0)
    running = climb(running, "gz", 3, 1)
    local, edge_l, edge_h, xs = call(
        points_kernel, [(10, 10, 8, 128), (10, 16, 128), (10, 16, 128), (56, 128)], [(1696, 128)], 2
    )(modes, factors)
    xr = swap(xs, "gx", 1)
    ya, yb = call(yfold_send_kernel, [(80, 128), (64, 128)], [], 4)(edge_l, edge_h, xr, running)
    ya, yb = swap(ya, "gy", 1), swap_odd(yb, "gy")
    running = running + jnp.where(level_of >= 4, ya[64:80], 0.0)
    running = climb(running, "gx", 1, 7)
    parts = (local, edge_l, edge_h, xr, ya, yb)
    za, zb = call(zfold_send_kernel, [(24, 128), (8, 128)], [(128, 128)] * 2, 7)(*parts, running)
    za, zb = swap(za, "gz", 1), swap_odd(zb, "gz")
    smooth, tile = call(
        gather_kernel, [(256, 256), (64, 128)], [(128, 128), (128, 128), (2, 256, 128), (8, 8, 8, 128)], 7
    )(*parts, coarse_basis)
    (out,) = call(
        post_kernel, [(256, 256)], [(256, 256)], 7, semaphores=(pltpu.SemaphoreType.DMA((2,)),), out_space=pltpu.HBM
    )(smooth, tile, za, zb, sep, running, ownsol)
    return out.reshape(residual.shape)


def solution(mesh):
    in_specs = (
        P("gx", "gy", "gz"),
        P("gx", "gy", "gz", None, None, None, None),
        P("gx", "gy", "gz", None, None, None),
        P(),
        P("gx", "gy", "gz", None, None),
        P("gx", "gy", "gz", None, None, None),
    )
    return jax.shard_map(work, mesh=mesh, in_specs=in_specs, out_specs=P("gx", "gy", "gz"), check_vma=False)
```

```python
import functools

import jax
import jax.numpy as jnp
from jax import lax
from jax.experimental import pallas as pl
from jax.experimental.pallas import tpu as pltpu
from jax.sharding import PartitionSpec as P


F32 = jnp.float32
VM = pl.BlockSpec(memory_space=pltpu.VMEM)


def iotas(rows=8):
    lane = lax.broadcasted_iota(jnp.int32, (rows, 128), 1)
    sub = lax.broadcasted_iota(jnp.int32, (rows, 128), 0)
    return lane, sub


def roll(value, shift):
    shift = shift % 128
    return value if shift == 0 else pltpu.roll(value, shift, value.ndim - 1)


def row(ref, index, rows=8):
    return jnp.broadcast_to(ref[pl.ds(index, 1), :], (rows, 128))


def total(terms):
    terms = list(terms)
    while len(terms) > 1:
        terms = [a + b for a, b in zip(terms[::2], terms[1::2])] + terms[len(terms) & ~1 :]
    return terms[0]


def chain(pairs):
    acc = None
    for a, b in pairs:
        acc = a * b if acc is None else acc + a * b
    return acc


def pre_kernel(
    x_ref, sep_ref, basis_ref, own_ref, core_ref, xs_ref, run_ref, ownsol_ref, xv, xt, sepv, basisv, ownv, xsem, sems
):
    copies = [pltpu.make_async_copy(x_ref.at[pl.ds(p * 128, 128), :], xv.at[p], xsem.at[p]) for p in range(2)]
    small = [
        pltpu.make_async_copy(a, b, sems.at[n])
        for n, (a, b) in enumerate(((basis_ref, basisv), (own_ref, ownv), (sep_ref, sepv)))
    ]
    for copy in copies + small:
        copy.start()
    gx = lax.axis_index("gx")
    lane, _ = iotas()
    low_q = (lane & 32) == 0
    high_p = lane >= 64
    for p in range(2):
        copies[p].wait()
        xt[p] = xv[p].T
    for pair in range(4):
        k0, k1 = 2 * pair, 2 * pair + 1
        pieces = [xt[p, pl.ds(k, 32, stride=8), :] for p in range(2) for k in (k0, k1)]
        block = jnp.concatenate(pieces, 0).T
        for i in range(8):
            a = block[i * 16 : i * 16 + 8]
            b = block[i * 16 + 8 : i * 16 + 16]
            core_ref[i, k0] = jnp.where(low_q, a, roll(b, 32))
            core_ref[i, k1] = jnp.where(low_q, roll(a, 96), b)

    def outgoing(k):
        return jnp.where(gx == 0, core_ref[7, k], roll(core_ref[0, k], 64))

    for k in range(4):
        xs_ref[k * 8 : k * 8 + 8] = jnp.where(high_p, outgoing(k), roll(outgoing(k + 4), 64))
    small[0].wait()
    sums = []
    for i in range(8):
        weights = basisv[i]
        sums.append(chain((core_ref[i, k], jnp.broadcast_to(weights[:, k : k + 1], (8, 128))) for k in range(8)))
    lanes = jnp.sum(total(sums), axis=0, keepdims=True)
    lane16, sub16 = iotas(16)
    spread = jnp.where(((lane16 & 31) >> 1) == sub16, jnp.broadcast_to(lanes, (16, 128)), 0.0)
    rhs = jnp.sum(spread, axis=1, keepdims=True)
    small[1].wait()
    own = ownv[...]
    coef = jnp.sum(own * rhs, axis=0, keepdims=True)
    ownsol_ref[...] = jnp.broadcast_to(jnp.sum(own * coef, axis=1, keepdims=True), (16, 128))
    small[2].wait()
    for level in range(sep_ref.shape[0]):
        part = jnp.sum(sepv[level] * rhs, axis=0, keepdims=True)
        for h in range(2):
            run_ref[8 * h + level : 8 * h + level + 1, :] = part[:, h * 128 : h * 128 + 128]


def zface_kernel(core_ref, xr_ref, ends_ref, za_ref, zb_ref):
    gx = lax.axis_index("gx")
    even = lax.rem(lax.axis_index("gz"), 2) == 0
    lane, _ = iotas()
    high_p = lane >= 64
    slot = lane & 31
    for k in range(8):
        at = (k % 4) * 8
        got = xr_ref[at : at + 8]
        if k >= 4:
            got = roll(got, 64)
        ends_ref[0, k] = jnp.where(high_p, roll(core_ref[7, k], 64), jnp.where(gx == 1, roll(got, 64), 0.0))
        ends_ref[1, k] = jnp.where(high_p, jnp.where(gx == 0, got, 0.0), roll(core_ref[0, k], 64))
    upper = jnp.zeros((8, 128), F32)
    lower = jnp.zeros((8, 128), F32)
    for i in range(10):
        upper = jnp.where(slot == i, roll(plane(core_ref, ends_ref, i, 7), i - 31), upper)
        lower = jnp.where(slot == i, roll(plane(core_ref, ends_ref, i, 0), i), lower)
    za_ref[...] = jnp.where(even, upper, lower)
    zb_ref[...] = jnp.where(even, lower, upper)


def plane(core_ref, ends_ref, i, k):
    return core_ref[i - 1, k] if 1 <= i <= 8 else ends_ref[i // 9, k]


def sides(a, b, axis):
    index = lax.axis_index(axis)
    even = lax.rem(index, 2) == 0
    above = jnp.where(index == lax.axis_size(axis) - 1, 0.0, jnp.where(even, a, b))
    below = jnp.where(index == 0, 0.0, jnp.where(even, b, a))
    return above, below


def z_halo(core_ref, ends_ref, za_ref, zb_ref, slot):
    from_above, from_below = sides(za_ref[...], zb_ref[...], "gz")
    first, last = [], []
    for i in range(10):
        first.append(jnp.where(slot == 0, roll(from_below, -i), roll(plane(core_ref, ends_ref, i, 7), 1)))
        last.append(jnp.where(slot == 31, roll(from_above, 31 - i), roll(plane(core_ref, ends_ref, i, 0), -1)))
    return first, last


def y_rows(first, last, core2_ref, ends2_ref, scr):
    for i in range(10):
        scr[pl.ds(i * 8, 8), :] = first[i]
        scr[pl.ds(128 + i * 8, 8), :] = last[i]
    low, high = [], []
    for i in range(10):
        ref, at = (core2_ref, (i - 1) * 64) if 1 <= i <= 8 else (ends2_ref, (i // 9) * 64)
        low.append(ref[pl.ds(at, 8, stride=8), :])
        high.append(ref[pl.ds(at + 7, 8, stride=8), :])
    low_ends = [scr[pl.ds(b, 16, stride=8), :] for b in (0, 128)]
    high_ends = [scr[pl.ds(b + 7, 16, stride=8), :] for b in (0, 128)]
    return low, high, low_ends, high_ends


def yface_kernel(core_ref, core2_ref, ends_ref, ends2_ref, za_ref, zb_ref, ya_ref, yb_ref, scr):
    even_y = lax.rem(lax.axis_index("gy"), 2) == 0
    lane, _ = iotas()
    low_q = (lane & 32) == 0
    first, last = z_halo(core_ref, ends_ref, za_ref, zb_ref, lane & 31)
    low, high, low_ends, high_ends = y_rows(first, last, core2_ref, ends2_ref, scr)
    for i in range(5):
        down = jnp.where(low_q, low[i], roll(low[i + 5], 32))
        up = jnp.where(low_q, roll(high[i + 5], 96), high[i])
        ya_ref[i * 8 : i * 8 + 8] = jnp.where(even_y, up, down)
        yb_ref[i * 8 : i * 8 + 8] = jnp.where(even_y, down, up)
    low_q = (iotas(16)[0] & 32) == 0
    down = jnp.where(low_q, low_ends[0], roll(low_ends[1], 32))
    up = jnp.where(low_q, roll(high_ends[1], 96), high_ends[0])
    ya_ref[40:56] = jnp.where(even_y, up, down)
    yb_ref[40:56] = jnp.where(even_y, down, up)


def factors_kernel(vec_ref, eig_ref, s_ref, held_ref):
    held_ref[...] = eig_ref[...]
    for a in range(10):
        for i in range(10):
            s_ref[(i * 10 + a) * 8 : (i * 10 + a) * 8 + 3] = vec_ref[i, a].astype(F32)


def factor_of(s):
    return lambda d, i, a: row(s, (i * 10 + a) * 8 + d)


def along_x(source, target, factor, transposed):
    def step(k, _):
        for h in range(2):
            at = k * 16 + 8 * h
            held = [source[pl.ds(i * 160 + at, 8), :] for i in range(10)]
            for a in range(10):
                target[pl.ds(a * 160 + at, 8), :] = chain(
                    (factor(0, a, i) if transposed else factor(0, i, a), held[i]) for i in range(10)
                )
        return 0

    lax.fori_loop(0, 10, step, 0)


def y_factors(s):
    return [[s[pl.ds((j * 10 + 8 * h) * 8 + 1, 8, stride=8), :] for j in range(10)] for h in range(2)]


def front_kernel(core_ref, ends_ref, za_ref, zb_ref, s, u, edge_ref, block):
    lane, _ = iotas()
    first, last = z_halo(core_ref, ends_ref, za_ref, zb_ref, lane & 31)
    for i in range(10):
        block[pl.ds(i * 80, 8), :] = first[i]
        block[pl.ds(i * 80 + 72, 8), :] = last[i]
        for k in range(8):
            block[pl.ds(i * 80 + 8 + k * 8, 8), :] = plane(core_ref, ends_ref, i, k)
    for i in range(10):
        edge_ref[i * 16 : i * 16 + 16] = roll(block[pl.ds(i * 80 + 7, 16, stride=8), :], 32)
        edge_ref[160 + i * 16 : 176 + i * 16] = roll(block[pl.ds(i * 80, 16, stride=8), :], 96)
    factor = factor_of(s)
    front = y_factors(s)

    def along(k, _):
        held = [block[pl.ds(i * 80 + k * 8, 8), :] for i in range(10)]
        for a in range(10):
            block[pl.ds(a * 80 + k * 8, 8), :] = chain((factor(0, i, a), held[i]) for i in range(10))
        return 0

    lax.fori_loop(0, 10, along, 0)

    def own_rows(a, _):
        for k in range(10):
            at = (a * 10 + k) * 8
            rows = [row(block, at + j) for j in range(8)]
            for h in range(2):
                u[pl.ds(at * 2 + 8 * h, 8), :] = chain((front[h][j + 1], rows[j]) for j in range(8))
        return 0

    lax.fori_loop(0, 10, own_rows, 0)


def modes_kernel(u_ref, edge_ref, ya_ref, yb_ref, s, u, rows):
    low_q = (iotas(16)[0] & 32) == 0
    ends_above, ends_below = sides(ya_ref[40:56], yb_ref[40:56], "gy")
    for i in range(10):
        at = (i % 5) * 8
        above, below = sides(ya_ref[at : at + 8], yb_ref[at : at + 8], "gy")
        if i < 5:
            above, below = roll(above, 32), roll(below, 96)
        for base, middle, zero, nine in (
            (0, below, roll(ends_below, 96), ends_below),
            (160, above, roll(ends_above, 32), ends_above),
        ):
            rows[base + i * 16 + 1 : base + i * 16 + 9] = middle
            rows[base + i * 16 : base + i * 16 + 1] = zero[i : i + 1]
            rows[base + i * 16 + 9 : base + i * 16 + 10] = nine[i : i + 1]
    low = [jnp.where(low_q, rows[i * 16 : i * 16 + 16], edge_ref[i * 16 : i * 16 + 16]) for i in range(10)]
    high = [
        jnp.where(low_q, edge_ref[160 + i * 16 : 176 + i * 16], rows[160 + i * 16 : 176 + i * 16]) for i in range(10)
    ]
    front = y_factors(s)
    for a in range(10):
        weights = [row(s, (i * 10 + a) * 8, 16) for i in range(10)]
        rows[320 + a * 16 : 336 + a * 16] = chain((weights[i], low[i]) for i in range(10))
        rows[480 + a * 16 : 496 + a * 16] = chain((weights[i], high[i]) for i in range(10))

    def add_edges(a, _):
        for k in range(10):
            before, after = row(rows, 320 + a * 16 + k), row(rows, 480 + a * 16 + k)
            for h in range(2):
                at = (a * 10 + k) * 16 + 8 * h
                u[pl.ds(at, 8), :] = u_ref[pl.ds(at, 8), :] + (front[h][0] * before + front[h][9] * after)
        return 0

    lax.fori_loop(0, 10, add_edges, 0)


def middle_kernel(u_ref, s, eig_ref, u, eg):
    eg[...] = jnp.ones((16, 128), F32)
    for a in range(10):
        eg[a : a + 1] = eig_ref[1, a]
    factor = factor_of(s)

    def wide(value):
        return jnp.broadcast_to(value, (8, 128))

    def along_z(a, _):
        for h in range(2):
            at = a * 160 + 8 * h
            held = [u_ref[pl.ds(at + k * 16, 8), :] for k in range(10)]
            base = wide(eig_ref[0, a]) + eg[8 * h : 8 * h + 8]
            modes = []
            for c in range(10):
                modes.append(chain((factor(2, k, c), held[k]) for k in range(10)) / (base + wide(eig_ref[2, c])))
            for k in range(10):
                u[pl.ds(at + k * 16, 8), :] = chain((factor(2, k, c), modes[c]) for c in range(10))
        return 0

    lax.fori_loop(0, 10, along_z, 0)


def points_kernel(u_ref, s, l_ref, hl_ref, hh_ref, xs_ref, u):
    gx = lax.axis_index("gx")
    lane, _ = iotas()
    factor = factor_of(s)
    along_x(u_ref, u, factor, True)
    back = [s[pl.ds((10 + b) * 8 + 1, 8, stride=80), :] for b in range(10)]

    def back_y(i, _):
        for k in range(10):
            at = (i * 10 + k) * 16
            l_ref[i, k] = chain((back[b], row(u, at + b)) for b in range(10))
        for h in range(2):
            cut = [u[pl.ds(i * 160 + 128 * h + b, 8, stride=16), :] for b in range(10)]
            hl_ref[i, 8 * h : 8 * h + 8] = chain((factor(1, 0, b), cut[b]) for b in range(10))
            hh_ref[i, 8 * h : 8 * h + 8] = chain((factor(1, 9, b), cut[b]) for b in range(10))
        return 0

    lax.fori_loop(0, 10, back_y, 0)
    high_p = lane >= 64

    def outgoing(ref, k):
        return jnp.where(gx == 0, ref[9, k], roll(ref[0, k], 64))

    for k in range(5):
        xs_ref[k * 8 : k * 8 + 8] = jnp.where(high_p, outgoing(l_ref, k), roll(outgoing(l_ref, k + 5), 64))
    high_p = iotas(16)[0] >= 64
    edge_l = jnp.where(gx == 0, hl_ref[9], roll(hl_ref[0], 64))
    edge_h = jnp.where(gx == 0, hh_ref[9], roll(hh_ref[0], 64))
    xs_ref[40:56] = jnp.where(high_p, edge_l, roll(edge_h, 64))


def fold_x(value, i, opposite, received, gx, high_p):
    if i == 8:
        return value + jnp.where(high_p, jnp.where(gx == 0, received, 0.0), roll(opposite, 64))
    if i == 1:
        return value + jnp.where(high_p, roll(opposite, 64), jnp.where(gx == 1, roll(received, 64), 0.0))
    return value


def edge_rows(hl_ref, hh_ref, xr_ref, gx):
    high_p = iotas(16)[0] >= 64
    packed = xr_ref[40:56]
    low, high = [], []
    for i in range(1, 9):
        j = {1: 9, 8: 0}.get(i, i)
        low.append(fold_x(hl_ref[i], i, hl_ref[j], packed, gx, high_p))
        high.append(fold_x(hh_ref[i], i, hh_ref[j], roll(packed, 64), gx, high_p))
    return low, high


def yfold_send_kernel(hl_ref, hh_ref, xr_ref, run_ref, ya_ref, yb_ref):
    ya_ref[40:56] = run_ref[...]
    gx = lax.axis_index("gx")
    even_y = lax.rem(lax.axis_index("gy"), 2) == 0
    low_q = (iotas(16)[0] & 32) == 0
    low, high = edge_rows(hl_ref, hh_ref, xr_ref, gx)
    for i in range(4):
        down = jnp.where(low_q, low[i], roll(low[i + 4], 32))
        up = jnp.where(low_q, roll(high[i + 4], 96), high[i])
        for ref, value in ((ya_ref, jnp.where(even_y, up, down)), (yb_ref, jnp.where(even_y, down, up))):
            ref[i * 8 : i * 8 + 8] = value[:8]
            ref[32 + 2 * i : 34 + 2 * i] = value[8:10]


def fold_rows(hl_ref, hh_ref, xr_ref, ya_ref, yb_ref, rows_first, rows_last, gx):
    low_q = (iotas(16)[0] & 32) == 0
    low, high = edge_rows(hl_ref, hh_ref, xr_ref, gx)
    for i in range(8):
        n = i % 4
        rows = [jnp.concatenate([ref[n * 8 : n * 8 + 8], ref[32 + 2 * n : 40 + 2 * n]], 0) for ref in (ya_ref, yb_ref)]
        above, below = sides(*rows, "gy")
        if i < 4:
            above, below = roll(above, 32), roll(below, 96)
        rows_last[pl.ds(i * 16, 16), :] = jnp.where(low_q, roll(low[i], 96), above)
        rows_first[pl.ds(i * 16, 16), :] = jnp.where(low_q, below, roll(high[i], 32))


def folded_xy(l_ref, xr_ref, rows_first, rows_last, i, k, gx, lane, sub):
    high_p = lane >= 64
    value = l_ref[i, k]
    if i in (1, 8):
        packed = xr_ref[(k % 5) * 8 : (k % 5) * 8 + 8]
        received = packed if k < 5 else roll(packed, 64)
        value = fold_x(value, i, l_ref[9 if i == 1 else 0, k], received, gx, high_p)
    at = (i - 1) * 16 + k
    return value + jnp.where(sub == 0, row(rows_first, at), jnp.where(sub == 7, row(rows_last, at), 0.0))


def zfold_send_kernel(l_ref, hl_ref, hh_ref, xr_ref, ya_ref, yb_ref, run_ref, za_ref, zb_ref, rows_first, rows_last):
    za_ref[8:24] = run_ref[...]
    gx = lax.axis_index("gx")
    even_z = lax.rem(lax.axis_index("gz"), 2) == 0
    lane, sub = iotas()
    slot = lane & 31
    fold_rows(hl_ref, hh_ref, xr_ref, ya_ref, yb_ref, rows_first, rows_last, gx)
    down = jnp.zeros((8, 128), F32)
    up = jnp.zeros((8, 128), F32)
    for i in range(8):
        down = jnp.where(slot == i, roll(folded_xy(l_ref, xr_ref, rows_first, rows_last, i + 1, 0, gx, lane, sub), i), down)
        up = jnp.where(slot == i, roll(folded_xy(l_ref, xr_ref, rows_first, rows_last, i + 1, 9, gx, lane, sub), i - 31), up)
    za_ref[:8] = jnp.where(even_z, up, down)
    zb_ref[...] = jnp.where(even_z, down, up)


def gather_kernel(
    l_ref, hl_ref, hh_ref, xr_ref, ya_ref, yb_ref, basis_ref, sum_ref, tile_ref, rows_first, rows_last, xt, grid
):
    gx = lax.axis_index("gx")
    lane, sub = iotas()
    slot = lane & 31
    low_q = (lane & 32) == 0
    fold_rows(hl_ref, hh_ref, xr_ref, ya_ref, yb_ref, rows_first, rows_last, gx)
    for i in range(8):
        get = functools.partial(folded_xy, l_ref, xr_ref, rows_first, rows_last, i + 1, gx=gx, lane=lane, sub=sub)
        before, after = get(0), get(9)
        for k in range(8):
            value = get(k + 1)
            if k == 0:
                value = value + jnp.where(slot == 0, 0.0, roll(after, 1))
            if k == 7:
                value = value + jnp.where(slot == 31, 0.0, roll(before, -1))
            grid[i, k] = value
        weights = jnp.concatenate([basis_ref[i]] * 16, 1)
        tile_ref[i * 8 : i * 8 + 8] = weights
    for pair in range(4):
        k0, k1 = 2 * pair, 2 * pair + 1
        pieces = []
        for i in range(8):
            c0, c1 = grid[i, k0], grid[i, k1]
            pieces.append(jnp.where(low_q, c0, roll(c1, 32)))
            pieces.append(jnp.where(low_q, roll(c0, 96), c1))
        block = jnp.concatenate(pieces, 0).T
        for p in range(2):
            for t, k in enumerate((k0, k1)):
                at = p * 64 + t * 32
                xt[p, pl.ds(k, 32, stride=8), :] = block[at : at + 32]
    sum_ref[...] = jnp.concatenate([xt[0], xt[1]], 1).T


def post_kernel(sum_ref, tile_ref, za_ref, zb_ref, sep_ref, run_ref, ownsol_ref, out_ref, total_ref, sems):
    lane, _ = iotas()
    running = run_ref[...] + za_ref[8:24]
    weighted = total(
        sep_ref[level][:, h * 128 : h * 128 + 128] * running[8 * h + level : 8 * h + level + 1, :]
        for h in range(2)
        for level in range(sep_ref.shape[0])
    )
    solution_col = ownsol_ref[:, :1] + jnp.sum(weighted, axis=1, keepdims=True)
    lane16, sub16 = iotas(16)
    along_z = []
    for t in range(2):
        spread = jnp.where((lane16 >> 4) + 8 * t == sub16, jnp.broadcast_to(solution_col, (16, 128)), 0.0)
        along_z.append(jnp.broadcast_to(jnp.sum(spread, axis=0, keepdims=True), (8, 128)))
    from_above, from_below = sides(za_ref[:8], zb_ref[...], "gz")
    copies = []
    for p in range(2):
        for i in range(8):
            weights = tile_ref[i * 8 : i * 8 + 8]
            low, high = weights * along_z[0], weights * along_z[1]
            for q in range(2):
                at = ((p * 8 + i) * 2 + q) * 8
                source = p * 64 + q * 32 + i
                first = sum_ref[at : at + 8, :128] + low
                last = sum_ref[at : at + 8, 128:] + high
                total_ref[at : at + 8, :128] = first + jnp.where(lane == 0, roll(from_below, -source), 0.0)
                total_ref[at : at + 8, 128:] = last + jnp.where(lane == 127, roll(from_above, 127 - source), 0.0)
        rows = pl.ds(p * 128, 128)
        copies.append(pltpu.make_async_copy(total_ref.at[rows, :], out_ref.at[rows, :], sems.at[p]))
        copies[p].start()
    for copy in copies:
        copy.wait()


def call(kernel, outs, scratch, n_in, limit=4 << 20, far=0, semaphores=(), out_space=pltpu.VMEM):
    return pl.pallas_call(
        kernel,
        out_shape=[jax.ShapeDtypeStruct(shape, F32) for shape in outs],
        in_specs=[pl.BlockSpec(memory_space=pltpu.HBM)] * far + [VM] * (n_in - far),
        out_specs=[pl.BlockSpec(memory_space=out_space)] * len(outs),
        scratch_shapes=[pltpu.VMEM(shape, F32) for shape in scratch] + list(semaphores),
        compiler_params=pltpu.CompilerParams(vmem_limit_bytes=limit),
    )


def far(value):
    return pltpu.with_memory_space_constraint(value, pltpu.HBM)


def swap(value, axis, distance):
    return lax.ppermute(value, axis, [(i, i ^ distance) for i in range(lax.axis_size(axis))])


def swap_odd(value, axis):
    count = lax.axis_size(axis)
    return lax.ppermute(value, axis, [(i, (i + 1 if i % 2 else i - 1) % count) for i in range(count)])


def work(residual, fdm_vectors, fdm_eigen, coarse_basis, x_interior, x_separator):
    levels, unknowns, width = x_separator.shape[3:]
    x = residual.reshape(256, 256)
    vectors = fdm_vectors.reshape(3, 10, 10, 128).transpose(1, 2, 0, 3)
    eigen = fdm_eigen.reshape(3, 10, 1, 128)
    own = x_interior.reshape(unknowns, unknowns)
    sep = x_separator.reshape(levels, unknowns, width)
    level_of = lax.broadcasted_iota(jnp.int32, (16, 128), 0) & 7

    def climb(running, axis, distance, first):
        return running + jnp.where(level_of >= first, swap(running, axis, distance), 0.0)

    core, xs, running, ownsol = call(
        pre_kernel,
        [(8, 8, 8, 128), (32, 128), (16, 128), (16, 128)],
        [(2, 128, 256), (2, 256, 128), (levels, unknowns, width), (8, 8, 8), (unknowns, unknowns)],
        4,
        far=4,
        semaphores=(pltpu.SemaphoreType.DMA((2,)), pltpu.SemaphoreType.DMA((3,))),
    )(far(x), far(sep), far(coarse_basis), far(own))
    xr = swap(xs, "gx", 1)
    ends, za, zb = call(zface_kernel, [(2, 8, 8, 128), (8, 128), (8, 128)], [], 2)(core, xr)
    running = climb(running, "gy", 2, 5)
    za, zb = swap(za, "gz", 1), swap_odd(zb, "gz")
    running = climb(running, "gy", 6, 6)
    factors, eigen = call(factors_kernel, [(848, 128), eigen.shape], [], 2)(vectors, eigen)
    block = (core, core.reshape(512, 128), ends, ends.reshape(128, 128), za, zb)
    ya, yb = call(yface_kernel, [(56, 128), (56, 128)], [(256, 128)], 6)(*block)
    ya, yb = swap(ya, "gy", 1), swap_odd(yb, "gy")
    four, twelve, eight = (swap(running, "gz", d) for d in (4, 12, 8))
    modes, edges = call(front_kernel, [(1696, 128), (320, 128)], [(848, 128)], 5)(core, ends, *block[4:], factors)
    (modes,) = call(modes_kernel, [(1696, 128)], [(640, 128)], 5)(modes, edges, ya, yb, factors)
    (modes,) = call(middle_kernel, [(1696, 128)], [(16, 128)], 3)(modes, factors, eigen)
    both = jnp.where(level_of >= 3, four + (twelve + eight), four)
    running = running + jnp.where(level_of >= 2, both, 0.0)
    running = climb(running, "gz", 3, 1)
    local, edge_l, edge_h, xs = call(
        points_kernel, [(10, 10, 8, 128), (10, 16, 128), (10, 16, 128), (56, 128)], [(1696, 128)], 2
    )(modes, factors)
    xr = swap(xs, "gx", 1)
    ya, yb = call(yfold_send_kernel, [(56, 128), (48, 128)], [], 4)(edge_l, edge_h, xr, running)
    ya, yb = swap(ya, "gy", 1), swap_odd(yb, "gy")
    running = running + jnp.where(level_of >= 4, ya[40:56], 0.0)
    running = climb(running, "gx", 1, 7)
    parts = (local, edge_l, edge_h, xr, ya, yb)
    za, zb = call(zfold_send_kernel, [(24, 128), (8, 128)], [(128, 128)] * 2, 7)(*parts, running)
    za, zb = swap(za, "gz", 1), swap_odd(zb, "gz")
    smooth, tile = call(
        gather_kernel, [(256, 256), (64, 128)], [(128, 128), (128, 128), (2, 256, 128), (8, 8, 8, 128)], 7
    )(*parts, coarse_basis)
    (out,) = call(
        post_kernel, [(256, 256)], [(256, 256)], 7, semaphores=(pltpu.SemaphoreType.DMA((2,)),), out_space=pltpu.HBM
    )(smooth, tile, za, zb, sep, running, ownsol)
    return out.reshape(residual.shape)


def solution(mesh):
    in_specs = (
        P("gx", "gy", "gz"),
        P("gx", "gy", "gz", None, None, None, None),
        P("gx", "gy", "gz", None, None, None),
        P(),
        P("gx", "gy", "gz", None, None),
        P("gx", "gy", "gz", None, None, None),
    )
    return jax.shard_map(work, mesh=mesh, in_specs=in_specs, out_specs=P("gx", "gy", "gz"), check_vma=False)
```

```python
import functools

import jax
import jax.numpy as jnp
from jax import lax
from jax.experimental import pallas as pl
from jax.experimental.pallas import tpu as pltpu
from jax.sharding import PartitionSpec as P


F32 = jnp.float32
VM = pl.BlockSpec(memory_space=pltpu.VMEM)


def iotas(rows=8):
    lane = lax.broadcasted_iota(jnp.int32, (rows, 128), 1)
    sub = lax.broadcasted_iota(jnp.int32, (rows, 128), 0)
    return lane, sub


def roll(value, shift):
    shift = shift % 128
    return value if shift == 0 else pltpu.roll(value, shift, value.ndim - 1)


def row(ref, index, rows=8):
    return jnp.broadcast_to(ref[pl.ds(index, 1), :], (rows, 128))


def total(terms):
    terms = list(terms)
    while len(terms) > 1:
        terms = [a + b for a, b in zip(terms[::2], terms[1::2])] + terms[len(terms) & ~1 :]
    return terms[0]


def chain(pairs):
    acc = None
    for a, b in pairs:
        acc = a * b if acc is None else acc + a * b
    return acc


def pre_kernel(
    x_ref, sep_ref, basis_ref, own_ref, core_ref, xs_ref, run_ref, ownsol_ref, xv, xt, sepv, basisv, ownv, xsem, sems
):
    copies = [pltpu.make_async_copy(x_ref.at[pl.ds(p * 128, 128), :], xv.at[p], xsem.at[p]) for p in range(2)]
    small = [
        pltpu.make_async_copy(a, b, sems.at[n])
        for n, (a, b) in enumerate(((basis_ref, basisv), (own_ref, ownv), (sep_ref, sepv)))
    ]
    for copy in copies + small:
        copy.start()
    gx = lax.axis_index("gx")
    lane, _ = iotas()
    low_q = (lane & 32) == 0
    high_p = lane >= 64
    for p in range(2):
        copies[p].wait()
        xt[p] = xv[p].T
    for pair in range(4):
        k0, k1 = 2 * pair, 2 * pair + 1
        pieces = [xt[p, pl.ds(k, 32, stride=8), :] for p in range(2) for k in (k0, k1)]
        block = jnp.concatenate(pieces, 0).T
        for i in range(8):
            a = block[i * 16 : i * 16 + 8]
            b = block[i * 16 + 8 : i * 16 + 16]
            core_ref[i, k0] = jnp.where(low_q, a, roll(b, 32))
            core_ref[i, k1] = jnp.where(low_q, roll(a, 96), b)

    def outgoing(k):
        return jnp.where(gx == 0, core_ref[7, k], roll(core_ref[0, k], 64))

    for k in range(4):
        xs_ref[k * 8 : k * 8 + 8] = jnp.where(high_p, outgoing(k), roll(outgoing(k + 4), 64))
    small[0].wait()
    sums = []
    for i in range(8):
        weights = basisv[i]
        sums.append(chain((core_ref[i, k], jnp.broadcast_to(weights[:, k : k + 1], (8, 128))) for k in range(8)))
    lanes = jnp.sum(total(sums), axis=0, keepdims=True)
    lane16, sub16 = iotas(16)
    spread = jnp.where(((lane16 & 31) >> 1) == sub16, jnp.broadcast_to(lanes, (16, 128)), 0.0)
    rhs = jnp.sum(spread, axis=1, keepdims=True)
    small[1].wait()
    own = ownv[...]
    coef = jnp.sum(own * rhs, axis=0, keepdims=True)
    ownsol_ref[...] = jnp.broadcast_to(jnp.sum(own * coef, axis=1, keepdims=True), (16, 128))
    small[2].wait()
    for level in range(sep_ref.shape[0]):
        part = jnp.sum(sepv[level] * rhs, axis=0, keepdims=True)
        for h in range(2):
            run_ref[8 * h + level : 8 * h + level + 1, :] = part[:, h * 128 : h * 128 + 128]


def zface_kernel(core_ref, xr_ref, ends_ref, za_ref, zb_ref):
    gx = lax.axis_index("gx")
    even = lax.rem(lax.axis_index("gz"), 2) == 0
    lane, _ = iotas()
    high_p = lane >= 64
    slot = lane & 31
    for k in range(8):
        at = (k % 4) * 8
        got = xr_ref[at : at + 8]
        if k >= 4:
            got = roll(got, 64)
        ends_ref[0, k] = jnp.where(high_p, roll(core_ref[7, k], 64), jnp.where(gx == 1, roll(got, 64), 0.0))
        ends_ref[1, k] = jnp.where(high_p, jnp.where(gx == 0, got, 0.0), roll(core_ref[0, k], 64))
    upper = jnp.zeros((8, 128), F32)
    lower = jnp.zeros((8, 128), F32)
    for i in range(10):
        upper = jnp.where(slot == i, roll(plane(core_ref, ends_ref, i, 7), i - 31), upper)
        lower = jnp.where(slot == i, roll(plane(core_ref, ends_ref, i, 0), i), lower)
    za_ref[...] = jnp.where(even, upper, lower)
    zb_ref[...] = jnp.where(even, lower, upper)


def plane(core_ref, ends_ref, i, k):
    return core_ref[i - 1, k] if 1 <= i <= 8 else ends_ref[i // 9, k]


def sides(a, b, axis):
    index = lax.axis_index(axis)
    even = lax.rem(index, 2) == 0
    above = jnp.where(index == lax.axis_size(axis) - 1, 0.0, jnp.where(even, a, b))
    below = jnp.where(index == 0, 0.0, jnp.where(even, b, a))
    return above, below


def z_halo(core_ref, ends_ref, za_ref, zb_ref, slot):
    from_above, from_below = sides(za_ref[...], zb_ref[...], "gz")
    first, last = [], []
    for i in range(10):
        first.append(jnp.where(slot == 0, roll(from_below, -i), roll(plane(core_ref, ends_ref, i, 7), 1)))
        last.append(jnp.where(slot == 31, roll(from_above, 31 - i), roll(plane(core_ref, ends_ref, i, 0), -1)))
    return first, last


def y_rows(first, last, core2_ref, ends2_ref, scr):
    for i in range(10):
        scr[pl.ds(i * 8, 8), :] = first[i]
        scr[pl.ds(128 + i * 8, 8), :] = last[i]
    low, high = [], []
    for i in range(10):
        ref, at = (core2_ref, (i - 1) * 64) if 1 <= i <= 8 else (ends2_ref, (i // 9) * 64)
        low.append(ref[pl.ds(at, 8, stride=8), :])
        high.append(ref[pl.ds(at + 7, 8, stride=8), :])
    low_ends = [scr[pl.ds(b, 16, stride=8), :] for b in (0, 128)]
    high_ends = [scr[pl.ds(b + 7, 16, stride=8), :] for b in (0, 128)]
    return low, high, low_ends, high_ends


def yface_kernel(core_ref, core2_ref, ends_ref, ends2_ref, za_ref, zb_ref, ya_ref, yb_ref, scr):
    even_y = lax.rem(lax.axis_index("gy"), 2) == 0
    lane, _ = iotas()
    low_q = (lane & 32) == 0
    first, last = z_halo(core_ref, ends_ref, za_ref, zb_ref, lane & 31)
    low, high, low_ends, high_ends = y_rows(first, last, core2_ref, ends2_ref, scr)
    for i in range(5):
        down = jnp.where(low_q, low[i], roll(low[i + 5], 32))
        up = jnp.where(low_q, roll(high[i + 5], 96), high[i])
        ya_ref[i * 8 : i * 8 + 8] = jnp.where(even_y, up, down)
        yb_ref[i * 8 : i * 8 + 8] = jnp.where(even_y, down, up)
    low_q = (iotas(16)[0] & 32) == 0
    down = jnp.where(low_q, low_ends[0], roll(low_ends[1], 32))
    up = jnp.where(low_q, roll(high_ends[1], 96), high_ends[0])
    ya_ref[40:56] = jnp.where(even_y, up, down)
    yb_ref[40:56] = jnp.where(even_y, down, up)


def factors_kernel(vec_ref, eig_ref, s_ref, held_ref):
    held_ref[...] = eig_ref[...]
    for a in range(10):
        for i in range(10):
            s_ref[(i * 10 + a) * 8 : (i * 10 + a) * 8 + 3] = vec_ref[i, a].astype(F32)


def factor_of(s):
    return lambda d, i, a: row(s, (i * 10 + a) * 8 + d)


def along_x(source, target, factor, transposed):
    def step(k, _):
        for h in range(2):
            at = k * 16 + 8 * h
            held = [source[pl.ds(i * 160 + at, 8), :] for i in range(10)]
            for a in range(10):
                target[pl.ds(a * 160 + at, 8), :] = chain(
                    (factor(0, a, i) if transposed else factor(0, i, a), held[i]) for i in range(10)
                )
        return 0

    lax.fori_loop(0, 10, step, 0)


def y_factors(s):
    return [[s[pl.ds((j * 10 + 8 * h) * 8 + 1, 8, stride=8), :] for j in range(10)] for h in range(2)]


def front_kernel(core_ref, ends_ref, za_ref, zb_ref, s, u, edge_ref, block):
    lane, _ = iotas()
    first, last = z_halo(core_ref, ends_ref, za_ref, zb_ref, lane & 31)
    for i in range(10):
        block[pl.ds(i * 80, 8), :] = first[i]
        block[pl.ds(i * 80 + 72, 8), :] = last[i]
        for k in range(8):
            block[pl.ds(i * 80 + 8 + k * 8, 8), :] = plane(core_ref, ends_ref, i, k)
    for i in range(10):
        edge_ref[i * 16 : i * 16 + 16] = roll(block[pl.ds(i * 80 + 7, 16, stride=8), :], 32)
        edge_ref[160 + i * 16 : 176 + i * 16] = roll(block[pl.ds(i * 80, 16, stride=8), :], 96)
    factor = factor_of(s)
    front = y_factors(s)

    def along(k, _):
        held = [block[pl.ds(i * 80 + k * 8, 8), :] for i in range(10)]
        for a in range(10):
            block[pl.ds(a * 80 + k * 8, 8), :] = chain((factor(0, i, a), held[i]) for i in range(10))
        return 0

    lax.fori_loop(0, 10, along, 0)

    def own_rows(a, _):
        for k in range(10):
            at = (a * 10 + k) * 8
            rows = [row(block, at + j) for j in range(8)]
            for h in range(2):
                u[pl.ds(at * 2 + 8 * h, 8), :] = chain((front[h][j + 1], rows[j]) for j in range(8))
        return 0

    lax.fori_loop(0, 10, own_rows, 0)


def modes_kernel(u_ref, edge_ref, ya_ref, yb_ref, s, u, rows):
    low_q = (iotas(16)[0] & 32) == 0
    ends_above, ends_below = sides(ya_ref[40:56], yb_ref[40:56], "gy")
    for i in range(10):
        at = (i % 5) * 8
        above, below = sides(ya_ref[at : at + 8], yb_ref[at : at + 8], "gy")
        if i < 5:
            above, below = roll(above, 32), roll(below, 96)
        for base, middle, zero, nine in (
            (0, below, roll(ends_below, 96), ends_below),
            (160, above, roll(ends_above, 32), ends_above),
        ):
            rows[base + i * 16 + 1 : base + i * 16 + 9] = middle
            rows[base + i * 16 : base + i * 16 + 1] = zero[i : i + 1]
            rows[base + i * 16 + 9 : base + i * 16 + 10] = nine[i : i + 1]
    low = [jnp.where(low_q, rows[i * 16 : i * 16 + 16], edge_ref[i * 16 : i * 16 + 16]) for i in range(10)]
    high = [
        jnp.where(low_q, edge_ref[160 + i * 16 : 176 + i * 16], rows[160 + i * 16 : 176 + i * 16]) for i in range(10)
    ]
    front = y_factors(s)
    for a in range(10):
        weights = [row(s, (i * 10 + a) * 8, 16) for i in range(10)]
        rows[320 + a * 16 : 336 + a * 16] = chain((weights[i], low[i]) for i in range(10))
        rows[480 + a * 16 : 496 + a * 16] = chain((weights[i], high[i]) for i in range(10))

    def add_edges(a, _):
        for k in range(10):
            before, after = row(rows, 320 + a * 16 + k), row(rows, 480 + a * 16 + k)
            for h in range(2):
                at = (a * 10 + k) * 16 + 8 * h
                u[pl.ds(at, 8), :] = u_ref[pl.ds(at, 8), :] + (front[h][0] * before + front[h][9] * after)
        return 0

    lax.fori_loop(0, 10, add_edges, 0)


def middle_kernel(u_ref, s, eig_ref, u, eg):
    eg[...] = jnp.ones((16, 128), F32)
    for a in range(10):
        eg[a : a + 1] = eig_ref[1, a]
    factor = factor_of(s)

    def wide(value):
        return jnp.broadcast_to(value, (8, 128))

    def along_z(a, _):
        for h in range(2):
            at = a * 160 + 8 * h
            held = [u_ref[pl.ds(at + k * 16, 8), :] for k in range(10)]
            base = wide(eig_ref[0, a]) + eg[8 * h : 8 * h + 8]
            modes = []
            for c in range(10):
                modes.append(chain((factor(2, k, c), held[k]) for k in range(10)) / (base + wide(eig_ref[2, c])))
            for k in range(10):
                u[pl.ds(at + k * 16, 8), :] = chain((factor(2, k, c), modes[c]) for c in range(10))
        return 0

    lax.fori_loop(0, 10, along_z, 0)


def points_kernel(u_ref, s, l_ref, hl_ref, hh_ref, xs_ref, u):
    gx = lax.axis_index("gx")
    lane, _ = iotas()
    factor = factor_of(s)
    along_x(u_ref, u, factor, True)
    back = [s[pl.ds((10 + b) * 8 + 1, 8, stride=80), :] for b in range(10)]

    def back_y(i, _):
        for k in range(10):
            at = (i * 10 + k) * 16
            l_ref[i, k] = chain((back[b], row(u, at + b)) for b in range(10))
        for h in range(2):
            cut = [u[pl.ds(i * 160 + 128 * h + b, 8, stride=16), :] for b in range(10)]
            hl_ref[i, 8 * h : 8 * h + 8] = chain((factor(1, 0, b), cut[b]) for b in range(10))
            hh_ref[i, 8 * h : 8 * h + 8] = chain((factor(1, 9, b), cut[b]) for b in range(10))
        return 0

    lax.fori_loop(0, 10, back_y, 0)
    high_p = lane >= 64

    def outgoing(ref, k):
        return jnp.where(gx == 0, ref[9, k], roll(ref[0, k], 64))

    for k in range(5):
        xs_ref[k * 8 : k * 8 + 8] = jnp.where(high_p, outgoing(l_ref, k), roll(outgoing(l_ref, k + 5), 64))
    high_p = iotas(16)[0] >= 64
    edge_l = jnp.where(gx == 0, hl_ref[9], roll(hl_ref[0], 64))
    edge_h = jnp.where(gx == 0, hh_ref[9], roll(hh_ref[0], 64))
    xs_ref[40:56] = jnp.where(high_p, edge_l, roll(edge_h, 64))


def fold_x(value, i, opposite, received, gx, high_p):
    if i == 8:
        return value + jnp.where(high_p, jnp.where(gx == 0, received, 0.0), roll(opposite, 64))
    if i == 1:
        return value + jnp.where(high_p, roll(opposite, 64), jnp.where(gx == 1, roll(received, 64), 0.0))
    return value


def edge_rows(hl_ref, hh_ref, xr_ref, gx):
    high_p = iotas(16)[0] >= 64
    packed = xr_ref[40:56]
    low, high = [], []
    for i in range(1, 9):
        j = {1: 9, 8: 0}.get(i, i)
        low.append(fold_x(hl_ref[i], i, hl_ref[j], packed, gx, high_p))
        high.append(fold_x(hh_ref[i], i, hh_ref[j], roll(packed, 64), gx, high_p))
    return low, high


def yfold_send_kernel(hl_ref, hh_ref, xr_ref, run_ref, ya_ref, yb_ref):
    ya_ref[40:56] = run_ref[...]
    gx = lax.axis_index("gx")
    even_y = lax.rem(lax.axis_index("gy"), 2) == 0
    low_q = (iotas(16)[0] & 32) == 0
    low, high = edge_rows(hl_ref, hh_ref, xr_ref, gx)
    for i in range(4):
        down = jnp.where(low_q, low[i], roll(low[i + 4], 32))
        up = jnp.where(low_q, roll(high[i + 4], 96), high[i])
        for ref, value in ((ya_ref, jnp.where(even_y, up, down)), (yb_ref, jnp.where(even_y, down, up))):
            ref[i * 8 : i * 8 + 8] = value[:8]
            ref[32 + 2 * i : 34 + 2 * i] = value[8:10]


def fold_rows(hl_ref, hh_ref, xr_ref, ya_ref, yb_ref, rows_first, rows_last, gx):
    low_q = (iotas(16)[0] & 32) == 0
    low, high = edge_rows(hl_ref, hh_ref, xr_ref, gx)
    for i in range(8):
        n = i % 4
        rows = [jnp.concatenate([ref[n * 8 : n * 8 + 8], ref[32 + 2 * n : 40 + 2 * n]], 0) for ref in (ya_ref, yb_ref)]
        above, below = sides(*rows, "gy")
        if i < 4:
            above, below = roll(above, 32), roll(below, 96)
        rows_last[pl.ds(i * 16, 16), :] = jnp.where(low_q, roll(low[i], 96), above)
        rows_first[pl.ds(i * 16, 16), :] = jnp.where(low_q, below, roll(high[i], 32))


def folded_xy(l_ref, xr_ref, rows_first, rows_last, i, k, gx, lane, sub):
    high_p = lane >= 64
    value = l_ref[i, k]
    if i in (1, 8):
        packed = xr_ref[(k % 5) * 8 : (k % 5) * 8 + 8]
        received = packed if k < 5 else roll(packed, 64)
        value = fold_x(value, i, l_ref[9 if i == 1 else 0, k], received, gx, high_p)
    at = (i - 1) * 16 + k
    return value + jnp.where(sub == 0, row(rows_first, at), jnp.where(sub == 7, row(rows_last, at), 0.0))


def zplane_kernel(l_ref, hl_ref, hh_ref, xr_ref, plane_ref, rows_first, rows_last):
    gx = lax.axis_index("gx")
    lane, sub = iotas()
    low_q = (iotas(16)[0] & 32) == 0
    low, high = edge_rows(hl_ref, hh_ref, xr_ref, gx)
    for i in range(8):
        rows_last[pl.ds(i * 16, 16), :] = jnp.where(low_q, roll(low[i], 96), 0.0)
        rows_first[pl.ds(i * 16, 16), :] = jnp.where(low_q, 0.0, roll(high[i], 32))
    for n, k in enumerate((0, 9)):
        for i in range(8):
            plane_ref[n, i] = folded_xy(l_ref, xr_ref, rows_first, rows_last, i + 1, k, gx, lane, sub)


def zfold_send_kernel(plane_ref, ya_ref, yb_ref, run_ref, za_ref, zb_ref):
    za_ref[8:24] = run_ref[...]
    even_z = lax.rem(lax.axis_index("gz"), 2) == 0
    lane, sub = iotas()
    slot = lane & 31
    low_q = (lane & 32) == 0

    def folded(n, i):
        at = (i % 4) * 8 if n == 0 else 33 + 2 * (i % 4)
        above, below = sides(row(ya_ref, at), row(yb_ref, at), "gy")
        if i < 4:
            above, below = roll(above, 32), roll(below, 96)
        received = jnp.where(sub == 0, jnp.where(low_q, below, 0.0), jnp.where(low_q, 0.0, above))
        return plane_ref[n, i] + jnp.where((sub == 0) | (sub == 7), received, 0.0)

    down = jnp.zeros((8, 128), F32)
    up = jnp.zeros((8, 128), F32)
    for i in range(8):
        down = jnp.where(slot == i, roll(folded(0, i), i), down)
        up = jnp.where(slot == i, roll(folded(1, i), i - 31), up)
    za_ref[:8] = jnp.where(even_z, up, down)
    zb_ref[...] = jnp.where(even_z, down, up)


def gather_kernel(
    l_ref, hl_ref, hh_ref, xr_ref, ya_ref, yb_ref, basis_ref, sum_ref, tile_ref, rows_first, rows_last, xt, grid
):
    gx = lax.axis_index("gx")
    lane, sub = iotas()
    slot = lane & 31
    low_q = (lane & 32) == 0
    fold_rows(hl_ref, hh_ref, xr_ref, ya_ref, yb_ref, rows_first, rows_last, gx)
    for i in range(8):
        get = functools.partial(folded_xy, l_ref, xr_ref, rows_first, rows_last, i + 1, gx=gx, lane=lane, sub=sub)
        before, after = get(0), get(9)
        for k in range(8):
            value = get(k + 1)
            if k == 0:
                value = value + jnp.where(slot == 0, 0.0, roll(after, 1))
            if k == 7:
                value = value + jnp.where(slot == 31, 0.0, roll(before, -1))
            grid[i, k] = value
        weights = jnp.concatenate([basis_ref[i]] * 16, 1)
        tile_ref[i * 8 : i * 8 + 8] = weights
    for pair in range(4):
        k0, k1 = 2 * pair, 2 * pair + 1
        pieces = []
        for i in range(8):
            c0, c1 = grid[i, k0], grid[i, k1]
            pieces.append(jnp.where(low_q, c0, roll(c1, 32)))
            pieces.append(jnp.where(low_q, roll(c0, 96), c1))
        block = jnp.concatenate(pieces, 0).T
        for p in range(2):
            for t, k in enumerate((k0, k1)):
                at = p * 64 + t * 32
                xt[p, pl.ds(k, 32, stride=8), :] = block[at : at + 32]
    sum_ref[...] = jnp.concatenate([xt[0], xt[1]], 1).T


def post_kernel(sum_ref, tile_ref, za_ref, zb_ref, sep_ref, run_ref, ownsol_ref, out_ref, total_ref, sems):
    lane, _ = iotas()
    running = run_ref[...] + za_ref[8:24]
    weighted = total(
        sep_ref[level][:, h * 128 : h * 128 + 128] * running[8 * h + level : 8 * h + level + 1, :]
        for h in range(2)
        for level in range(sep_ref.shape[0])
    )
    solution_col = ownsol_ref[:, :1] + jnp.sum(weighted, axis=1, keepdims=True)
    lane16, sub16 = iotas(16)
    along_z = []
    for t in range(2):
        spread = jnp.where((lane16 >> 4) + 8 * t == sub16, jnp.broadcast_to(solution_col, (16, 128)), 0.0)
        along_z.append(jnp.broadcast_to(jnp.sum(spread, axis=0, keepdims=True), (8, 128)))
    from_above, from_below = sides(za_ref[:8], zb_ref[...], "gz")
    copies = []
    for p in range(2):
        for i in range(8):
            weights = tile_ref[i * 8 : i * 8 + 8]
            low, high = weights * along_z[0], weights * along_z[1]
            for q in range(2):
                at = ((p * 8 + i) * 2 + q) * 8
                source = p * 64 + q * 32 + i
                first = sum_ref[at : at + 8, :128] + low
                last = sum_ref[at : at + 8, 128:] + high
                total_ref[at : at + 8, :128] = first + jnp.where(lane == 0, roll(from_below, -source), 0.0)
                total_ref[at : at + 8, 128:] = last + jnp.where(lane == 127, roll(from_above, 127 - source), 0.0)
            if i % 4 == 3:
                rows = pl.ds(p * 128 + (i // 4) * 64, 64)
                copies.append(pltpu.make_async_copy(total_ref.at[rows, :], out_ref.at[rows, :], sems.at[p * 2 + i // 4]))
                copies[-1].start()
    for copy in copies:
        copy.wait()


def call(kernel, outs, scratch, n_in, limit=4 << 20, far=0, semaphores=(), out_space=pltpu.VMEM):
    return pl.pallas_call(
        kernel,
        out_shape=[jax.ShapeDtypeStruct(shape, F32) for shape in outs],
        in_specs=[pl.BlockSpec(memory_space=pltpu.HBM)] * far + [VM] * (n_in - far),
        out_specs=[pl.BlockSpec(memory_space=out_space)] * len(outs),
        scratch_shapes=[pltpu.VMEM(shape, F32) for shape in scratch] + list(semaphores),
        compiler_params=pltpu.CompilerParams(vmem_limit_bytes=limit),
    )


def far(value):
    return pltpu.with_memory_space_constraint(value, pltpu.HBM)


def swap(value, axis, distance):
    return lax.ppermute(value, axis, [(i, i ^ distance) for i in range(lax.axis_size(axis))])


def swap_odd(value, axis):
    count = lax.axis_size(axis)
    return lax.ppermute(value, axis, [(i, (i + 1 if i % 2 else i - 1) % count) for i in range(count)])


def work(residual, fdm_vectors, fdm_eigen, coarse_basis, x_interior, x_separator):
    levels, unknowns, width = x_separator.shape[3:]
    x = residual.reshape(256, 256)
    vectors = fdm_vectors.reshape(3, 10, 10, 128).transpose(1, 2, 0, 3)
    eigen = fdm_eigen.reshape(3, 10, 1, 128)
    own = x_interior.reshape(unknowns, unknowns)
    sep = x_separator.reshape(levels, unknowns, width)
    level_of = lax.broadcasted_iota(jnp.int32, (16, 128), 0) & 7

    def climb(running, axis, distance, first):
        return running + jnp.where(level_of >= first, swap(running, axis, distance), 0.0)

    core, xs, running, ownsol = call(
        pre_kernel,
        [(8, 8, 8, 128), (32, 128), (16, 128), (16, 128)],
        [(2, 128, 256), (2, 256, 128), (levels, unknowns, width), (8, 8, 8), (unknowns, unknowns)],
        4,
        far=4,
        semaphores=(pltpu.SemaphoreType.DMA((2,)), pltpu.SemaphoreType.DMA((3,))),
    )(far(x), far(sep), far(coarse_basis), far(own))
    xr = swap(xs, "gx", 1)
    ends, za, zb = call(zface_kernel, [(2, 8, 8, 128), (8, 128), (8, 128)], [], 2)(core, xr)
    running = climb(running, "gy", 2, 5)
    za, zb = swap(za, "gz", 1), swap_odd(zb, "gz")
    running = climb(running, "gy", 6, 6)
    factors, eigen = call(factors_kernel, [(848, 128), eigen.shape], [], 2)(vectors, eigen)
    block = (core, core.reshape(512, 128), ends, ends.reshape(128, 128), za, zb)
    ya, yb = call(yface_kernel, [(56, 128), (56, 128)], [(256, 128)], 6)(*block)
    ya, yb = swap(ya, "gy", 1), swap_odd(yb, "gy")
    four, twelve, eight = (swap(running, "gz", d) for d in (4, 12, 8))
    modes, edges = call(front_kernel, [(1696, 128), (320, 128)], [(848, 128)], 5)(core, ends, *block[4:], factors)
    (modes,) = call(modes_kernel, [(1696, 128)], [(640, 128)], 5)(modes, edges, ya, yb, factors)
    (modes,) = call(middle_kernel, [(1696, 128)], [(16, 128)], 3)(modes, factors, eigen)
    both = jnp.where(level_of >= 3, four + (twelve + eight), four)
    running = running + jnp.where(level_of >= 2, both, 0.0)
    running = climb(running, "gz", 3, 1)
    local, edge_l, edge_h, xs = call(
        points_kernel, [(10, 10, 8, 128), (10, 16, 128), (10, 16, 128), (56, 128)], [(1696, 128)], 2
    )(modes, factors)
    xr = swap(xs, "gx", 1)
    ya, yb = call(yfold_send_kernel, [(56, 128), (48, 128)], [], 4)(edge_l, edge_h, xr, running)
    ya, yb = swap(ya, "gy", 1), swap_odd(yb, "gy")
    running = running + jnp.where(level_of >= 4, ya[40:56], 0.0)
    running = climb(running, "gx", 1, 7)
    parts = (local, edge_l, edge_h, xr, ya, yb)
    (planes,) = call(zplane_kernel, [(2, 8, 8, 128)], [(128, 128)] * 2, 4)(*parts[:4])
    za, zb = call(zfold_send_kernel, [(24, 128), (8, 128)], [], 4)(planes, ya, yb, running)
    za, zb = swap(za, "gz", 1), swap_odd(zb, "gz")
    smooth, tile = call(
        gather_kernel, [(256, 256), (64, 128)], [(128, 128), (128, 128), (2, 256, 128), (8, 8, 8, 128)], 7
    )(*parts, coarse_basis)
    (out,) = call(
        post_kernel, [(256, 256)], [(256, 256)], 7, semaphores=(pltpu.SemaphoreType.DMA((4,)),), out_space=pltpu.HBM
    )(smooth, tile, za, zb, sep, running, ownsol)
    return out.reshape(residual.shape)


def solution(mesh):
    in_specs = (
        P("gx", "gy", "gz"),
        P("gx", "gy", "gz", None, None, None, None),
        P("gx", "gy", "gz", None, None, None),
        P(),
        P("gx", "gy", "gz", None, None),
        P("gx", "gy", "gz", None, None, None),
    )
    return jax.shard_map(work, mesh=mesh, in_specs=in_specs, out_specs=P("gx", "gy", "gz"), check_vma=False)
```
